32 devices in a mesh: dp: 16 (over z, x, core), tensor: 2 (over y).
Axes of the slice: x: 2, y: 2, z: 4, core: 2. Of those that a mesh axis runs over, the one named last changes fastest.
Arguments:
- x_given: bfloat16 [16, 1024, 768], P(None, ('dp', 'tensor')), may hold values from -6 to 6
- dealing: int32 [16], replicated, may hold values from 0 to 15, each once
- seq_lengths: int32 [16], replicated, may hold values from 256 to 1024, as said below
- first_gain: bfloat16 [768], P('dp'), may hold values from 0.099609375 to 1.8984375
- query_weight: bfloat16 [768, 768], P('dp', 'tensor'), may hold values from -0.3125 to 0.3125
- key_weight: bfloat16 [768, 768], P('dp', 'tensor'), may hold values from -0.3125 to 0.3125
- value_weight: bfloat16 [768, 768], P('dp', 'tensor'), may hold values from -0.21875 to 0.21875
- output_weight: bfloat16 [768, 768], P('dp', 'tensor'), may hold values from -0.875 to 0.875
- second_gain: bfloat16 [768], P('dp'), may hold values from 0.099609375 to 1.8984375
- gate_weight: bfloat16 [768, 2560], P('dp', 'tensor'), may hold values from -0.21875 to 0.21875
- up_weight: bfloat16 [768, 2560], P('dp', 'tensor'), may hold values from -0.21875 to 0.21875
- down_weight: bfloat16 [768, 2560], P('dp', 'tensor'), may hold values from -0.25 to 0.25
- grad_output: bfloat16 [16, 16, 2, 32, 768], P('dp', None, 'tensor'), may hold values from -6 to 6
Outputs:
- layer_out: bfloat16 [16, 16, 2, 32, 768], P('dp', None, 'tensor')
- grad_in: bfloat16 [16, 1024, 768], P(None, ('dp', 'tensor'))
- grad_first_gain: float32 [768], P('dp')
- grad_query_weight: float32 [768, 768], P('dp', 'tensor')
- grad_key_weight: float32 [768, 768], P('dp', 'tensor')
- grad_value_weight: float32 [768, 768], P('dp', 'tensor')
- grad_output_weight: float32 [768, 768], P('dp', 'tensor')
- grad_second_gain: float32 [768], P('dp')
- grad_gate_weight: float32 [768, 2560], P('dp', 'tensor')
- grad_up_weight: float32 [768, 2560], P('dp', 'tensor')
- grad_down_weight: float32 [768, 2560], P('dp', 'tensor')
The draws below stay inside these ranges and needn't reach their ends.
Inputs may be any that keep to these rules, and one draw needn't show every extreme that they name: `dealing`: a permutation of the 16 sequences. `seq_lengths`: some sequence is live at all 1024 positions.
All inputs are finite; a program needn't handle non-finite values.
Results may differ from the reference program's by a relative error of at most 0.025.
Values may be sent and summed in bfloat16 or wider, within the bound.
A program may use at most 128 MiB of HBM per device.

```python
import jax
import jax.numpy as jnp
from jax import lax

D = 768
HEADS = 16
HD = 48
FF = 2560
NSEQ = 16
SEQ = 1024
PIECE = 32
N_DP = 16
N_TENSOR = 2


def draw_seq_lengths(key, part):
    first_key, second_key = jax.random.split(key)
    lengths = jax.random.randint(first_key, (NSEQ,), SEQ // 4, SEQ + 1)
    fullest = jax.random.randint(second_key, (), 0, NSEQ)
    return jnp.where(jnp.arange(NSEQ) == fullest, SEQ, lengths).astype(jnp.int32)


def block_scale(stream_key, shape, cuts, least, largest):
    gain = 1.0
    for axis_at, blocks in cuts:
        draws = jax.random.uniform(jax.random.fold_in(jax.random.fold_in(stream_key, 6), axis_at), (blocks,), jnp.float32, least / len(cuts), largest / len(cuts))
        gain = gain * jnp.repeat(jnp.exp(draws), shape[axis_at] // blocks).reshape((-1,) + (1,) * (len(shape) - 1 - axis_at))
    return gain


def gaussian(key, dims, width, reach, shards=(), kind=jnp.bfloat16):
    loudness = block_scale(key, dims, shards, -0.22, 0.18) if shards else 1.0
    entries = jax.random.normal(key, dims, jnp.float32) * width * loudness
    return jnp.minimum(jnp.maximum(entries, -reach), reach).astype(kind)


def setup_inputs(seed: int = 0) -> dict:
    keys = jax.random.split(jax.random.key(seed), 14)
    x_given = gaussian(keys[0], (NSEQ, SEQ, D), 1.0, 6.0, ((1, 32),))
    dealing = jax.random.permutation(keys[1], NSEQ).astype(jnp.int32)
    seq_lengths = draw_seq_lengths(jax.random.fold_in(keys[13], 71), 0)
    first_gain = jnp.clip(1.0 + 0.18 * jax.random.normal(keys[3], (D,), jnp.float32), 0.099609375, 1.8984375).astype(jnp.bfloat16)
    query_weight = gaussian(keys[4], (D, D), (D // 2) ** -0.5, 0.3125, ((0, 16), (1, 2)))
    key_weight = gaussian(keys[5], (D, D), (D // 2) ** -0.5, 0.3125, ((0, 16), (1, 2)))
    value_weight = gaussian(keys[6], (D, D), D ** -0.5, 0.21875, ((0, 16), (1, 2)))
    output_weight = gaussian(keys[7], (D, D), (D // 16) ** -0.5, 0.875, ((0, 16), (1, 2)))
    second_gain = jnp.clip(1.0 + 0.18 * jax.random.normal(keys[8], (D,), jnp.float32), 0.099609375, 1.8984375).astype(jnp.bfloat16)
    gate_weight = gaussian(keys[9], (D, FF), D ** -0.5, 0.21875, ((0, 16), (1, 2)))
    up_weight = gaussian(keys[10], (D, FF), D ** -0.5, 0.21875, ((0, 16), (1, 2)))
    down_weight = gaussian(keys[11], (D, FF), (FF // 4) ** -0.5, 0.25, ((0, 16), (1, 2)))
    grad_output = gaussian(keys[12], (NSEQ, N_DP, N_TENSOR, PIECE, D), 1.0, 6.0, ((0, 16), (2, 2)))
    return dict(x_given=x_given, dealing=dealing, seq_lengths=seq_lengths, first_gain=first_gain, query_weight=query_weight, key_weight=key_weight, value_weight=value_weight, output_weight=output_weight, second_gain=second_gain, gate_weight=gate_weight, up_weight=up_weight, down_weight=down_weight, grad_output=grad_output)


EPS = 1e-05
BASE = 10000.0

@jax.custom_vjp
def low(v):
    return lax.optimization_barrier(v.astype(jnp.bfloat16)).astype(jnp.float32)

@jax.custom_vjp
def low_back(v):
    return v

def low_keep(v):
    return (low(v), None)

def low_pass(kept, grad):
    return (grad,)

def back_keep(v):
    return (v, None)

def back_low(kept, grad):
    return (low(grad),)
low.defvjp(low_keep, low_pass)
low_back.defvjp(back_keep, back_low)

def matmul(left_side, right_side):
    return jnp.dot(left_side, right_side, precision=lax.Precision.HIGHEST)

def tables(positions):
    freq_index = jnp.arange(HD // 2, dtype=jnp.float32)
    frequency = BASE ** (-2.0 * freq_index / HD)
    angles = positions[:, None] * frequency[None, :]
    return (jnp.cos(angles)[:, None, :], jnp.sin(angles)[:, None, :])

def rotary(values, cosine, sine_table):
    half_width = values.shape[-1] // 2
    first_half = values[..., :half_width]
    second_half = values[..., half_width:]
    return jnp.concatenate([first_half * cosine - second_half * sine_table, second_half * cosine + first_half * sine_table], axis=-1)

def layer(weights_in, x_rows, live_rows):
    first_gain, query_weight, key_weight, value_weight, output_weight, second_gain, gate_weight, up_weight, down_weight = weights_in
    cosine, sine_table = tables(jnp.arange(SEQ, dtype=jnp.float32))
    scale_one = lax.rsqrt(lax.optimization_barrier(jnp.mean(x_rows * x_rows, axis=-1, keepdims=True)) + EPS)
    normed = low(x_rows * scale_one * first_gain)
    queries = low(rotary(low_back(matmul(normed, query_weight)).reshape(SEQ, HEADS, HD), cosine, sine_table))
    key_rows = low(rotary(low_back(matmul(normed, key_weight)).reshape(SEQ, HEADS, HD), cosine, sine_table))
    values = low(low_back(matmul(normed, value_weight))).reshape(SEQ, HEADS, HD)
    block_rows = min(512, SEQ)
    key_positions = jnp.arange(SEQ)

    def attend(offset):
        query_part = lax.dynamic_slice_in_dim(queries, offset, block_rows, 0)
        scores = jnp.einsum('qhd,khd->hqk', query_part, key_rows, precision=lax.Precision.HIGHEST)
        scores = low_back(scores * HD ** (-0.5))
        query_positions = offset + jnp.arange(block_rows)
        allowed = key_positions[None, :] <= query_positions[:, None]
        scores = jnp.where(allowed[None], scores, -1e+30)
        prob_soft = jax.nn.softmax(scores, axis=-1)
        return jnp.einsum('hqk,khd->qhd', low(prob_soft), values, precision=lax.Precision.HIGHEST)
    block_starts = jnp.arange(SEQ // block_rows, dtype=jnp.int32) * block_rows
    mixed = lax.map(jax.checkpoint(attend), block_starts).reshape(SEQ, D)
    mixed = low(low_back(mixed))
    attention = low_back(matmul(mixed, output_weight.T))
    hidden_one = x_rows + live_rows[:, None] * attention
    scale_two = lax.rsqrt(lax.optimization_barrier(jnp.mean(hidden_one * hidden_one, axis=-1, keepdims=True)) + EPS)
    normed_two = low(hidden_one * scale_two * second_gain)
    gate_act = low_back(matmul(normed_two, gate_weight))
    up_act = low_back(matmul(normed_two, up_weight))
    hidden = low(jax.nn.silu(gate_act) * up_act)
    branch = low_back(matmul(hidden, down_weight.T))
    return hidden_one + live_rows[:, None] * branch

def reference(x_given, dealing, seq_lengths, first_gain, query_weight, key_weight, value_weight, output_weight, second_gain, gate_weight, up_weight, down_weight, grad_output):
    weights_in = tuple((weight.astype(jnp.float32) for weight in (first_gain, query_weight, key_weight, value_weight, output_weight, second_gain, gate_weight, up_weight, down_weight)))

    def per_slot(totals, slot_index):
        sequence = dealing[slot_index]
        x_rows = lax.dynamic_index_in_dim(x_given, sequence, 0, keepdims=False).astype(jnp.float32)
        live_rows = (jnp.arange(SEQ) < seq_lengths[sequence]).astype(jnp.float32)
        cotangent = grad_output[slot_index].reshape(SEQ, D).astype(jnp.float32)
        outputs, pullback = jax.vjp(lambda weights_now, rows_now: layer(weights_now, rows_now, live_rows), weights_in, x_rows)
        gradients, input_grad = pullback(cotangent)
        totals = jax.tree.map(lambda acc_value, new_value: acc_value + new_value, totals, gradients)
        return (totals, (outputs.astype(jnp.bfloat16), input_grad.astype(jnp.bfloat16)))
    zero_grads = jax.tree.map(jnp.zeros_like, weights_in)
    totals, (outputs, input_grads) = lax.scan(per_slot, zero_grads, jnp.arange(NSEQ, dtype=jnp.int32))
    layer_out = outputs.reshape(NSEQ, N_DP, N_TENSOR, PIECE, D)
    grad_in = jnp.zeros((NSEQ, SEQ, D), jnp.bfloat16).at[dealing].set(input_grads)
    return (layer_out, grad_in, totals[0], totals[1], totals[2], totals[3], totals[4], totals[5], totals[6], totals[7], totals[8])
```

```python
import functools

import jax
import jax.numpy as jnp
import numpy as np
from jax import lax
from jax.experimental import pallas as pl
from jax.experimental.pallas import tpu as pltpu
from jax.sharding import PartitionSpec as P

HD = 48


EPS = 1e-05
BASE = 10000.0
VMEM_LIMIT = 64 * 1024 * 1024 - 65536


def tables(positions, head_size):
    freq_index = jnp.arange(head_size // 2, dtype=jnp.float32)
    frequency = BASE ** (-2.0 * freq_index / head_size)
    angles = positions[:, None] * frequency[None, :]
    return (jnp.cos(angles)[:, None, :], jnp.sin(angles)[:, None, :])


def rotary(values, cosine, sine_table):
    half_width = values.shape[-1] // 2
    first_half = values[..., :half_width]
    second_half = values[..., half_width:]
    return jnp.concatenate(
        [
            first_half * cosine - second_half * sine_table,
            second_half * cosine + first_half * sine_table,
        ],
        axis=-1,
    )


def rotary_back(values, cosine, sine_table):
    half_width = values.shape[-1] // 2
    first_half = values[..., :half_width]
    second_half = values[..., half_width:]
    return jnp.concatenate(
        [
            first_half * cosine + second_half * sine_table,
            second_half * cosine - first_half * sine_table,
        ],
        axis=-1,
    )


def row_dot(left_side, right_side):
    return jnp.dot(left_side, right_side, preferred_element_type=jnp.float32)


def dot_trans(left_side, right_side):
    return lax.dot_general(
        left_side, right_side, (((1,), (1,)), ((), ())), preferred_element_type=jnp.float32
    )


def dot_first(left_side, right_side):
    return lax.dot_general(
        left_side, right_side, (((0,), (0,)), ((), ())), preferred_element_type=jnp.float32
    )


def tensor_major(values, groups, pieces, piece_rows):
    columns = values.shape[1]
    return (
        values.reshape(groups, pieces, piece_rows, columns)
        .transpose(1, 0, 2, 3)
        .reshape(groups * pieces * piece_rows, columns)
    )


def rms_back(grad_normed, x_rows, scale_rows, gain):
    normed = x_rows * scale_rows
    weighted = grad_normed * gain
    x_grad = scale_rows * (weighted - normed * jnp.mean(weighted * normed, axis=-1, keepdims=True))
    return (x_grad, jnp.sum(grad_normed * normed, axis=0))


def block_scores(queries, key_rows, query_start, key_start, block_rows, score_scale):
    query_part = lax.dynamic_slice_in_dim(queries, query_start, block_rows, 0)
    key_part = lax.dynamic_slice_in_dim(key_rows, key_start, block_rows, 0)
    scores = (
        jnp.einsum("qhd,khd->hqk", query_part, key_part, preferred_element_type=jnp.float32)
        * score_scale
    )
    row_offsets = jnp.arange(block_rows)
    allowed = (key_start + row_offsets)[None, :] <= (query_start + row_offsets)[:, None]
    return jnp.where(allowed[None], scores, -1e30)


def attend_forward(queries, key_rows, value_rows, live_blocks, block_rows, score_scale):
    seq_len, heads, head_size = queries.shape

    def one_block(query_index, state_now):
        outputs, log_sums = state_now
        query_start = query_index * block_rows

        def stats(key_index, carried):
            running, exp_total = carried
            scores = block_scores(
                queries, key_rows, query_start, key_index * block_rows, block_rows, score_scale
            )
            newest = jnp.maximum(running, jnp.max(scores, axis=-1))
            exp_total = exp_total * jnp.exp(running - newest) + jnp.sum(
                jnp.exp(scores - newest[..., None]), axis=-1
            )
            return (newest, exp_total)

        initial = (
            jnp.full((heads, block_rows), -1e30, jnp.float32),
            jnp.zeros((heads, block_rows), jnp.float32),
        )
        running, exp_total = lax.fori_loop(0, query_index + 1, stats, initial)
        log_sum = running + jnp.log(exp_total)

        def accumulate(key_index, accumulated):
            key_start = key_index * block_rows
            scores = block_scores(
                queries, key_rows, query_start, key_start, block_rows, score_scale
            )
            prob_low = jnp.exp(scores - log_sum[..., None]).astype(jnp.bfloat16)
            value_part = lax.dynamic_slice_in_dim(value_rows, key_start, block_rows, 0)
            return accumulated + jnp.einsum(
                "hqk,khd->qhd", prob_low, value_part, preferred_element_type=jnp.float32
            )

        result = lax.fori_loop(
            0, query_index + 1, accumulate, jnp.zeros((block_rows, heads, head_size), jnp.float32)
        )
        outputs = lax.dynamic_update_slice_in_dim(outputs, result, query_start, 0)
        log_sums = lax.dynamic_update_slice_in_dim(log_sums, log_sum, query_start, 1)
        return (outputs, log_sums)

    initial = (
        jnp.zeros((seq_len, heads, head_size), jnp.float32),
        jnp.zeros((heads, seq_len), jnp.float32),
    )
    return lax.fori_loop(0, live_blocks, one_block, initial)


def attend_backward(
    queries, key_rows, value_rows, outputs, log_sums, out_grad, live_blocks, block_rows, score_scale
):
    seq_len, heads, head_size = queries.shape
    row_delta = jnp.einsum("qhd,qhd->hq", out_grad.astype(jnp.float32), outputs)

    def one_block(query_index, state_now):
        query_grads, key_grads, value_grads = state_now
        query_start = query_index * block_rows
        query_part = lax.dynamic_slice_in_dim(queries, query_start, block_rows, 0)
        grad_part = lax.dynamic_slice_in_dim(out_grad, query_start, block_rows, 0)
        logsum_part = lax.dynamic_slice_in_dim(log_sums, query_start, block_rows, 1)
        delta_part = lax.dynamic_slice_in_dim(row_delta, query_start, block_rows, 1)

        def inner(key_index, carried):
            query_acc, key_grads, value_grads = carried
            key_start = key_index * block_rows
            key_part = lax.dynamic_slice_in_dim(key_rows, key_start, block_rows, 0)
            value_part = lax.dynamic_slice_in_dim(value_rows, key_start, block_rows, 0)
            scores = block_scores(
                queries, key_rows, query_start, key_start, block_rows, score_scale
            )
            prob_soft = jnp.exp(scores - logsum_part[..., None])
            prob_low = prob_soft.astype(jnp.bfloat16)
            prob_grad = jnp.einsum(
                "qhd,khd->hqk", grad_part, value_part, preferred_element_type=jnp.float32
            )
            score_grad = (prob_soft * (prob_grad - delta_part[..., None])).astype(jnp.bfloat16)
            query_acc = (
                query_acc
                + jnp.einsum(
                    "hqk,khd->qhd", score_grad, key_part, preferred_element_type=jnp.float32
                )
                * score_scale
            )
            key_new = (
                jnp.einsum(
                    "hqk,qhd->khd", score_grad, query_part, preferred_element_type=jnp.float32
                )
                * score_scale
            )
            value_new = jnp.einsum(
                "hqk,qhd->khd", prob_low, grad_part, preferred_element_type=jnp.float32
            )
            key_old = lax.dynamic_slice_in_dim(key_grads, key_start, block_rows, 0)
            value_old = lax.dynamic_slice_in_dim(value_grads, key_start, block_rows, 0)
            key_grads = lax.dynamic_update_slice_in_dim(key_grads, key_old + key_new, key_start, 0)
            value_grads = lax.dynamic_update_slice_in_dim(
                value_grads, value_old + value_new, key_start, 0
            )
            return (query_acc, key_grads, value_grads)

        initial = (jnp.zeros((block_rows, heads, head_size), jnp.float32), key_grads, value_grads)
        query_acc, key_grads, value_grads = lax.fori_loop(0, query_index + 1, inner, initial)
        query_grads = lax.dynamic_update_slice_in_dim(query_grads, query_acc, query_start, 0)
        return (query_grads, key_grads, value_grads)

    zero_grads = jnp.zeros((seq_len, heads, head_size), jnp.float32)
    return lax.fori_loop(0, live_blocks, one_block, (zero_grads, zero_grads, zero_grads))


def body(
    x_given,
    dealing,
    seq_lengths,
    first_gain,
    query_weight,
    key_weight,
    value_weight,
    output_weight,
    second_gain,
    gate_weight,
    up_weight,
    down_weight,
    grad_output,
):
    groups = lax.axis_size("dp")
    pieces = lax.axis_size("tensor")
    group_index = lax.axis_index("dp")
    piece_index = lax.axis_index("tensor")
    seq_count, piece_rows, features = x_given.shape
    tokens = groups * piece_rows
    seq_len = tokens * pieces
    head_width = query_weight.shape[1]
    heads_local = head_width // HD
    block_rows = min(512, seq_len)
    score_scale = HD ** (-0.5)
    sequence = dealing[group_index]
    length = seq_lengths[sequence]
    live_blocks = (length + block_rows - 1) // block_rows
    outgoing = jnp.take(x_given, dealing, axis=0)
    arrived = lax.all_to_all(outgoing, "dp", split_axis=0, concat_axis=1, tiled=True)
    x_rows = arrived.reshape(tokens, features).astype(jnp.float32)
    row_ids = jnp.arange(tokens)
    positions_local = (
        row_ids // piece_rows * pieces + piece_index
    ) * piece_rows + row_ids % piece_rows
    live_rows = (positions_local < length).astype(jnp.float32)[:, None]
    columns = (
        lax.all_gather(gate_weight, "tensor", axis=1, tiled=True),
        lax.all_gather(up_weight, "tensor", axis=1, tiled=True),
        lax.all_gather(down_weight, "tensor", axis=1, tiled=True),
    )
    gathered = (
        lax.all_gather(first_gain, "dp", axis=0, tiled=True),
        lax.all_gather(second_gain, "dp", axis=0, tiled=True),
        lax.all_gather(query_weight, "dp", axis=0, tiled=True),
        lax.all_gather(key_weight, "dp", axis=0, tiled=True),
        lax.all_gather(value_weight, "dp", axis=0, tiled=True),
        lax.all_gather(output_weight, "dp", axis=0, tiled=True),
        lax.all_gather(columns[0], "dp", axis=0, tiled=True),
        lax.all_gather(columns[1], "dp", axis=0, tiled=True),
        lax.all_gather(columns[2], "dp", axis=0, tiled=True),
    )
    (
        gain_one,
        gain_two,
        query_full,
        key_full,
        value_full,
        out_full,
        gate_full,
        up_full,
        down_full,
    ) = gathered
    qkv_weight = jnp.concatenate([query_full, key_full, value_full], axis=1)
    scale_one = lax.rsqrt(jnp.mean(x_rows * x_rows, axis=-1, keepdims=True) + EPS)
    normed = (x_rows * scale_one * gain_one).astype(jnp.bfloat16)
    normed_full = lax.all_gather(
        normed.reshape(groups, 1, piece_rows, features), "tensor", axis=1, tiled=True
    ).reshape(seq_len, features)
    projected = row_dot(normed_full, qkv_weight)
    cosine, sine_table = tables(jnp.arange(seq_len, dtype=jnp.float32), HD)
    queries = rotary(
        projected[:, :head_width].reshape(seq_len, heads_local, HD), cosine, sine_table
    ).astype(jnp.bfloat16)
    key_rows = rotary(
        projected[:, head_width : 2 * head_width].reshape(seq_len, heads_local, HD),
        cosine,
        sine_table,
    ).astype(jnp.bfloat16)
    value_rows = (
        projected[:, 2 * head_width :].astype(jnp.bfloat16).reshape(seq_len, heads_local, HD)
    )
    mixed, log_sums = attend_forward(
        queries, key_rows, value_rows, live_blocks, block_rows, score_scale
    )
    mixed_low = mixed.reshape(seq_len, head_width).astype(jnp.bfloat16)
    mixed_major = tensor_major(mixed_low, groups, pieces, piece_rows)
    attention = lax.psum_scatter(
        dot_trans(mixed_major, out_full).astype(jnp.bfloat16),
        "tensor",
        scatter_dimension=0,
        tiled=True,
    ).astype(jnp.float32)
    hidden_one = x_rows + live_rows * attention
    scale_two = lax.rsqrt(jnp.mean(hidden_one * hidden_one, axis=-1, keepdims=True) + EPS)
    normed_two = (hidden_one * scale_two * gain_two).astype(jnp.bfloat16)
    gate_act = row_dot(normed_two, gate_full)
    up_act = row_dot(normed_two, up_full)
    sigmoid_act = jax.nn.sigmoid(gate_act)
    silu_act = gate_act * sigmoid_act
    hidden = (silu_act * up_act).astype(jnp.bfloat16)
    branch = dot_trans(hidden, down_full)
    result = hidden_one + live_rows * branch
    layer_out = result.astype(jnp.bfloat16).reshape(1, groups, 1, piece_rows, features)
    out_grad = grad_output.reshape(tokens, features).astype(jnp.float32)
    branch_grad = (live_rows * out_grad).astype(jnp.bfloat16)
    hidden_grad = row_dot(branch_grad, down_full)
    down_term = dot_first(branch_grad, hidden)
    gate_grad = (
        hidden_grad * up_act * sigmoid_act * (1.0 + gate_act * (1.0 - sigmoid_act))
    ).astype(jnp.bfloat16)
    up_grad = (hidden_grad * silu_act).astype(jnp.bfloat16)
    normed_two_grad = dot_trans(gate_grad, gate_full) + dot_trans(up_grad, up_full)
    gate_term = dot_first(normed_two, gate_grad)
    up_term = dot_first(normed_two, up_grad)
    hidden_one_grad, gain_two_term = rms_back(normed_two_grad, hidden_one, scale_two, gain_two)
    hidden_one_grad = hidden_one_grad + out_grad
    attention_grad = (live_rows * hidden_one_grad).astype(jnp.bfloat16)
    attention_full = lax.all_gather(
        attention_grad.reshape(groups, 1, piece_rows, features), "tensor", axis=1, tiled=True
    ).reshape(seq_len, features)
    mixed_grad = row_dot(attention_full, out_full).astype(jnp.bfloat16)
    out_term = dot_first(attention_full, mixed_low)
    query_grads, key_grads, value_grads = attend_backward(
        queries,
        key_rows,
        value_rows,
        mixed,
        log_sums,
        mixed_grad.reshape(seq_len, heads_local, HD),
        live_blocks,
        block_rows,
        score_scale,
    )
    query_back = (
        rotary_back(query_grads, cosine, sine_table)
        .reshape(seq_len, head_width)
        .astype(jnp.bfloat16)
    )
    key_back = (
        rotary_back(key_grads, cosine, sine_table).reshape(seq_len, head_width).astype(jnp.bfloat16)
    )
    value_back = value_grads.reshape(seq_len, head_width).astype(jnp.bfloat16)
    projected_grad = jnp.concatenate([query_back, key_back, value_back], axis=1)
    qkv_term = dot_first(normed_full, projected_grad)
    grad_major = tensor_major(projected_grad, groups, pieces, piece_rows)
    normed_grad = lax.psum_scatter(
        dot_trans(grad_major, qkv_weight).astype(jnp.bfloat16),
        "tensor",
        scatter_dimension=0,
        tiled=True,
    ).astype(jnp.float32)
    input_grad, gain_one_term = rms_back(normed_grad, x_rows, scale_one, gain_one)
    input_grad = input_grad + hidden_one_grad
    returned = lax.all_to_all(
        input_grad.astype(jnp.bfloat16).reshape(groups, piece_rows, features),
        "dp",
        split_axis=0,
        concat_axis=0,
        tiled=True,
    )
    grad_in = jnp.zeros_like(x_given).at[dealing].set(returned)
    gain_pair = jnp.stack([gain_one_term, gain_two_term], axis=1)
    query_term = qkv_term[:, :head_width]
    key_term = qkv_term[:, head_width : 2 * head_width]
    value_term = qkv_term[:, 2 * head_width :]
    summed = (
        lax.psum_scatter(
            gain_pair.astype(jnp.bfloat16), "dp", scatter_dimension=0, tiled=True
        ).astype(jnp.float32),
        lax.psum_scatter(
            query_term.astype(jnp.bfloat16), "dp", scatter_dimension=0, tiled=True
        ).astype(jnp.float32),
        lax.psum_scatter(
            key_term.astype(jnp.bfloat16), "dp", scatter_dimension=0, tiled=True
        ).astype(jnp.float32),
        lax.psum_scatter(
            value_term.astype(jnp.bfloat16), "dp", scatter_dimension=0, tiled=True
        ).astype(jnp.float32),
        lax.psum_scatter(
            out_term.astype(jnp.bfloat16), "dp", scatter_dimension=0, tiled=True
        ).astype(jnp.float32),
        lax.psum_scatter(
            gate_term.astype(jnp.bfloat16), "dp", scatter_dimension=0, tiled=True
        ).astype(jnp.float32),
        lax.psum_scatter(
            up_term.astype(jnp.bfloat16), "dp", scatter_dimension=0, tiled=True
        ).astype(jnp.float32),
        lax.psum_scatter(
            down_term.astype(jnp.bfloat16), "dp", scatter_dimension=0, tiled=True
        ).astype(jnp.float32),
    )
    across = (
        lax.psum_scatter(
            jnp.tile(summed[0], (1, pieces)).astype(jnp.bfloat16),
            "tensor",
            scatter_dimension=1,
            tiled=True,
        ).astype(jnp.float32),
        lax.psum_scatter(
            summed[5].astype(jnp.bfloat16), "tensor", scatter_dimension=1, tiled=True
        ).astype(jnp.float32),
        lax.psum_scatter(
            summed[6].astype(jnp.bfloat16), "tensor", scatter_dimension=1, tiled=True
        ).astype(jnp.float32),
        lax.psum_scatter(
            summed[7].astype(jnp.bfloat16), "tensor", scatter_dimension=1, tiled=True
        ).astype(jnp.float32),
    )
    gain_sums = across[0]
    query_sum, key_sum, value_sum, out_sum = (summed[1], summed[2], summed[3], summed[4])
    gate_sum, up_sum, down_sum = (across[1], across[2], across[3])
    return (
        layer_out,
        grad_in,
        gain_sums[:, 0],
        query_sum,
        key_sum,
        value_sum,
        out_sum,
        gain_sums[:, 1],
        gate_sum,
        up_sum,
        down_sum,
    )


MESH = pl.DeviceIdType.MESH
BF = jnp.bfloat16
F32 = jnp.float32
NN = (((1,), (0,)), ((), ()))
NT = (((1,), (1,)), ((), ()))
TN = (((0,), (0,)), ((), ()))
LOG2E = 1.4426950408889634
ROWS = 256


def mm(kind, left_side, right_side):
    return lax.dot_general(left_side, right_side, kind, preferred_element_type=F32)


def fused_kernel(
    shape,
    deal, lens, x_ref, dy_ref, g1, g2, wq, wk, wv, wo, wg, wu, wd, tab,
    lo_ref, gi_ref, dq_out, dk_out, dv_out, do_out, dg_out, du_out, dd_out, dgain_out,
    xs, xbuf, dybuf, src_a, src_f, w_a, w_o, w_f, wp, wop, eqk, ev, cosb, sinb, ct, st,
    abuf, qb, kb, vb, vt, ot, ob, lse, own, sb1, sb2, rb1, rb2, x1b, r1b, r2b, bbuf, dfb,
    facc, uacc, act, dob, delta, rx_a, ry_a, ry2_a, rz_a, rx_o, ry_o, ry2_o, rz_o,
    rx_f, ry_f, ry2_f, rz_f, ret, gs, gr, rsum,
    a2a_s, a2a_r, dy_s, dy_r, ag_z, ag_x, ag_y, ag_d, ag_s, rs_x, rs_y, rs_z, rs_s,
    ex_s, ex_r, lo_s, lo_r, ret_s, ret_r, gg_s, gg_r,
):
    nz, nf, dim, hw, chunk, nrow = shape
    groups = 4 * nz
    seq_len = 64 * groups
    half = dim // 2
    nrb = seq_len // ROWS
    kd = nz // 2
    dp = lax.axis_index("dp")
    y = lax.axis_index("tensor")
    z = dp // 4
    x = (dp // 2) % 2
    c = dp % 2
    xb, yb, oth = 1 - x, 1 - y, 1 - c
    home = c == y
    away = c != y
    slot = (z * 2 + x) * 2 + y
    score_scale = HD ** (-0.5)

    def dev(z_, x_, c_, y_):
        return ((z_ * 2 + x_) * 2 + c_, y_)

    partner = dev(z, x, oth, y)
    xnbr = dev(z, xb, c, y)
    ynbr = dev(z, x, c, yb)
    swap = dev(z, x, oth, yb)

    def rc(src, dst, ss, rs, to):
        return pltpu.make_async_remote_copy(
            src_ref=src, dst_ref=dst, send_sem=ss, recv_sem=rs, device_id=to, device_id_type=MESH
        )

    def wait(ref, sem):
        pltpu.make_async_copy(ref, ref, sem).wait()

    bar = pltpu.get_barrier_semaphore()
    ndev = groups * 2

    def greet(i, _):
        t = lax.rem(dp * 2 + y + i, ndev)
        pl.semaphore_signal(bar, inc=1, device_id=(t // 2, t % 2), device_id_type=MESH)
        return 0

    lax.fori_loop(1, ndev, greet, 0)
    pl.semaphore_wait(bar, ndev - 1)

    def stage(j, _):
        xs[j] = x_ref[deal[j]]
        return 0

    lax.fori_loop(0, groups, stage, 0)

    def deal_out(i, _):
        j = lax.rem(slot + i, groups)
        dpd = (j // 2) * 2 + y
        td = j % 2
        same = (dpd == dp) & (td == y)

        @pl.when(same)
        def _():
            pltpu.make_async_copy(xs.at[j], xbuf.at[dp], a2a_r).start()

        @pl.when(jnp.logical_not(same))
        def _():
            rc(xs.at[j], xbuf.at[dp], a2a_s, a2a_r, (dpd, td)).start()

        return 0

    lax.fori_loop(0, groups, deal_out, 0)

    def unit(k):
        if isinstance(k, str):
            return (src_a, w_a, 0) if k == "a" else (wo, w_o, 1)
        return (src_f.at[k], w_f.at[k], k + 2)

    def zsend(k):
        src, buf, n = unit(k)
        for i in range(1, nz):
            zt = lax.rem(z + i, nz)
            rc(src, buf.at[z, x, c], ag_s.at[n, i - 1], ag_z.at[n], dev(zt, x, y, y)).start()

        @pl.when(home)
        def _():
            pltpu.make_async_copy(src, buf.at[z, x, c], ag_z.at[n]).start()

        @pl.when(away)
        def _():
            rc(src, buf.at[z, x, c], ag_s.at[n, nz - 1], ag_z.at[n], dev(z, x, y, y)).start()

    def ag1(k):
        src, buf, n = unit(k)

        @pl.when(home)
        def _():
            wait(buf.at[:, x], ag_z.at[n])
            rc(buf.at[:, x], buf.at[:, x], ag_s.at[n, nz], ag_y.at[n], ynbr).start()
            rc(buf.at[:, x], buf.at[:, x], ag_s.at[n, nz + 1], ag_x.at[n], xnbr).start()

    def ag2(k):
        src, buf, n = unit(k)

        @pl.when(home)
        def _():
            wait(buf.at[:, xb], ag_x.at[n])
            part = buf.at[pl.ds(0, kd), xb]
            rc(part, part, ag_s.at[n, nz + 2], ag_d.at[n, 0], ynbr).start()

        @pl.when(away)
        def _():
            wait(buf.at[:, x], ag_y.at[n])
            part = buf.at[pl.ds(kd, nz - kd), x]
            rc(part, part, ag_s.at[n, nz + 2], ag_d.at[n, 1], xnbr).start()

    def ag3(k):
        src, buf, n = unit(k)

        @pl.when(away)
        def _():
            wait(buf.at[pl.ds(0, kd), xb], ag_d.at[n, 0])
            wait(buf.at[pl.ds(kd, nz - kd), xb], ag_d.at[n, 1])

    def ag_done(k):
        src, buf, n = unit(k)
        for i in range(nz - 1):
            wait(src, ag_s.at[n, i])

        @pl.when(home)
        def _():
            wait(buf.at[:, x], ag_s.at[n, nz])
            wait(buf.at[:, x], ag_s.at[n, nz + 1])
            wait(buf.at[pl.ds(0, kd), xb], ag_s.at[n, nz + 2])

        @pl.when(away)
        def _():
            wait(src, ag_s.at[n, nz - 1])
            wait(buf.at[pl.ds(kd, nz - kd), x], ag_s.at[n, nz + 2])

    def rs_unit(k):
        if isinstance(k, str):
            if k == "a":
                return (w_a, rx_a, ry_a, ry2_a, rz_a, 0)
            return (w_o, rx_o, ry_o, ry2_o, rz_o, 1)
        return (w_f.at[k], rx_f.at[k], ry_f.at[k], ry2_f.at[k], rz_f.at[k], k + 2)

    lo_z = pl.ds(0, kd)
    hi_z = pl.ds(kd, nz - kd)

    def at_unit(ref, k, *spot):
        spot = spot if isinstance(k, str) else (k,) + spot
        return ref[spot if spot else ...].astype(F32)

    def put_unit(ref, k, total, *spot):
        spot = spot if isinstance(k, str) else (k,) + spot
        ref[spot if spot else ...] = total.astype(BF)

    def rs_refs(k):
        if isinstance(k, str):
            return (w_a, rx_a, ry_a, ry2_a) if k == "a" else (w_o, rx_o, ry_o, ry2_o)
        return w_f, rx_f, ry_f, ry2_f

    every = slice(None)

    def by_x(step):
        for v in range(2):
            pl.when(x == v)(functools.partial(step, v, 1 - v))

    def rs0(k):
        g, rx, ry, ry2, rz, n = rs_unit(k)
        rc(g.at[hi_z, xb], rx.at[hi_z], rs_s.at[n, 0], rs_x.at[n, 1], xnbr).start()

        @pl.when(away)
        def _():
            rc(g.at[lo_z], ry, rs_s.at[n, 1], rs_y.at[n, 0], ynbr).start()

    def rs1(k):
        g, rx, ry, ry2, rz, n = rs_unit(k)
        g_all, rx_all, ry_all, ry2_all = rs_refs(k)

        @pl.when(away)
        def _():
            wait(rx.at[hi_z], rs_x.at[n, 1])

            @by_x
            def _(v, vb):
                put_unit(ry2_all, k, at_unit(g_all, k, hi_z, v) + at_unit(rx_all, k, hi_z))

            rc(ry2, ry2, rs_s.at[n, 2], rs_y.at[n, 1], ynbr).start()

        @pl.when(home)
        def _():
            wait(ry, rs_y.at[n, 0])

            @by_x
            def _(v, vb):
                total = at_unit(g_all, k, lo_z, vb) + at_unit(ry_all, k, every, vb)
                put_unit(ry_all, k, total, every, vb)

            rc(ry.at[:, xb], rx.at[lo_z], rs_s.at[n, 2], rs_x.at[n, 0], xnbr).start()

    def rs2(k):
        g, rx, ry, ry2, rz, n = rs_unit(k)
        g_all, rx_all, ry_all, ry2_all = rs_refs(k)

        @pl.when(home)
        def _():
            wait(rx.at[hi_z], rs_x.at[n, 1])
            wait(ry2, rs_y.at[n, 1])

            @by_x
            def _(v, vb):
                total = at_unit(g_all, k, hi_z, v) + at_unit(rx_all, k, hi_z) + at_unit(ry2_all, k)
                put_unit(rx_all, k, total, hi_z)

            wait(rx.at[lo_z], rs_x.at[n, 0])

            @by_x
            def _(v, vb):
                total = at_unit(g_all, k, lo_z, v) + at_unit(ry_all, k, every, v)
                put_unit(rx_all, k, total + at_unit(rx_all, k, lo_z), lo_z)

            for i in range(1, nz):
                zt = lax.rem(z + i, nz)
                for cc in range(2):
                    rc(
                        rx.at[zt, cc], rz.at[z], rs_s.at[n, 3 + 2 * (i - 1) + cc], rs_z.at[n],
                        dev(zt, x, cc, y),
                    ).start()
            rc(rx.at[z, oth], rz.at[z], rs_s.at[n, 2 * nz + 1], rs_z.at[n], partner).start()
            pltpu.make_async_copy(rx.at[z, c], rz.at[z], rs_z.at[n]).start()

    def rs_done(k):
        g, rx, ry, ry2, rz, n = rs_unit(k)
        wait(rx.at[hi_z], rs_s.at[n, 0])

        @pl.when(away)
        def _():
            wait(ry, rs_s.at[n, 1])
            wait(ry2, rs_s.at[n, 2])

        @pl.when(home)
        def _():
            wait(rx.at[lo_z], rs_s.at[n, 2])
            for i in range(2 * (nz - 1) + 1):
                wait(rz.at[0], rs_s.at[n, 3 + i])

    def rs3(k):
        g, rx, ry, ry2, rz, n = rs_unit(k)
        wait(rz, rs_z.at[n])
        total = None
        for i in range(nz):
            part = (rz[i] if isinstance(k, str) else rz_f[k, i]).astype(F32)
            total = part if total is None else total + part
        return total

    gain1 = g1[...]
    gain2 = g2[...]
    for i, w in enumerate((wq, wk, wv)):
        src_a[:, i * hw : (i + 1) * hw] = (w[...].astype(F32) * gain1).astype(BF)
    zsend("a")
    zsend("o")

    @pl.when(home)
    def _():
        pltpu.make_async_copy(dy_ref, dybuf, dy_r).start()

    @pl.when(away)
    def _():
        rc(dy_ref, dybuf, dy_s, dy_r, swap).start()

    for f in range(nf):
        cols = slice(f * chunk, (f + 1) * chunk)
        src_f[f, :, 0:chunk] = (wg[:, cols].astype(F32) * gain2).astype(BF)
        src_f[f, :, chunk : 2 * chunk] = (wu[:, cols].astype(F32) * gain2).astype(BF)
        src_f[f, :, 2 * chunk : 3 * chunk] = wd[:, cols]

    def rope_rows(i, _):
        ca, sa = tab[0, pl.ds(i, 1), :], tab[1, pl.ds(i, 1), :]
        cb, sb = tab[2], tab[3]
        at = pl.ds(pl.multiple_of(i * 32, 32), 32)
        cosb[at, :] = ca * cb - sa * sb
        sinb[at, :] = sa * cb + ca * sb
        return 0

    lax.fori_loop(0, seq_len // 32, rope_rows, 0)
    for i in range(nrb):
        at = slice(i * ROWS, (i + 1) * ROWS)
        ct[:, at] = cosb[at, :].T[0:32]
        st[:, at] = sinb[at, :].T[0:32]
    pw = wop.shape[1]
    row = lax.broadcasted_iota(jnp.int32, (hw, pw), 0)
    col = lax.broadcasted_iota(jnp.int32, (hw, pw), 1)
    low = col & 31
    spot = ((col >> 8) * 4 + ((col >> 5) & 3)) * HD + ((col >> 7) & 1) * (HD // 2) + low
    eqk[...] = jnp.where((row == spot) & (low < HD // 2), 1.0, 0.0).astype(BF)
    low = col & 63
    ev[...] = jnp.where((row == (col >> 6) * HD + low) & (low < HD), 1.0, 0.0).astype(BF)
    facc[...] = jnp.zeros_like(facc)
    uacc[...] = jnp.zeros_like(uacc)

    length = lens[deal[slot]]

    def live_at(i):
        at = (i * 2 + c) * 32 + lax.broadcasted_iota(jnp.int32, (32, 1), 0)
        return at < length

    def mean(values):
        return jnp.mean(values, axis=1, keepdims=True)

    def swap_start(n, src, dst):
        rc(src, dst, ex_s.at[n], ex_r.at[n], partner).start()

    def blk(i):
        return pl.ds(i * (ROWS // 64), ROWS // 64)

    ag1("a")
    ag1("o")
    zsend(0)
    zsend(1)
    wait(xbuf, a2a_r)
    wait(dybuf, dy_r)

    def norm_one(i, _):
        rows_now = xbuf[i].astype(F32)
        r = lax.rsqrt(mean(rows_now * rows_now) + EPS)
        r1b[i] = jnp.broadcast_to(r, (32, 128))
        abuf[i, c] = (rows_now * r).astype(BF)
        dfb[i, c] = jnp.where(live_at(i), dybuf[i], jnp.zeros((32, dim), BF))
        return 0

    lax.fori_loop(0, groups, norm_one, 0, unroll=2)
    swap_start(0, abuf.at[:, c], abuf.at[:, c])
    swap_start(1, dfb.at[:, c], dfb.at[:, c])
    ag2("a")
    ag1(0)
    ag3("a")
    for i in range(3):
        e = eqk if i < 2 else ev
        wp[:, i * pw : (i + 1) * pw] = mm(
            NN, w_a[:, :, :, :, i * hw : (i + 1) * hw].reshape(dim, hw), e[...]
        ).astype(BF)
    wait(abuf.at[:, oth], ex_r.at[0])

    query_scale = score_scale * LOG2E
    lane64 = lax.broadcasted_iota(jnp.int32, (ROWS, pw), 1) & 63

    def project(i, _):
        a = abuf[blk(i)].reshape(ROWS, dim)
        at = pl.ds(pl.multiple_of(i * ROWS, ROWS), ROWS)
        cos, sin = cosb[at, :], sinb[at, :]
        for t, (dst, scale) in enumerate(((qb, query_scale), (kb, 1.0))):
            u = mm(NN, a, wp[:, t * pw : (t + 1) * pw]) * scale
            for g in range(pw // 256):
                f1 = u[:, g * 256 : g * 256 + 128]
                f2 = u[:, g * 256 + 128 : g * 256 + 256]
                dst[blk(i), :, :, g * 256 : g * 256 + 128] = (
                    (f1 * cos - f2 * sin).astype(BF).reshape(ROWS // 64, 2, 32, 128)
                )
                dst[blk(i), :, :, g * 256 + 128 : g * 256 + 256] = (
                    (f2 * cos + f1 * sin).astype(BF).reshape(ROWS // 64, 2, 32, 128)
                )
        v = mm(NN, a, wp[:, 2 * pw : 3 * pw])
        v = jnp.where(lane64 == HD, 1.0, v).astype(BF)
        vb[blk(i)] = v.reshape(ROWS // 64, 2, 32, pw)
        vt[:, at] = v.T
        return 0

    lax.fori_loop(0, nrb, project, 0)
    zsend(2)
    ag1(1)
    ag2("o")

    lane = lax.broadcasted_iota(jnp.int32, (ROWS, 256), 1)
    diag = lax.broadcasted_iota(jnp.int32, (ROWS, ROWS), 0) <= lax.broadcasted_iota(
        jnp.int32, (ROWS, ROWS), 1
    )

    def rows_of(ref, first, count, lanes):
        return ref[pl.ds(first // 64, count // 64), :, :, lanes].reshape(count, 256)

    def attend(i):
        keys = (i + 1) * ROWS

        def group(g, _):
            lanes = pl.ds(pl.multiple_of(g * 256, 256), 256)
            q = rows_of(qb, i * ROWS, ROWS, lanes)
            for hh in range(4):
                qm = jnp.where(((lane >> 5) & 3) == hh, q, jnp.zeros_like(q))
                sd = mm(NT, rows_of(kb, i * ROWS, ROWS, lanes), qm)
                sd = jnp.where(diag, sd, -1e30)
                top = jnp.max(sd, axis=0, keepdims=True)
                if i:
                    s = mm(NT, rows_of(kb, 0, i * ROWS, lanes), qm)
                    top = jnp.maximum(top, jnp.max(s, axis=0, keepdims=True))
                    p = jnp.concatenate(
                        [jnp.exp2(s - top).astype(BF), jnp.exp2(sd - top).astype(BF)], axis=0
                    )
                else:
                    p = jnp.exp2(sd - top).astype(BF)
                hs = pl.multiple_of(g * 256 + hh * 64, 64)
                o = mm(NN, vt[pl.ds(hs, 64), 0:keys], p)
                total = o[HD : HD + 1, :]
                ot[pl.ds(hs, 64), i * ROWS : keys] = (o * (1.0 / total)).astype(BF)
                lse[pl.ds(g * 4 + hh, 1), i * ROWS : keys] = top + jnp.log2(total)
            return 0

        lax.fori_loop(0, pw // 256, group, 0)

    def during_one():
        ag2(0)
        ag3("o")
        wop[...] = mm(NN, w_o[...].reshape(dim, hw), ev[...]).astype(BF)
        ag1(2)
        zsend(3)
        zsend(4)

    def during_two():
        ag2(1)
        ag1(3)

    def with_steps(part, steps):
        for i in range(nrb):
            part(i)
            for at, step in steps:
                if min(at, nrb - 1) == i:
                    step()

    with_steps(attend, ((1, during_one), (2, during_two)))

    def turn(i, _):
        at = pl.ds(pl.multiple_of(i * ROWS, ROWS), ROWS)
        ob[blk(i)] = ot[:, at].T.reshape(ROWS // 64, 2, 32, pw)
        return 0

    lax.fori_loop(0, nrb, turn, 0)

    half_rows = ROWS // 32

    def att_other(j, _):
        at = pl.ds(j * half_rows, half_rows)
        o = ob[at, oth].reshape(ROWS, pw)
        sb1[at] = mm(NT, o, wop[...]).astype(BF).reshape(half_rows, 32, dim)
        return 0

    def att_own(j, _):
        at = pl.ds(j * half_rows, half_rows)
        o = ob[at, c].reshape(ROWS, pw)
        own[at] = mm(NT, o, wop[...]).reshape(half_rows, 32, dim)
        return 0

    lax.fori_loop(0, groups // half_rows, att_other, 0)
    swap_start(2, sb1, rb1)
    lax.fori_loop(0, groups // half_rows, att_own, 0)
    ag1(4)
    wait(rb1, ex_r.at[2])

    def norm_two(i, _):
        att = own[i] + rb1[i].astype(F32)
        x1 = xbuf[i].astype(F32) + jnp.where(live_at(i), att, 0.0)
        x1b[i] = x1
        r = lax.rsqrt(mean(x1 * x1) + EPS)
        r2b[i] = jnp.broadcast_to(r, (32, 128))
        bbuf[i, c] = (x1 * r).astype(BF)
        return 0

    lax.fori_loop(0, groups, norm_two, 0, unroll=2)
    swap_start(3, bbuf.at[:, c], bbuf.at[:, c])
    wait(dfb.at[:, oth], ex_r.at[1])
    ag2(2)
    wait(bbuf.at[:, oth], ex_r.at[3])

    def ffn(f, _):
        ag3(f)

        def one(i, _):
            b = bbuf[blk(i)].reshape(ROWS, dim)
            d = dfb[blk(i)].reshape(ROWS, dim)
            w_gu = w_f[f, :, :, :, :, 0 : 2 * chunk].reshape(dim, 2 * chunk)
            w_d = w_f[f, :, :, :, :, 2 * chunk : 3 * chunk].reshape(dim, chunk)
            gu = mm(NN, b, w_gu)
            dh = mm(NN, d, w_d)
            gate, up = gu[:, 0:chunk], gu[:, chunk:]
            sg = jax.nn.sigmoid(gate)
            silu = gate * sg
            hid = (silu * up).astype(BF)
            dgate = (dh * up * sg * (1.0 + gate * (1.0 - sg))).astype(BF)
            dup = (dh * silu).astype(BF)
            at = pl.ds(pl.multiple_of(i * ROWS, ROWS), ROWS)
            act[at, 0:chunk] = dgate
            act[at, chunk : 2 * chunk] = dup
            act[at, 2 * chunk : 3 * chunk] = hid
            facc[blk(i)] += mm(NT, hid, w_d).reshape(ROWS // 64, 2, 32, dim)
            dgu = jnp.concatenate([dgate, dup], axis=1)
            uacc[blk(i)] += mm(NT, dgu, w_gu).reshape(ROWS // 64, 2, 32, dim)
            return 0

        lax.fori_loop(0, nrb, one, 0)
        ag_done(f)
        for m in range(2):
            feats = slice(m * half, (m + 1) * half)
            zs = slice(m * nz // 2, (m + 1) * nz // 2)
            left = bbuf[:, :, :, feats].reshape(seq_len, half)
            t = mm(TN, left, act[:, 0 : 2 * chunk]).astype(BF)
            w_f[f, zs, :, :, :, 0 : 2 * chunk] = t.reshape(nz // 2, 2, 2, nrow, 2 * chunk)
            left = dfb[:, :, :, feats].reshape(seq_len, half)
            t = mm(TN, left, act[:, 2 * chunk : 3 * chunk]).astype(BF)
            w_f[f, zs, :, :, :, 2 * chunk : 3 * chunk] = t.reshape(nz // 2, 2, 2, nrow, chunk)
        rs0(f)

        @pl.when(f + 3 < nf)
        def _():
            ag2(f + 3)

        @pl.when(f >= 1)
        def _():
            rs1(f - 1)

        @pl.when(f >= 2)
        def _():
            rs2(f - 2)

        return 0

    lax.fori_loop(0, nf, ffn, 0)

    wait(sb1, ex_s.at[2])

    def cast_u(i, _):
        sb1[i] = uacc[i, oth].astype(BF)
        return 0

    def cast_f(i, _):
        sb2[i] = facc[i, oth].astype(BF)
        return 0

    lax.fori_loop(0, groups, cast_u, 0)
    swap_start(4, sb1, rb1)
    lax.fori_loop(0, groups, cast_f, 0)
    swap_start(5, sb2, rb2)
    rs1(nf - 1)

    @pl.when(home)
    def _():
        wait(xs.at[pl.ds(0, groups - 1)], a2a_s)

    @pl.when(away)
    def _():
        wait(xs, a2a_s)

    wait(rb1, ex_r.at[4])
    wait(rb2, ex_r.at[5])
    wait(bbuf.at[:, c], ex_s.at[3])

    def norm_three(i, _):
        alive = live_at(i)
        x1 = x1b[i]
        r = r2b[i][:, 0:1]
        n = x1 * r
        u = uacc[i, c] + rb1[i].astype(F32)
        dx1 = dybuf[i].astype(F32) + r * (u - n * mean(u * n))
        bbuf[i, c] = jnp.where(alive, dx1, 0.0).astype(BF)
        ffn_out = facc[i, c] + rb2[i].astype(F32)
        xs[i] = (x1 + jnp.where(alive, ffn_out, 0.0)).astype(BF)
        x1b[i] = dx1
        return 0

    lax.fori_loop(0, groups, norm_three, 0, unroll=2)
    swap_start(6, bbuf.at[:, c], bbuf.at[:, c])

    @pl.when(home)
    def _():
        pltpu.make_async_copy(xs, lo_ref, lo_r).start()

    @pl.when(away)
    def _():
        rc(xs, lo_ref, lo_s, lo_r, swap).start()

    rs2(nf - 2)

    def turn_k(i, _):
        at = pl.ds(pl.multiple_of(i * ROWS, ROWS), ROWS)
        t = kb[blk(i)].reshape(ROWS, pw).T
        for h in range(pw // 64):
            for part in range(2):
                first = (h // 4) * 256 + part * 128 + (h % 4) * 32
                vt[h * 64 + part * 32 : h * 64 + part * 32 + 32, at] = t[first : first + 32]
        return 0

    lax.fori_loop(0, nrb, turn_k, 0)
    facc[...] = jnp.zeros_like(facc)
    uacc[...] = jnp.zeros_like(uacc)
    heads16 = lax.broadcasted_iota(jnp.int32, (16, pw), 0)
    pick = jnp.where(
        (lax.broadcasted_iota(jnp.int32, (16, pw), 1) >> 6) == heads16, 1.0, 0.0
    ).astype(BF)
    wait(bbuf.at[:, oth], ex_r.at[6])

    def out_back(i, _):
        at = pl.ds(pl.multiple_of(i * ROWS, ROWS), ROWS)
        t = mm(NN, bbuf[blk(i)].reshape(ROWS, dim), wop[...]).astype(BF)
        dob[blk(i)] = t.reshape(ROWS // 64, 2, 32, pw)
        prod = t.astype(F32) * ob[blk(i)].reshape(ROWS, pw).astype(F32)
        delta[:, at] = mm(NT, pick, prod.astype(BF))
        return 0

    lax.fori_loop(0, nrb, out_back, 0)
    ag_done("o")
    for m in range(2):
        left = bbuf[:, :, :, m * half : (m + 1) * half].reshape(seq_len, half)
        t = mm(TN, left, ob[...].reshape(seq_len, pw)).astype(BF)
        zs = slice(m * nz // 2, (m + 1) * nz // 2)
        w_o[zs] = mm(NT, t, ev[...]).astype(BF).reshape(nz // 2, 2, 2, nrow, hw)
    rs0("o")

    def attend_back(i):
        keys = (i + 1) * ROWS

        def group(g, _):
            lanes = pl.ds(pl.multiple_of(g * 256, 256), 256)
            q = rows_of(qb, i * ROWS, ROWS, lanes)
            d = rows_of(dob, i * ROWS, ROWS, lanes)
            for hh in range(4):
                qm = jnp.where(((lane >> 5) & 3) == hh, q, jnp.zeros_like(q))
                dm = jnp.where((lane >> 6) == hh, d, jnp.zeros_like(d))
                row_lse = lse[pl.ds(g * 4 + hh, 1), i * ROWS : keys]
                row_delta = delta[pl.ds(g * 4 + hh, 1), i * ROWS : keys]

                def part(first, count, masked):
                    s = mm(NT, rows_of(kb, first, count, lanes), qm)
                    if masked:
                        s = jnp.where(diag, s, -1e30)
                    p = jnp.exp2(s - row_lse)
                    dp_ = mm(NT, rows_of(vb, first, count, lanes), dm)
                    ds = (p * (dp_ - row_delta)).astype(BF)
                    at = pl.ds(first // 64, count // 64)
                    uacc[at, :, :, lanes] += mm(NN, p.astype(BF), dm).reshape(
                        count // 64, 2, 32, 256
                    )
                    facc[at, :, :, lanes] += mm(NN, ds, qm).reshape(count // 64, 2, 32, 256)
                    return ds

                ds = part(i * ROWS, ROWS, True)
                if i:
                    ds = jnp.concatenate([part(0, i * ROWS, False), ds], axis=0)
                hs = pl.multiple_of(g * 256 + hh * 64, 64)
                t = mm(NN, vt[pl.ds(hs, 64), 0:keys], ds) * score_scale
                c_now, s_now = ct[:, i * ROWS : keys], st[:, i * ROWS : keys]
                f1, f2 = t[0:32], t[32:64]
                hs = pl.multiple_of(g * 256 + hh * 32, 32)
                ot[pl.ds(hs, 32), i * ROWS : keys] = (f1 * c_now + f2 * s_now).astype(BF)
                ot[pl.ds(hs + 128, 32), i * ROWS : keys] = (f2 * c_now - f1 * s_now).astype(BF)
            return 0

        lax.fori_loop(0, pw // 256, group, 0)

    with_steps(
        attend_back,
        ((0, lambda: rs2(nf - 1)), (1, lambda: rs1("o")), (2, lambda: rs2("o"))),
    )

    def turn_back(i, _):
        at = pl.ds(pl.multiple_of(i * ROWS, ROWS), ROWS)
        qb[blk(i)] = ot[:, at].T.reshape(ROWS // 64, 2, 32, pw)
        vb[blk(i)] = uacc[blk(i), :, :, 0:pw].astype(BF)
        cos, sin = cosb[at, :], sinb[at, :]
        for g in range(pw // 256):
            f1 = facc[blk(i), :, :, g * 256 : g * 256 + 128].reshape(ROWS, 128)
            f2 = facc[blk(i), :, :, g * 256 + 128 : g * 256 + 256].reshape(ROWS, 128)
            kb[blk(i), :, :, g * 256 : g * 256 + 128] = (
                ((f1 * cos + f2 * sin) * (1.0 / LOG2E)).astype(BF).reshape(ROWS // 64, 2, 32, 128)
            )
            kb[blk(i), :, :, g * 256 + 128 : g * 256 + 256] = (
                ((f2 * cos - f1 * sin) * (1.0 / LOG2E)).astype(BF).reshape(ROWS // 64, 2, 32, 128)
            )
        return 0

    lax.fori_loop(0, nrb, turn_back, 0)
    ag_done("a")
    for t, (src, e) in enumerate(((qb, eqk), (kb, eqk), (vb, ev))):
        for m in range(2):
            left = abuf[:, :, :, m * half : (m + 1) * half].reshape(seq_len, half)
            part = mm(TN, left, src[...].reshape(seq_len, pw)).astype(BF)
            zs = slice(m * nz // 2, (m + 1) * nz // 2)
            w_a[zs, :, :, :, t * hw : (t + 1) * hw] = (
                mm(NT, part, e[...]).astype(BF).reshape(nz // 2, 2, 2, nrow, hw)
            )
    rs0("a")
    wait(sb1, ex_s.at[4])

    def da_rows(at, which):
        total = None
        for t, src in enumerate((qb, kb, vb)):
            term = mm(NT, src[at, which].reshape(ROWS, pw), wp[:, t * pw : (t + 1) * pw])
            total = term if total is None else total + term
        return total.reshape(half_rows, 32, dim)

    def da_other(j, _):
        at = pl.ds(j * half_rows, half_rows)
        sb1[at] = da_rows(at, oth).astype(BF)
        return 0

    def da_own(j, _):
        at = pl.ds(j * half_rows, half_rows)
        own[at] = da_rows(at, c)
        return 0

    lax.fori_loop(0, groups // half_rows, da_other, 0)
    swap_start(7, sb1, rb1)
    lax.fori_loop(0, groups // half_rows, da_own, 0)

    @pl.when(away)
    def _():
        wait(xs, lo_s)

    wait(lo_ref, lo_r)
    wait(rb1, ex_r.at[7])

    def norm_four(i, _):
        rows_now = xbuf[i].astype(F32)
        r = r1b[i][:, 0:1]
        n = rows_now * r
        u = own[i] + rb1[i].astype(F32)
        dx = x1b[i] + r * (u - n * mean(u * n))
        xs[i] = dx.astype(BF)
        same = (i == dp) & (c == y)

        @pl.when(same)
        def _():
            pltpu.make_async_copy(xs.at[i], ret.at[slot], ret_r).start()

        @pl.when(jnp.logical_not(same))
        def _():
            rc(xs.at[i], ret.at[slot], ret_s, ret_r, (i, c)).start()

        return 0

    lax.fori_loop(0, groups, norm_four, 0)
    rs1("a")

    def finish_f(f, total):
        sums = jnp.zeros((nrow, 1), F32) if total is None else total
        t = rs3(f)
        at = pl.ds(pl.multiple_of(f * chunk, chunk), chunk)
        dg, du = t[:, 0:chunk], t[:, chunk : 2 * chunk]
        dg_out[:, at] = dg * gain2
        du_out[:, at] = du * gain2
        dd_out[:, at] = t[:, 2 * chunk : 3 * chunk]
        both = dg * wg[:, at].astype(F32) + du * wu[:, at].astype(F32)
        return sums + jnp.sum(both, axis=1, keepdims=True)

    sums2 = lax.fori_loop(0, nf, finish_f, jnp.zeros((nrow, 1), F32))
    rs2("a")
    do_out[...] = rs3("o")
    t = rs3("a")
    sums1 = jnp.zeros((nrow, 1), F32)
    for i, (w, out) in enumerate(((wq, dq_out), (wk, dk_out), (wv, dv_out))):
        part = t[:, i * hw : (i + 1) * hw]
        out[...] = part * gain1
        sums1 = sums1 + jnp.sum(part * w[...].astype(F32), axis=1, keepdims=True)
    first_half = lax.broadcasted_iota(jnp.int32, (nrow, 128), 1) < 64
    gs[...] = jnp.where(first_half, sums1, sums2)
    rc(gs, gr, gg_s, gg_r, ynbr).start()

    wait(ret, ret_r)

    def restore(s, _):
        def find(j, at):
            return jnp.where(deal[j] == s, j, at)

        gi_ref[s] = ret[lax.fori_loop(0, groups, find, 0)]
        return 0

    lax.fori_loop(0, groups, restore, 0)
    wait(gr, gg_r)
    dgain_out[...] = gs[...] + gr[...]

    wait(gs, gg_s)
    for f in range(nf):
        rs_done(f)
    rs_done("o")
    rs_done("a")

    @pl.when(away)
    def _():
        wait(dybuf, dy_s)

    @pl.when(home)
    def _():
        wait(xs.at[pl.ds(0, groups - 1)], ret_s)

    @pl.when(away)
    def _():
        wait(xs, ret_s)

    wait(abuf.at[:, c], ex_s.at[0])
    wait(dfb.at[:, c], ex_s.at[1])
    wait(sb2, ex_s.at[5])
    wait(bbuf.at[:, c], ex_s.at[6])
    wait(sb1, ex_s.at[7])


def rotary_tables(count):
    lanes = np.arange(128) % 32
    frequency = np.where(lanes < HD // 2, BASE ** (-2.0 * lanes / HD), 0.0)
    high = np.zeros((32, 128))
    high[:count] = 32.0 * np.arange(count)[:, None] * frequency[None, :]
    low = np.arange(32)[:, None] * frequency[None, :]
    return np.stack([np.cos(high), np.sin(high), np.cos(low), np.sin(low)]).astype(np.float32)


def fused_body(
    x_given, dealing, seq_lengths, first_gain, query_weight, key_weight, value_weight,
    output_weight, second_gain, gate_weight, up_weight, down_weight, grad_output,
):
    groups, piece_rows, dim = x_given.shape
    hw = query_weight.shape[1]
    local_hidden = gate_weight.shape[1]
    chunk = 256
    nf = local_hidden // chunk
    nz = groups // 4
    rows = query_weight.shape[0]
    pw = hw // HD * 64
    seq_len = groups * 64
    vm, anym, sm = (
        pl.BlockSpec(memory_space=pltpu.VMEM),
        pl.BlockSpec(memory_space=pl.ANY),
        pl.BlockSpec(memory_space=pltpu.SMEM),
    )
    blocks = (groups, piece_rows, dim)
    pairs = (groups, 2, piece_rows)

    def gathered(width, lead=()):
        return pltpu.VMEM(lead + (nz, 2, 2, rows, width), BF)

    kd = nz // 2

    def landing(width, lead=()):
        return [
            pltpu.VMEM(lead + (nz, 2, rows, width), BF),
            pltpu.VMEM(lead + (kd, 2, 2, rows, width), BF),
            pltpu.VMEM(lead + (nz - kd, 2, rows, width), BF),
            pltpu.VMEM(lead + (nz, rows, width), BF),
        ]

    units = nf + 2
    dma = pltpu.SemaphoreType.DMA
    scratch = (
        [pltpu.VMEM(blocks, BF)] * 3
        + [pltpu.VMEM((rows, 3 * hw), BF), pltpu.VMEM((nf, rows, 3 * chunk), BF)]
        + [gathered(3 * hw), gathered(hw), gathered(3 * chunk, (nf,))]
        + [pltpu.VMEM((dim, 3 * pw), BF), pltpu.VMEM((dim, pw), BF)]
        + [pltpu.VMEM((hw, pw), BF)] * 2
        + [pltpu.VMEM((seq_len, 128), F32)] * 2
        + [pltpu.VMEM((32, seq_len), F32)] * 2
        + [pltpu.VMEM(pairs + (dim,), BF)]
        + [pltpu.VMEM(pairs + (pw,), BF)] * 3
        + [pltpu.VMEM((pw, seq_len), BF)] * 2
        + [pltpu.VMEM(pairs + (pw,), BF)]
        + [pltpu.VMEM((8, seq_len), F32)]
        + [pltpu.VMEM(blocks, F32)]
        + [pltpu.VMEM(blocks, BF)] * 4
        + [pltpu.VMEM(blocks, F32)]
        + [pltpu.VMEM((groups, piece_rows, 128), F32)] * 2
        + [pltpu.VMEM(pairs + (dim,), BF)] * 2
        + [pltpu.VMEM(pairs + (dim,), F32)] * 2
        + [pltpu.VMEM((seq_len, 3 * chunk), BF)]
        + [pltpu.VMEM(pairs + (pw,), BF)]
        + [pltpu.VMEM((16, seq_len), F32)]
        + landing(3 * hw)
        + landing(hw)
        + landing(3 * chunk, (nf,))
        + [pltpu.VMEM(blocks, BF)]
        + [pltpu.VMEM((rows, 128), F32)] * 3
        + [dma(())] * 4
        + [dma((units,)), dma((units,)), dma((units,)), dma((units, 2)), dma((units, nz + 3))]
        + [dma((units, 2)), dma((units, 2)), dma((units,)), dma((units, 2 * nz + 2))]
        + [dma((8,)), dma((8,))]
        + [dma(())] * 6
    )
    small = jax.ShapeDtypeStruct((rows, hw), F32)
    wide = jax.ShapeDtypeStruct((rows, local_hidden), F32)
    piece = jax.ShapeDtypeStruct(blocks, BF)
    outs = pl.pallas_call(
        functools.partial(fused_kernel, (nz, nf, dim, hw, chunk, rows)),
        out_shape=[piece, piece, small, small, small, small, wide, wide, wide]
        + [jax.ShapeDtypeStruct((rows, 128), F32)],
        in_specs=[sm, sm, vm, anym] + [vm] * 10,
        out_specs=[anym] + [vm] * 9,
        scratch_shapes=scratch,
        compiler_params=pltpu.CompilerParams(
            collective_id=0, has_side_effects=True, vmem_limit_bytes=VMEM_LIMIT
        ),
        name="layer",
    )(
        dealing, seq_lengths, x_given, grad_output.reshape(blocks),
        first_gain.astype(F32).reshape(rows, 1), second_gain.astype(F32).reshape(rows, 1),
        query_weight, key_weight, value_weight, output_weight, gate_weight, up_weight, down_weight,
        rotary_tables(seq_len // 32),
    )
    layer_out, grad_in, gq, gk, gv, go, gg, gu, gd, gains = outs
    return (
        layer_out.reshape(grad_output.shape), grad_in, gains[:, 0], gq, gk, gv, go,
        gains[:, 64], gg, gu, gd,
    )


def fits_fused(mesh):
    return mesh.shape["tensor"] == 2 and mesh.shape["dp"] % 8 == 0


def solution(mesh):
    placed = (
        P(None, ("dp", "tensor"), None),
        P(),
        P(),
        P("dp"),
        P("dp", "tensor"),
        P("dp", "tensor"),
        P("dp", "tensor"),
        P("dp", "tensor"),
        P("dp"),
        P("dp", "tensor"),
        P("dp", "tensor"),
        P("dp", "tensor"),
        P("dp", None, "tensor", None, None),
    )
    return jax.shard_map(
        fused_body if fits_fused(mesh) else body,
        mesh=mesh,
        in_specs=placed,
        out_specs=(
            P("dp", None, "tensor", None, None),
            P(None, ("dp", "tensor"), None),
            P("dp"),
            P("dp", "tensor"),
            P("dp", "tensor"),
            P("dp", "tensor"),
            P("dp", "tensor"),
            P("dp"),
            P("dp", "tensor"),
            P("dp", "tensor"),
            P("dp", "tensor"),
        ),
        check_vma=False,
    )
```

```python
import functools

import jax
import jax.numpy as jnp
import numpy as np
from jax import lax
from jax.experimental import pallas as pl
from jax.experimental.pallas import tpu as pltpu
from jax.sharding import PartitionSpec as P

HD = 48


EPS = 1e-05
BASE = 10000.0
VMEM_LIMIT = 64 * 1024 * 1024 - 65536


def tables(positions, head_size):
    freq_index = jnp.arange(head_size // 2, dtype=jnp.float32)
    frequency = BASE ** (-2.0 * freq_index / head_size)
    angles = positions[:, None] * frequency[None, :]
    return (jnp.cos(angles)[:, None, :], jnp.sin(angles)[:, None, :])


def rotary(values, cosine, sine_table):
    half_width = values.shape[-1] // 2
    first_half = values[..., :half_width]
    second_half = values[..., half_width:]
    return jnp.concatenate(
        [
            first_half * cosine - second_half * sine_table,
            second_half * cosine + first_half * sine_table,
        ],
        axis=-1,
    )


def rotary_back(values, cosine, sine_table):
    half_width = values.shape[-1] // 2
    first_half = values[..., :half_width]
    second_half = values[..., half_width:]
    return jnp.concatenate(
        [
            first_half * cosine + second_half * sine_table,
            second_half * cosine - first_half * sine_table,
        ],
        axis=-1,
    )


def row_dot(left_side, right_side):
    return jnp.dot(left_side, right_side, preferred_element_type=jnp.float32)


def dot_trans(left_side, right_side):
    return lax.dot_general(
        left_side, right_side, (((1,), (1,)), ((), ())), preferred_element_type=jnp.float32
    )


def dot_first(left_side, right_side):
    return lax.dot_general(
        left_side, right_side, (((0,), (0,)), ((), ())), preferred_element_type=jnp.float32
    )


def tensor_major(values, groups, pieces, piece_rows):
    columns = values.shape[1]
    return (
        values.reshape(groups, pieces, piece_rows, columns)
        .transpose(1, 0, 2, 3)
        .reshape(groups * pieces * piece_rows, columns)
    )


def rms_back(grad_normed, x_rows, scale_rows, gain):
    normed = x_rows * scale_rows
    weighted = grad_normed * gain
    x_grad = scale_rows * (weighted - normed * jnp.mean(weighted * normed, axis=-1, keepdims=True))
    return (x_grad, jnp.sum(grad_normed * normed, axis=0))


def block_scores(queries, key_rows, query_start, key_start, block_rows, score_scale):
    query_part = lax.dynamic_slice_in_dim(queries, query_start, block_rows, 0)
    key_part = lax.dynamic_slice_in_dim(key_rows, key_start, block_rows, 0)
    scores = (
        jnp.einsum("qhd,khd->hqk", query_part, key_part, preferred_element_type=jnp.float32)
        * score_scale
    )
    row_offsets = jnp.arange(block_rows)
    allowed = (key_start + row_offsets)[None, :] <= (query_start + row_offsets)[:, None]
    return jnp.where(allowed[None], scores, -1e30)


def attend_forward(queries, key_rows, value_rows, live_blocks, block_rows, score_scale):
    seq_len, heads, head_size = queries.shape

    def one_block(query_index, state_now):
        outputs, log_sums = state_now
        query_start = query_index * block_rows

        def stats(key_index, carried):
            running, exp_total = carried
            scores = block_scores(
                queries, key_rows, query_start, key_index * block_rows, block_rows, score_scale
            )
            newest = jnp.maximum(running, jnp.max(scores, axis=-1))
            exp_total = exp_total * jnp.exp(running - newest) + jnp.sum(
                jnp.exp(scores - newest[..., None]), axis=-1
            )
            return (newest, exp_total)

        initial = (
            jnp.full((heads, block_rows), -1e30, jnp.float32),
            jnp.zeros((heads, block_rows), jnp.float32),
        )
        running, exp_total = lax.fori_loop(0, query_index + 1, stats, initial)
        log_sum = running + jnp.log(exp_total)

        def accumulate(key_index, accumulated):
            key_start = key_index * block_rows
            scores = block_scores(
                queries, key_rows, query_start, key_start, block_rows, score_scale
            )
            prob_low = jnp.exp(scores - log_sum[..., None]).astype(jnp.bfloat16)
            value_part = lax.dynamic_slice_in_dim(value_rows, key_start, block_rows, 0)
            return accumulated + jnp.einsum(
                "hqk,khd->qhd", prob_low, value_part, preferred_element_type=jnp.float32
            )

        result = lax.fori_loop(
            0, query_index + 1, accumulate, jnp.zeros((block_rows, heads, head_size), jnp.float32)
        )
        outputs = lax.dynamic_update_slice_in_dim(outputs, result, query_start, 0)
        log_sums = lax.dynamic_update_slice_in_dim(log_sums, log_sum, query_start, 1)
        return (outputs, log_sums)

    initial = (
        jnp.zeros((seq_len, heads, head_size), jnp.float32),
        jnp.zeros((heads, seq_len), jnp.float32),
    )
    return lax.fori_loop(0, live_blocks, one_block, initial)


def attend_backward(
    queries, key_rows, value_rows, outputs, log_sums, out_grad, live_blocks, block_rows, score_scale
):
    seq_len, heads, head_size = queries.shape
    row_delta = jnp.einsum("qhd,qhd->hq", out_grad.astype(jnp.float32), outputs)

    def one_block(query_index, state_now):
        query_grads, key_grads, value_grads = state_now
        query_start = query_index * block_rows
        query_part = lax.dynamic_slice_in_dim(queries, query_start, block_rows, 0)
        grad_part = lax.dynamic_slice_in_dim(out_grad, query_start, block_rows, 0)
        logsum_part = lax.dynamic_slice_in_dim(log_sums, query_start, block_rows, 1)
        delta_part = lax.dynamic_slice_in_dim(row_delta, query_start, block_rows, 1)

        def inner(key_index, carried):
            query_acc, key_grads, value_grads = carried
            key_start = key_index * block_rows
            key_part = lax.dynamic_slice_in_dim(key_rows, key_start, block_rows, 0)
            value_part = lax.dynamic_slice_in_dim(value_rows, key_start, block_rows, 0)
            scores = block_scores(
                queries, key_rows, query_start, key_start, block_rows, score_scale
            )
            prob_soft = jnp.exp(scores - logsum_part[..., None])
            prob_low = prob_soft.astype(jnp.bfloat16)
            prob_grad = jnp.einsum(
                "qhd,khd->hqk", grad_part, value_part, preferred_element_type=jnp.float32
            )
            score_grad = (prob_soft * (prob_grad - delta_part[..., None])).astype(jnp.bfloat16)
            query_acc = (
                query_acc
                + jnp.einsum(
                    "hqk,khd->qhd", score_grad, key_part, preferred_element_type=jnp.float32
                )
                * score_scale
            )
            key_new = (
                jnp.einsum(
                    "hqk,qhd->khd", score_grad, query_part, preferred_element_type=jnp.float32
                )
                * score_scale
            )
            value_new = jnp.einsum(
                "hqk,qhd->khd", prob_low, grad_part, preferred_element_type=jnp.float32
            )
            key_old = lax.dynamic_slice_in_dim(key_grads, key_start, block_rows, 0)
            value_old = lax.dynamic_slice_in_dim(value_grads, key_start, block_rows, 0)
            key_grads = lax.dynamic_update_slice_in_dim(key_grads, key_old + key_new, key_start, 0)
            value_grads = lax.dynamic_update_slice_in_dim(
                value_grads, value_old + value_new, key_start, 0
            )
            return (query_acc, key_grads, value_grads)

        initial = (jnp.zeros((block_rows, heads, head_size), jnp.float32), key_grads, value_grads)
        query_acc, key_grads, value_grads = lax.fori_loop(0, query_index + 1, inner, initial)
        query_grads = lax.dynamic_update_slice_in_dim(query_grads, query_acc, query_start, 0)
        return (query_grads, key_grads, value_grads)

    zero_grads = jnp.zeros((seq_len, heads, head_size), jnp.float32)
    return lax.fori_loop(0, live_blocks, one_block, (zero_grads, zero_grads, zero_grads))


def body(
    x_given,
    dealing,
    seq_lengths,
    first_gain,
    query_weight,
    key_weight,
    value_weight,
    output_weight,
    second_gain,
    gate_weight,
    up_weight,
    down_weight,
    grad_output,
):
    groups = lax.axis_size("dp")
    pieces = lax.axis_size("tensor")
    group_index = lax.axis_index("dp")
    piece_index = lax.axis_index("tensor")
    seq_count, piece_rows, features = x_given.shape
    tokens = groups * piece_rows
    seq_len = tokens * pieces
    head_width = query_weight.shape[1]
    heads_local = head_width // HD
    block_rows = min(512, seq_len)
    score_scale = HD ** (-0.5)
    sequence = dealing[group_index]
    length = seq_lengths[sequence]
    live_blocks = (length + block_rows - 1) // block_rows
    outgoing = jnp.take(x_given, dealing, axis=0)
    arrived = lax.all_to_all(outgoing, "dp", split_axis=0, concat_axis=1, tiled=True)
    x_rows = arrived.reshape(tokens, features).astype(jnp.float32)
    row_ids = jnp.arange(tokens)
    positions_local = (
        row_ids // piece_rows * pieces + piece_index
    ) * piece_rows + row_ids % piece_rows
    live_rows = (positions_local < length).astype(jnp.float32)[:, None]
    columns = (
        lax.all_gather(gate_weight, "tensor", axis=1, tiled=True),
        lax.all_gather(up_weight, "tensor", axis=1, tiled=True),
        lax.all_gather(down_weight, "tensor", axis=1, tiled=True),
    )
    gathered = (
        lax.all_gather(first_gain, "dp", axis=0, tiled=True),
        lax.all_gather(second_gain, "dp", axis=0, tiled=True),
        lax.all_gather(query_weight, "dp", axis=0, tiled=True),
        lax.all_gather(key_weight, "dp", axis=0, tiled=True),
        lax.all_gather(value_weight, "dp", axis=0, tiled=True),
        lax.all_gather(output_weight, "dp", axis=0, tiled=True),
        lax.all_gather(columns[0], "dp", axis=0, tiled=True),
        lax.all_gather(columns[1], "dp", axis=0, tiled=True),
        lax.all_gather(columns[2], "dp", axis=0, tiled=True),
    )
    (
        gain_one,
        gain_two,
        query_full,
        key_full,
        value_full,
        out_full,
        gate_full,
        up_full,
        down_full,
    ) = gathered
    qkv_weight = jnp.concatenate([query_full, key_full, value_full], axis=1)
    scale_one = lax.rsqrt(jnp.mean(x_rows * x_rows, axis=-1, keepdims=True) + EPS)
    normed = (x_rows * scale_one * gain_one).astype(jnp.bfloat16)
    normed_full = lax.all_gather(
        normed.reshape(groups, 1, piece_rows, features), "tensor", axis=1, tiled=True
    ).reshape(seq_len, features)
    projected = row_dot(normed_full, qkv_weight)
    cosine, sine_table = tables(jnp.arange(seq_len, dtype=jnp.float32), HD)
    queries = rotary(
        projected[:, :head_width].reshape(seq_len, heads_local, HD), cosine, sine_table
    ).astype(jnp.bfloat16)
    key_rows = rotary(
        projected[:, head_width : 2 * head_width].reshape(seq_len, heads_local, HD),
        cosine,
        sine_table,
    ).astype(jnp.bfloat16)
    value_rows = (
        projected[:, 2 * head_width :].astype(jnp.bfloat16).reshape(seq_len, heads_local, HD)
    )
    mixed, log_sums = attend_forward(
        queries, key_rows, value_rows, live_blocks, block_rows, score_scale
    )
    mixed_low = mixed.reshape(seq_len, head_width).astype(jnp.bfloat16)
    mixed_major = tensor_major(mixed_low, groups, pieces, piece_rows)
    attention = lax.psum_scatter(
        dot_trans(mixed_major, out_full).astype(jnp.bfloat16),
        "tensor",
        scatter_dimension=0,
        tiled=True,
    ).astype(jnp.float32)
    hidden_one = x_rows + live_rows * attention
    scale_two = lax.rsqrt(jnp.mean(hidden_one * hidden_one, axis=-1, keepdims=True) + EPS)
    normed_two = (hidden_one * scale_two * gain_two).astype(jnp.bfloat16)
    gate_act = row_dot(normed_two, gate_full)
    up_act = row_dot(normed_two, up_full)
    sigmoid_act = jax.nn.sigmoid(gate_act)
    silu_act = gate_act * sigmoid_act
    hidden = (silu_act * up_act).astype(jnp.bfloat16)
    branch = dot_trans(hidden, down_full)
    result = hidden_one + live_rows * branch
    layer_out = result.astype(jnp.bfloat16).reshape(1, groups, 1, piece_rows, features)
    out_grad = grad_output.reshape(tokens, features).astype(jnp.float32)
    branch_grad = (live_rows * out_grad).astype(jnp.bfloat16)
    hidden_grad = row_dot(branch_grad, down_full)
    down_term = dot_first(branch_grad, hidden)
    gate_grad = (
        hidden_grad * up_act * sigmoid_act * (1.0 + gate_act * (1.0 - sigmoid_act))
    ).astype(jnp.bfloat16)
    up_grad = (hidden_grad * silu_act).astype(jnp.bfloat16)
    normed_two_grad = dot_trans(gate_grad, gate_full) + dot_trans(up_grad, up_full)
    gate_term = dot_first(normed_two, gate_grad)
    up_term = dot_first(normed_two, up_grad)
    hidden_one_grad, gain_two_term = rms_back(normed_two_grad, hidden_one, scale_two, gain_two)
    hidden_one_grad = hidden_one_grad + out_grad
    attention_grad = (live_rows * hidden_one_grad).astype(jnp.bfloat16)
    attention_full = lax.all_gather(
        attention_grad.reshape(groups, 1, piece_rows, features), "tensor", axis=1, tiled=True
    ).reshape(seq_len, features)
    mixed_grad = row_dot(attention_full, out_full).astype(jnp.bfloat16)
    out_term = dot_first(attention_full, mixed_low)
    query_grads, key_grads, value_grads = attend_backward(
        queries,
        key_rows,
        value_rows,
        mixed,
        log_sums,
        mixed_grad.reshape(seq_len, heads_local, HD),
        live_blocks,
        block_rows,
        score_scale,
    )
    query_back = (
        rotary_back(query_grads, cosine, sine_table)
        .reshape(seq_len, head_width)
        .astype(jnp.bfloat16)
    )
    key_back = (
        rotary_back(key_grads, cosine, sine_table).reshape(seq_len, head_width).astype(jnp.bfloat16)
    )
    value_back = value_grads.reshape(seq_len, head_width).astype(jnp.bfloat16)
    projected_grad = jnp.concatenate([query_back, key_back, value_back], axis=1)
    qkv_term = dot_first(normed_full, projected_grad)
    grad_major = tensor_major(projected_grad, groups, pieces, piece_rows)
    normed_grad = lax.psum_scatter(
        dot_trans(grad_major, qkv_weight).astype(jnp.bfloat16),
        "tensor",
        scatter_dimension=0,
        tiled=True,
    ).astype(jnp.float32)
    input_grad, gain_one_term = rms_back(normed_grad, x_rows, scale_one, gain_one)
    input_grad = input_grad + hidden_one_grad
    returned = lax.all_to_all(
        input_grad.astype(jnp.bfloat16).reshape(groups, piece_rows, features),
        "dp",
        split_axis=0,
        concat_axis=0,
        tiled=True,
    )
    grad_in = jnp.zeros_like(x_given).at[dealing].set(returned)
    gain_pair = jnp.stack([gain_one_term, gain_two_term], axis=1)
    query_term = qkv_term[:, :head_width]
    key_term = qkv_term[:, head_width : 2 * head_width]
    value_term = qkv_term[:, 2 * head_width :]
    summed = (
        lax.psum_scatter(
            gain_pair.astype(jnp.bfloat16), "dp", scatter_dimension=0, tiled=True
        ).astype(jnp.float32),
        lax.psum_scatter(
            query_term.astype(jnp.bfloat16), "dp", scatter_dimension=0, tiled=True
        ).astype(jnp.float32),
        lax.psum_scatter(
            key_term.astype(jnp.bfloat16), "dp", scatter_dimension=0, tiled=True
        ).astype(jnp.float32),
        lax.psum_scatter(
            value_term.astype(jnp.bfloat16), "dp", scatter_dimension=0, tiled=True
        ).astype(jnp.float32),
        lax.psum_scatter(
            out_term.astype(jnp.bfloat16), "dp", scatter_dimension=0, tiled=True
        ).astype(jnp.float32),
        lax.psum_scatter(
            gate_term.astype(jnp.bfloat16), "dp", scatter_dimension=0, tiled=True
        ).astype(jnp.float32),
        lax.psum_scatter(
            up_term.astype(jnp.bfloat16), "dp", scatter_dimension=0, tiled=True
        ).astype(jnp.float32),
        lax.psum_scatter(
            down_term.astype(jnp.bfloat16), "dp", scatter_dimension=0, tiled=True
        ).astype(jnp.float32),
    )
    across = (
        lax.psum_scatter(
            jnp.tile(summed[0], (1, pieces)).astype(jnp.bfloat16),
            "tensor",
            scatter_dimension=1,
            tiled=True,
        ).astype(jnp.float32),
        lax.psum_scatter(
            summed[5].astype(jnp.bfloat16), "tensor", scatter_dimension=1, tiled=True
        ).astype(jnp.float32),
        lax.psum_scatter(
            summed[6].astype(jnp.bfloat16), "tensor", scatter_dimension=1, tiled=True
        ).astype(jnp.float32),
        lax.psum_scatter(
            summed[7].astype(jnp.bfloat16), "tensor", scatter_dimension=1, tiled=True
        ).astype(jnp.float32),
    )
    gain_sums = across[0]
    query_sum, key_sum, value_sum, out_sum = (summed[1], summed[2], summed[3], summed[4])
    gate_sum, up_sum, down_sum = (across[1], across[2], across[3])
    return (
        layer_out,
        grad_in,
        gain_sums[:, 0],
        query_sum,
        key_sum,
        value_sum,
        out_sum,
        gain_sums[:, 1],
        gate_sum,
        up_sum,
        down_sum,
    )


MESH = pl.DeviceIdType.MESH
BF = jnp.bfloat16
F32 = jnp.float32
NN = (((1,), (0,)), ((), ()))
NT = (((1,), (1,)), ((), ()))
TN = (((0,), (0,)), ((), ()))
LOG2E = 1.4426950408889634
ROWS = 256


def mm(kind, left_side, right_side):
    return lax.dot_general(left_side, right_side, kind, preferred_element_type=F32)


def fused_kernel(
    shape,
    deal, lens, x_ref, dy_ref, g1, g2, wq, wk, wv, wo, wg, wu, wd, tab,
    lo_ref, gi_ref, dq_out, dk_out, dv_out, do_out, dg_out, du_out, dd_out, dg1_out, dg2_out,
    xs, xbuf, dybuf, src_a, src_f, w_a, w_o, w_f, wp, wop, eqk, ev, cosb, sinb, ct, st,
    abuf, qb, kb, vb, vt, ot, ob, lse, own, sb1, sb2, rb1, rb2, x1b, r1b, r2b, bbuf, dfb,
    facc, uacc, act, dob, delta, rx_a, ry_a, ry2_a, rz_a, rx_o, ry_o, ry2_o, rz_o,
    rx_f, ry_f, ry2_f, rz_f, ret, gs, gr, rsum,
    a2a_s, a2a_r, dy_s, dy_r, ag_z, ag_x, ag_y, ag_d, ag_s, rs_x, rs_y, rs_z, rs_s,
    ex_s, ex_r, lo_s, lo_r, ret_s, ret_r, gg_s, gg_r,
):
    nz, nf, dim, hw, chunk, nrow = shape
    groups = 4 * nz
    seq_len = 64 * groups
    half = dim // 2
    nrb = seq_len // ROWS
    kd = nz // 2
    kg = nz // 2
    dp = lax.axis_index("dp")
    y = lax.axis_index("tensor")
    z = dp // 4
    x = (dp // 2) % 2
    c = dp % 2
    xb, yb, oth = 1 - x, 1 - y, 1 - c
    home = c == y
    away = c != y
    slot = (z * 2 + x) * 2 + y
    score_scale = HD ** (-0.5)

    def dev(z_, x_, c_, y_):
        return ((z_ * 2 + x_) * 2 + c_, y_)

    partner = dev(z, x, oth, y)
    xnbr = dev(z, xb, c, y)
    ynbr = dev(z, x, c, yb)
    swap = dev(z, x, oth, yb)

    def rc(src, dst, ss, rs, to):
        return pltpu.make_async_remote_copy(
            src_ref=src, dst_ref=dst, send_sem=ss, recv_sem=rs, device_id=to, device_id_type=MESH
        )

    def wait(ref, sem):
        pltpu.make_async_copy(ref, ref, sem).wait()

    bar = pltpu.get_barrier_semaphore()
    ndev = groups * 2

    def greet(i, _):
        t = lax.rem(dp * 2 + y + i, ndev)
        pl.semaphore_signal(bar, inc=1, device_id=(t // 2, t % 2), device_id_type=MESH)
        return 0

    lax.fori_loop(1, ndev, greet, 0)
    pl.semaphore_wait(bar, ndev - 1)

    def unit(k):
        if isinstance(k, str):
            return (src_a, w_a, 0) if k == "a" else (wo, w_o, 1)
        return (src_f.at[k], w_f.at[k], k + 2)

    def zsend(k):
        src, buf, n = unit(k)
        for i in range(1, nz):
            zt = lax.rem(z + i, nz)
            rc(src, buf.at[z, x, c], ag_s.at[n, i - 1], ag_z.at[n], dev(zt, x, y, y)).start()

        @pl.when(home)
        def _():
            pltpu.make_async_copy(src, buf.at[z, x, c], ag_z.at[n]).start()

        @pl.when(away)
        def _():
            rc(src, buf.at[z, x, c], ag_s.at[n, nz - 1], ag_z.at[n], dev(z, x, y, y)).start()

    def ag1(k):
        src, buf, n = unit(k)

        @pl.when(home)
        def _():
            wait(buf.at[:, x], ag_z.at[n])
            rc(buf.at[:, x], buf.at[:, x], ag_s.at[n, nz], ag_y.at[n], ynbr).start()
            rc(buf.at[:, x], buf.at[:, x], ag_s.at[n, nz + 1], ag_x.at[n], xnbr).start()

    def ag2(k):
        src, buf, n = unit(k)

        @pl.when(home)
        def _():
            wait(buf.at[:, xb], ag_x.at[n])
            part = buf.at[pl.ds(0, kg), xb]
            rc(part, part, ag_s.at[n, nz + 2], ag_d.at[n, 0], ynbr).start()

        @pl.when(away)
        def _():
            wait(buf.at[:, x], ag_y.at[n])
            part = buf.at[pl.ds(kg, nz - kg), x]
            rc(part, part, ag_s.at[n, nz + 2], ag_d.at[n, 1], xnbr).start()

    def ag3(k):
        src, buf, n = unit(k)

        @pl.when(away)
        def _():
            wait(buf.at[pl.ds(0, kg), xb], ag_d.at[n, 0])
            wait(buf.at[pl.ds(kg, nz - kg), xb], ag_d.at[n, 1])

    def ag_done(k):
        src, buf, n = unit(k)
        for i in range(nz - 1):
            wait(src, ag_s.at[n, i])

        @pl.when(home)
        def _():
            wait(buf.at[:, x], ag_s.at[n, nz])
            wait(buf.at[:, x], ag_s.at[n, nz + 1])
            wait(buf.at[pl.ds(0, kg), xb], ag_s.at[n, nz + 2])

        @pl.when(away)
        def _():
            wait(src, ag_s.at[n, nz - 1])
            wait(buf.at[pl.ds(kg, nz - kg), x], ag_s.at[n, nz + 2])

    def rs_unit(k):
        if isinstance(k, str):
            if k == "a":
                return (w_a, rx_a, ry_a, ry2_a, rz_a, 0)
            return (w_o, rx_o, ry_o, ry2_o, rz_o, 1)
        return (w_f.at[k], rx_f.at[k], ry_f.at[k], ry2_f.at[k], rz_f.at[k], k + 2)

    lo_z = pl.ds(0, kd)
    hi_z = pl.ds(kd, nz - kd)

    def at_unit(ref, k, *spot):
        spot = spot if isinstance(k, str) else (k,) + spot
        return ref[spot if spot else ...].astype(F32)

    def put_unit(ref, k, total, *spot):
        spot = spot if isinstance(k, str) else (k,) + spot
        ref[spot if spot else ...] = total.astype(BF)

    def rs_refs(k):
        if isinstance(k, str):
            return (w_a, rx_a, ry_a, ry2_a) if k == "a" else (w_o, rx_o, ry_o, ry2_o)
        return w_f, rx_f, ry_f, ry2_f

    every = slice(None)

    def by_x(step):
        for v in range(2):
            pl.when(x == v)(functools.partial(step, v, 1 - v))

    def rs0(k):
        g, rx, ry, ry2, rz, n = rs_unit(k)
        rc(g.at[hi_z, xb], rx.at[hi_z], rs_s.at[n, 0], rs_x.at[n, 1], xnbr).start()

        @pl.when(away)
        def _():
            rc(g.at[lo_z], ry, rs_s.at[n, 1], rs_y.at[n, 0], ynbr).start()

    def rs1(k):
        g, rx, ry, ry2, rz, n = rs_unit(k)
        g_all, rx_all, ry_all, ry2_all = rs_refs(k)

        @pl.when(away)
        def _():
            wait(rx.at[hi_z], rs_x.at[n, 1])

            @by_x
            def _(v, vb):
                put_unit(ry2_all, k, at_unit(g_all, k, hi_z, v) + at_unit(rx_all, k, hi_z))

            rc(ry2, ry2, rs_s.at[n, 2], rs_y.at[n, 1], ynbr).start()

        @pl.when(home)
        def _():
            wait(ry, rs_y.at[n, 0])

            @by_x
            def _(v, vb):
                total = at_unit(g_all, k, lo_z, vb) + at_unit(ry_all, k, every, vb)
                put_unit(ry_all, k, total, every, vb)

            rc(ry.at[:, xb], rx.at[lo_z], rs_s.at[n, 2], rs_x.at[n, 0], xnbr).start()

    def rs2(k):
        g, rx, ry, ry2, rz, n = rs_unit(k)
        g_all, rx_all, ry_all, ry2_all = rs_refs(k)

        @pl.when(home)
        def _():
            wait(rx.at[hi_z], rs_x.at[n, 1])
            wait(ry2, rs_y.at[n, 1])

            @by_x
            def _(v, vb):
                total = at_unit(g_all, k, hi_z, v) + at_unit(rx_all, k, hi_z) + at_unit(ry2_all, k)
                put_unit(rx_all, k, total, hi_z)

            wait(rx.at[lo_z], rs_x.at[n, 0])

            @by_x
            def _(v, vb):
                total = at_unit(g_all, k, lo_z, v) + at_unit(ry_all, k, every, v)
                put_unit(rx_all, k, total + at_unit(rx_all, k, lo_z), lo_z)

            for i in range(1, nz):
                zt = lax.rem(z + i, nz)
                for cc in range(2):
                    rc(
                        rx.at[zt, cc], rz.at[z], rs_s.at[n, 3 + 2 * (i - 1) + cc], rs_z.at[n],
                        dev(zt, x, cc, y),
                    ).start()
            rc(rx.at[z, oth], rz.at[z], rs_s.at[n, 2 * nz + 1], rs_z.at[n], partner).start()
            pltpu.make_async_copy(rx.at[z, c], rz.at[z], rs_z.at[n]).start()

    def rs_done(k):
        g, rx, ry, ry2, rz, n = rs_unit(k)
        wait(rx.at[hi_z], rs_s.at[n, 0])

        @pl.when(away)
        def _():
            wait(ry, rs_s.at[n, 1])
            wait(ry2, rs_s.at[n, 2])

        @pl.when(home)
        def _():
            wait(rx.at[lo_z], rs_s.at[n, 2])
            for i in range(2 * (nz - 1) + 1):
                wait(rz.at[0], rs_s.at[n, 3 + i])

    def rs3(k):
        g, rx, ry, ry2, rz, n = rs_unit(k)
        wait(rz, rs_z.at[n])
        total = None
        for i in range(nz):
            part = (rz[i] if isinstance(k, str) else rz_f[k, i]).astype(F32)
            total = part if total is None else total + part
        return total

    square = (nrow, nrow)
    on_diag = lax.broadcasted_iota(jnp.int32, square, 0) == lax.broadcasted_iota(
        jnp.int32, square, 1
    )

    def column(ref):
        spread = jnp.where(on_diag, ref[...].astype(F32), 0.0)
        return jnp.sum(spread, axis=1, keepdims=True)

    gain1 = column(g1)
    gain2 = column(g2)
    for i, w in enumerate((wq, wk, wv)):
        src_a[:, i * hw : (i + 1) * hw] = (w[...].astype(F32) * gain1).astype(BF)
    zsend("a")

    def stage(j, _):
        xs[j] = x_ref[deal[j]]
        return 0

    lax.fori_loop(0, groups, stage, 0)

    def deal_out(i, _):
        j = lax.rem(slot + i, groups)
        dpd = (j // 2) * 2 + y
        td = j % 2
        same = (dpd == dp) & (td == y)

        @pl.when(same)
        def _():
            pltpu.make_async_copy(xs.at[j], xbuf.at[dp], a2a_r).start()

        @pl.when(jnp.logical_not(same))
        def _():
            rc(xs.at[j], xbuf.at[dp], a2a_s, a2a_r, (dpd, td)).start()

        return 0

    lax.fori_loop(0, groups, deal_out, 0)

    for f in range(nf):
        cols = slice(f * chunk, (f + 1) * chunk)
        src_f[f, :, 0:chunk] = (wg[:, cols].astype(F32) * gain2).astype(BF)
        src_f[f, :, chunk : 2 * chunk] = (wu[:, cols].astype(F32) * gain2).astype(BF)
        src_f[f, :, 2 * chunk : 3 * chunk] = wd[:, cols]

    def rope_rows(i, _):
        ca, sa = tab[0, pl.ds(i, 1), :], tab[1, pl.ds(i, 1), :]
        cb, sb = tab[2], tab[3]
        at = pl.ds(pl.multiple_of(i * 32, 32), 32)
        cosb[at, :] = ca * cb - sa * sb
        sinb[at, :] = sa * cb + ca * sb
        return 0

    lax.fori_loop(0, seq_len // 32, rope_rows, 0)
    for i in range(nrb):
        at = slice(i * ROWS, (i + 1) * ROWS)
        ct[:, at] = cosb[at, :].T[0:32]
        st[:, at] = sinb[at, :].T[0:32]
    pw = wop.shape[1]
    row = lax.broadcasted_iota(jnp.int32, (hw, pw), 0)
    col = lax.broadcasted_iota(jnp.int32, (hw, pw), 1)
    low = col & 31
    spot = ((col >> 8) * 4 + ((col >> 5) & 3)) * HD + ((col >> 7) & 1) * (HD // 2) + low
    eqk[...] = jnp.where((row == spot) & (low < HD // 2), 1.0, 0.0).astype(BF)
    low = col & 63
    ev[...] = jnp.where((row == (col >> 6) * HD + low) & (low < HD), 1.0, 0.0).astype(BF)

    length = lens[deal[slot]]

    def live_at(i):
        at = (i * 2 + c) * 32 + lax.broadcasted_iota(jnp.int32, (32, 1), 0)
        return at < length

    def mean(values):
        return jnp.mean(values, axis=1, keepdims=True)

    def swap_start(n, src, dst):
        rc(src, dst, ex_s.at[n], ex_r.at[n], partner).start()

    def blk(i):
        return pl.ds(i * (ROWS // 64), ROWS // 64)

    ag1("a")
    zsend("o")
    zsend(0)

    @pl.when(home)
    def _():
        pltpu.make_async_copy(dy_ref, dybuf, dy_r).start()

    @pl.when(away)
    def _():
        rc(dy_ref, dybuf, dy_s, dy_r, swap).start()

    ag2("a")
    wait(xbuf, a2a_r)

    def norm_one(i, _):
        rows_now = xbuf[i].astype(F32)
        r = lax.rsqrt(mean(rows_now * rows_now) + EPS)
        r1b[i] = jnp.broadcast_to(r, (32, 128))
        abuf[i, c] = (rows_now * r).astype(BF)
        return 0

    lax.fori_loop(0, groups, norm_one, 0, unroll=2)
    swap_start(0, abuf.at[:, c], abuf.at[:, c])
    ag1("o")
    zsend(1)
    ag3("a")
    for i in range(3):
        e = eqk if i < 2 else ev
        wp[:, i * pw : (i + 1) * pw] = mm(
            NN, w_a[:, :, :, :, i * hw : (i + 1) * hw].reshape(dim, hw), e[...]
        ).astype(BF)
    wait(abuf.at[:, oth], ex_r.at[0])

    query_scale = score_scale * LOG2E
    lane64 = lax.broadcasted_iota(jnp.int32, (ROWS, pw), 1) & 63

    def project(i, _):
        a = abuf[blk(i)].reshape(ROWS, dim)
        at = pl.ds(pl.multiple_of(i * ROWS, ROWS), ROWS)
        cos, sin = cosb[at, :], sinb[at, :]
        for t, (dst, scale) in enumerate(((qb, query_scale), (kb, 1.0))):
            u = mm(NN, a, wp[:, t * pw : (t + 1) * pw]) * scale
            for g in range(pw // 256):
                f1 = u[:, g * 256 : g * 256 + 128]
                f2 = u[:, g * 256 + 128 : g * 256 + 256]
                dst[blk(i), :, :, g * 256 : g * 256 + 128] = (
                    (f1 * cos - f2 * sin).astype(BF).reshape(ROWS // 64, 2, 32, 128)
                )
                dst[blk(i), :, :, g * 256 + 128 : g * 256 + 256] = (
                    (f2 * cos + f1 * sin).astype(BF).reshape(ROWS // 64, 2, 32, 128)
                )
        v = mm(NN, a, wp[:, 2 * pw : 3 * pw])
        v = jnp.where(lane64 == HD, 1.0, v).astype(BF)
        vb[blk(i)] = v.reshape(ROWS // 64, 2, 32, pw)
        vt[:, at] = v.T
        return 0

    lax.fori_loop(0, nrb, project, 0)
    ag1(0)
    ag2("o")
    zsend(2)

    lane = lax.broadcasted_iota(jnp.int32, (ROWS, 256), 1)
    diag = lax.broadcasted_iota(jnp.int32, (ROWS, ROWS), 0) <= lax.broadcasted_iota(
        jnp.int32, (ROWS, ROWS), 1
    )

    def rows_of(ref, first, count, lanes):
        return ref[pl.ds(first // 64, count // 64), :, :, lanes].reshape(count, 256)

    def attend(i):
        keys = (i + 1) * ROWS

        def group(g, _):
            lanes = pl.ds(pl.multiple_of(g * 256, 256), 256)
            q = rows_of(qb, i * ROWS, ROWS, lanes)
            for hh in range(4):
                qm = jnp.where(((lane >> 5) & 3) == hh, q, jnp.zeros_like(q))
                sd = mm(NT, rows_of(kb, i * ROWS, ROWS, lanes), qm)
                sd = jnp.where(diag, sd, -1e30)
                top = jnp.max(sd, axis=0, keepdims=True)
                if i:
                    s = mm(NT, rows_of(kb, 0, i * ROWS, lanes), qm)
                    top = jnp.maximum(top, jnp.max(s, axis=0, keepdims=True))
                    p = jnp.concatenate(
                        [jnp.exp2(s - top).astype(BF), jnp.exp2(sd - top).astype(BF)], axis=0
                    )
                else:
                    p = jnp.exp2(sd - top).astype(BF)
                hs = pl.multiple_of(g * 256 + hh * 64, 64)
                o = mm(NN, vt[pl.ds(hs, 64), 0:keys], p)
                total = o[HD : HD + 1, :]
                ot[pl.ds(hs, 64), i * ROWS : keys] = (o * (1.0 / total)).astype(BF)
                lse[pl.ds(g * 4 + hh, 1), i * ROWS : keys] = top + jnp.log2(total)
            return 0

        lax.fori_loop(0, pw // 256, group, 0)

    def during_zero():
        ag1(1)
        zsend(3)
        ag3("o")
        wop[...] = mm(NN, w_o[...].reshape(dim, hw), ev[...]).astype(BF)

    def during_one():
        ag2(0)
        ag1(2)
        zsend(4)

    def during_two():
        ag2(1)
        ag1(3)

    def mask_dy(i, _):
        dfb[i, c] = jnp.where(live_at(i), dybuf[i], jnp.zeros((32, dim), BF))
        return 0

    def with_steps(part, steps):
        for i in range(nrb):
            part(i)
            for at, step in steps:
                if min(at, nrb - 1) == i:
                    step()

    with_steps(attend, ((0, during_zero), (1, during_one), (2, during_two)))
    wait(dybuf, dy_r)
    lax.fori_loop(0, groups, mask_dy, 0, unroll=2)
    swap_start(1, dfb.at[:, c], dfb.at[:, c])

    def turn(i, _):
        at = pl.ds(pl.multiple_of(i * ROWS, ROWS), ROWS)
        ob[blk(i)] = ot[:, at].T.reshape(ROWS // 64, 2, 32, pw)
        return 0

    lax.fori_loop(0, nrb, turn, 0)

    half_rows = ROWS // 32

    def att_other(j, _):
        at = pl.ds(j * half_rows, half_rows)
        o = ob[at, oth].reshape(ROWS, pw)
        sb1[at] = mm(NT, o, wop[...]).astype(BF).reshape(half_rows, 32, dim)
        return 0

    def att_own(j, _):
        at = pl.ds(j * half_rows, half_rows)
        o = ob[at, c].reshape(ROWS, pw)
        own[at] = mm(NT, o, wop[...]).reshape(half_rows, 32, dim)
        return 0

    lax.fori_loop(0, groups // half_rows, att_other, 0)
    swap_start(2, sb1, rb1)
    lax.fori_loop(0, groups // half_rows, att_own, 0)
    ag1(4)
    wait(rb1, ex_r.at[2])

    def norm_two(i, _):
        att = own[i] + rb1[i].astype(F32)
        x1 = xbuf[i].astype(F32) + jnp.where(live_at(i), att, 0.0)
        x1b[i] = x1
        r = lax.rsqrt(mean(x1 * x1) + EPS)
        r2b[i] = jnp.broadcast_to(r, (32, 128))
        bbuf[i, c] = (x1 * r).astype(BF)
        return 0

    lax.fori_loop(0, groups, norm_two, 0, unroll=2)
    swap_start(3, bbuf.at[:, c], bbuf.at[:, c])
    wait(dfb.at[:, oth], ex_r.at[1])
    wait(bbuf.at[:, oth], ex_r.at[3])

    def ffn(f, _):
        ag3(f)

        def one(i, _):
            b = bbuf[blk(i)].reshape(ROWS, dim)
            d = dfb[blk(i)].reshape(ROWS, dim)
            w_gu = w_f[f, :, :, :, :, 0 : 2 * chunk].reshape(dim, 2 * chunk)
            w_d = w_f[f, :, :, :, :, 2 * chunk : 3 * chunk].reshape(dim, chunk)
            gu = mm(NN, b, w_gu)
            dh = mm(NN, d, w_d)
            gate, up = gu[:, 0:chunk], gu[:, chunk:]
            sg = jax.nn.sigmoid(gate)
            silu = gate * sg
            hid = (silu * up).astype(BF)
            dgate = (dh * up * sg * (1.0 + gate * (1.0 - sg))).astype(BF)
            dup = (dh * silu).astype(BF)
            at = pl.ds(pl.multiple_of(i * ROWS, ROWS), ROWS)
            act[at, 0:chunk] = dgate
            act[at, chunk : 2 * chunk] = dup
            act[at, 2 * chunk : 3 * chunk] = hid
            fpart = mm(NT, hid, w_d).reshape(ROWS // 64, 2, 32, dim)
            dgu = jnp.concatenate([dgate, dup], axis=1)
            upart = mm(NT, dgu, w_gu).reshape(ROWS // 64, 2, 32, dim)

            @pl.when(f == 0)
            def _():
                facc[blk(i)] = fpart
                uacc[blk(i)] = upart

            @pl.when(f > 0)
            def _():
                facc[blk(i)] += fpart
                uacc[blk(i)] += upart

            return 0

        lax.fori_loop(0, nrb, one, 0)
        ag_done(f)
        for m in range(2):
            feats = slice(m * half, (m + 1) * half)
            zs = slice(m * nz // 2, (m + 1) * nz // 2)
            left = bbuf[:, :, :, feats].reshape(seq_len, half)
            t = mm(TN, left, act[:, 0 : 2 * chunk]).astype(BF)
            w_f[f, zs, :, :, :, 0 : 2 * chunk] = t.reshape(nz // 2, 2, 2, nrow, 2 * chunk)
            left = dfb[:, :, :, feats].reshape(seq_len, half)
            t = mm(TN, left, act[:, 2 * chunk : 3 * chunk]).astype(BF)
            w_f[f, zs, :, :, :, 2 * chunk : 3 * chunk] = t.reshape(nz // 2, 2, 2, nrow, chunk)
        rs0(f)

        @pl.when(f + 2 < nf)
        def _():
            ag2(f + 2)

        @pl.when(f >= 1)
        def _():
            rs1(f - 1)

        @pl.when(f >= 2)
        def _():
            rs2(f - 2)

        return 0

    lax.fori_loop(0, nf, ffn, 0)

    wait(sb1, ex_s.at[2])

    def cast_u(i, _):
        sb1[i] = uacc[i, oth].astype(BF)
        return 0

    def cast_f(i, _):
        sb2[i] = facc[i, oth].astype(BF)
        return 0

    lax.fori_loop(0, groups, cast_u, 0)
    swap_start(4, sb1, rb1)
    lax.fori_loop(0, groups, cast_f, 0)
    swap_start(5, sb2, rb2)
    rs1(nf - 1)

    @pl.when(home)
    def _():
        wait(xs.at[pl.ds(0, groups - 1)], a2a_s)

    @pl.when(away)
    def _():
        wait(xs, a2a_s)

    wait(rb1, ex_r.at[4])
    wait(rb2, ex_r.at[5])
    wait(bbuf.at[:, c], ex_s.at[3])

    def norm_three(i, _):
        alive = live_at(i)
        x1 = x1b[i]
        r = r2b[i][:, 0:1]
        n = x1 * r
        u = uacc[i, c] + rb1[i].astype(F32)
        dx1 = dybuf[i].astype(F32) + r * (u - n * mean(u * n))
        bbuf[i, c] = jnp.where(alive, dx1, 0.0).astype(BF)
        ffn_out = facc[i, c] + rb2[i].astype(F32)
        xs[i] = (x1 + jnp.where(alive, ffn_out, 0.0)).astype(BF)
        x1b[i] = dx1
        return 0

    lax.fori_loop(0, groups, norm_three, 0, unroll=2)
    swap_start(6, bbuf.at[:, c], bbuf.at[:, c])

    @pl.when(home)
    def _():
        pltpu.make_async_copy(xs, lo_ref, lo_r).start()

    @pl.when(away)
    def _():
        rc(xs, lo_ref, lo_s, lo_r, swap).start()

    rs2(nf - 2)

    def turn_k(i, _):
        at = pl.ds(pl.multiple_of(i * ROWS, ROWS), ROWS)
        t = kb[blk(i)].reshape(ROWS, pw).T
        for h in range(pw // 64):
            for part in range(2):
                first = (h // 4) * 256 + part * 128 + (h % 4) * 32
                vt[h * 64 + part * 32 : h * 64 + part * 32 + 32, at] = t[first : first + 32]
        return 0

    lax.fori_loop(0, nrb, turn_k, 0)
    heads16 = lax.broadcasted_iota(jnp.int32, (16, pw), 0)
    pick = jnp.where(
        (lax.broadcasted_iota(jnp.int32, (16, pw), 1) >> 6) == heads16, 1.0, 0.0
    ).astype(BF)
    wait(bbuf.at[:, oth], ex_r.at[6])

    def out_back(i, _):
        at = pl.ds(pl.multiple_of(i * ROWS, ROWS), ROWS)
        t = mm(NN, bbuf[blk(i)].reshape(ROWS, dim), wop[...]).astype(BF)
        dob[blk(i)] = t.reshape(ROWS // 64, 2, 32, pw)
        prod = t.astype(F32) * ob[blk(i)].reshape(ROWS, pw).astype(F32)
        delta[:, at] = mm(NT, pick, prod.astype(BF))
        return 0

    lax.fori_loop(0, nrb, out_back, 0)
    ag_done("o")
    for m in range(2):
        left = bbuf[:, :, :, m * half : (m + 1) * half].reshape(seq_len, half)
        t = mm(TN, left, ob[...].reshape(seq_len, pw)).astype(BF)
        zs = slice(m * nz // 2, (m + 1) * nz // 2)
        w_o[zs] = mm(NT, t, ev[...]).astype(BF).reshape(nz // 2, 2, 2, nrow, hw)
    rs0("o")

    def attend_back(i):
        keys = (i + 1) * ROWS

        def group(g, _):
            lanes = pl.ds(pl.multiple_of(g * 256, 256), 256)
            q = rows_of(qb, i * ROWS, ROWS, lanes)
            d = rows_of(dob, i * ROWS, ROWS, lanes)
            for hh in range(4):
                qm = jnp.where(((lane >> 5) & 3) == hh, q, jnp.zeros_like(q))
                dm = jnp.where((lane >> 6) == hh, d, jnp.zeros_like(d))
                row_lse = lse[pl.ds(g * 4 + hh, 1), i * ROWS : keys]
                row_delta = delta[pl.ds(g * 4 + hh, 1), i * ROWS : keys]

                def part(first, count, masked):
                    s = mm(NT, rows_of(kb, first, count, lanes), qm)
                    if masked:
                        s = jnp.where(diag, s, -1e30)
                    p = jnp.exp2(s - row_lse)
                    dp_ = mm(NT, rows_of(vb, first, count, lanes), dm)
                    ds = (p * (dp_ - row_delta)).astype(BF)
                    at = pl.ds(first // 64, count // 64)
                    dv_part = mm(NN, p.astype(BF), dm).reshape(count // 64, 2, 32, 256)
                    dk_part = mm(NN, ds, qm).reshape(count // 64, 2, 32, 256)
                    if masked and hh == 0:
                        uacc[at, :, :, lanes] = dv_part
                        facc[at, :, :, lanes] = dk_part
                    else:
                        uacc[at, :, :, lanes] += dv_part
                        facc[at, :, :, lanes] += dk_part
                    return ds

                ds = part(i * ROWS, ROWS, True)
                if i:
                    ds = jnp.concatenate([part(0, i * ROWS, False), ds], axis=0)
                hs = pl.multiple_of(g * 256 + hh * 64, 64)
                t = mm(NN, vt[pl.ds(hs, 64), 0:keys], ds) * score_scale
                c_now, s_now = ct[:, i * ROWS : keys], st[:, i * ROWS : keys]
                f1, f2 = t[0:32], t[32:64]
                hs = pl.multiple_of(g * 256 + hh * 32, 32)
                ot[pl.ds(hs, 32), i * ROWS : keys] = (f1 * c_now + f2 * s_now).astype(BF)
                ot[pl.ds(hs + 128, 32), i * ROWS : keys] = (f2 * c_now - f1 * s_now).astype(BF)
            return 0

        lax.fori_loop(0, pw // 256, group, 0)

    with_steps(
        attend_back,
        ((0, lambda: rs2(nf - 1)), (1, lambda: rs1("o")), (2, lambda: rs2("o"))),
    )

    def turn_back(i, _):
        at = pl.ds(pl.multiple_of(i * ROWS, ROWS), ROWS)
        qb[blk(i)] = ot[:, at].T.reshape(ROWS // 64, 2, 32, pw)
        vb[blk(i)] = uacc[blk(i), :, :, 0:pw].astype(BF)
        cos, sin = cosb[at, :], sinb[at, :]
        for g in range(pw // 256):
            f1 = facc[blk(i), :, :, g * 256 : g * 256 + 128].reshape(ROWS, 128)
            f2 = facc[blk(i), :, :, g * 256 + 128 : g * 256 + 256].reshape(ROWS, 128)
            kb[blk(i), :, :, g * 256 : g * 256 + 128] = (
                ((f1 * cos + f2 * sin) * (1.0 / LOG2E)).astype(BF).reshape(ROWS // 64, 2, 32, 128)
            )
            kb[blk(i), :, :, g * 256 + 128 : g * 256 + 256] = (
                ((f2 * cos - f1 * sin) * (1.0 / LOG2E)).astype(BF).reshape(ROWS // 64, 2, 32, 128)
            )
        return 0

    lax.fori_loop(0, nrb, turn_back, 0)
    ag_done("a")
    for t, (src, e) in enumerate(((qb, eqk), (kb, eqk), (vb, ev))):
        for m in range(2):
            left = abuf[:, :, :, m * half : (m + 1) * half].reshape(seq_len, half)
            part = mm(TN, left, src[...].reshape(seq_len, pw)).astype(BF)
            zs = slice(m * nz // 2, (m + 1) * nz // 2)
            w_a[zs, :, :, :, t * hw : (t + 1) * hw] = (
                mm(NT, part, e[...]).astype(BF).reshape(nz // 2, 2, 2, nrow, hw)
            )
    rs0("a")
    wait(sb1, ex_s.at[4])

    def da_rows(at, which):
        total = None
        for t, src in enumerate((qb, kb, vb)):
            term = mm(NT, src[at, which].reshape(ROWS, pw), wp[:, t * pw : (t + 1) * pw])
            total = term if total is None else total + term
        return total.reshape(half_rows, 32, dim)

    def da_other(j, _):
        at = pl.ds(j * half_rows, half_rows)
        sb1[at] = da_rows(at, oth).astype(BF)
        return 0

    def da_own(j, _):
        at = pl.ds(j * half_rows, half_rows)
        own[at] = da_rows(at, c)
        return 0

    lax.fori_loop(0, groups // half_rows, da_other, 0)
    swap_start(7, sb1, rb1)
    lax.fori_loop(0, groups // half_rows, da_own, 0)

    @pl.when(away)
    def _():
        wait(xs, lo_s)

    wait(lo_ref, lo_r)
    wait(rb1, ex_r.at[7])

    def norm_four(i, _):
        rows_now = xbuf[i].astype(F32)
        r = r1b[i][:, 0:1]
        n = rows_now * r
        u = own[i] + rb1[i].astype(F32)
        dx = x1b[i] + r * (u - n * mean(u * n))
        xs[i] = dx.astype(BF)
        same = (i == dp) & (c == y)

        @pl.when(same)
        def _():
            pltpu.make_async_copy(xs.at[i], ret.at[slot], ret_r).start()

        @pl.when(jnp.logical_not(same))
        def _():
            rc(xs.at[i], ret.at[slot], ret_s, ret_r, (i, c)).start()

        return 0

    lax.fori_loop(0, groups, norm_four, 0)
    rs1("a")

    def finish_f(f, total):
        sums = jnp.zeros((nrow, 1), F32) if total is None else total
        t = rs3(f)
        at = pl.ds(pl.multiple_of(f * chunk, chunk), chunk)
        dg, du = t[:, 0:chunk], t[:, chunk : 2 * chunk]
        dg_out[:, at] = dg * gain2
        du_out[:, at] = du * gain2
        dd_out[:, at] = t[:, 2 * chunk : 3 * chunk]
        both = dg * wg[:, at].astype(F32) + du * wu[:, at].astype(F32)
        return sums + jnp.sum(both, axis=1, keepdims=True)

    sums2 = lax.fori_loop(0, nf, finish_f, jnp.zeros((nrow, 1), F32))
    rs2("a")
    do_out[...] = rs3("o")
    t = rs3("a")
    sums1 = jnp.zeros((nrow, 1), F32)
    for i, (w, out) in enumerate(((wq, dq_out), (wk, dk_out), (wv, dv_out))):
        part = t[:, i * hw : (i + 1) * hw]
        out[...] = part * gain1
        sums1 = sums1 + jnp.sum(part * w[...].astype(F32), axis=1, keepdims=True)
    first_half = lax.broadcasted_iota(jnp.int32, (nrow, 128), 1) < 64
    gs[...] = jnp.where(first_half, sums1, sums2)
    rc(gs, gr, gg_s, gg_r, ynbr).start()

    wait(ret, ret_r)

    def restore(s, _):
        def find(j, at):
            return jnp.where(deal[j] == s, j, at)

        gi_ref[s] = ret[lax.fori_loop(0, groups, find, 0)]
        return 0

    lax.fori_loop(0, groups, restore, 0)
    wait(gr, gg_r)
    both = gs[...] + gr[...]
    dg1_out[...] = jnp.sum(jnp.where(on_diag, both[:, 0:1], 0.0), axis=0, keepdims=True)
    dg2_out[...] = jnp.sum(jnp.where(on_diag, both[:, 64:65], 0.0), axis=0, keepdims=True)

    wait(gs, gg_s)
    for f in range(nf):
        rs_done(f)
    rs_done("o")
    rs_done("a")

    @pl.when(away)
    def _():
        wait(dybuf, dy_s)

    @pl.when(home)
    def _():
        wait(xs.at[pl.ds(0, groups - 1)], ret_s)

    @pl.when(away)
    def _():
        wait(xs, ret_s)

    wait(abuf.at[:, c], ex_s.at[0])
    wait(dfb.at[:, c], ex_s.at[1])
    wait(sb2, ex_s.at[5])
    wait(bbuf.at[:, c], ex_s.at[6])
    wait(sb1, ex_s.at[7])


def rotary_tables(count):
    lanes = np.arange(128) % 32
    frequency = np.where(lanes < HD // 2, BASE ** (-2.0 * lanes / HD), 0.0)
    high = np.zeros((32, 128))
    high[:count] = 32.0 * np.arange(count)[:, None] * frequency[None, :]
    low = np.arange(32)[:, None] * frequency[None, :]
    return np.stack([np.cos(high), np.sin(high), np.cos(low), np.sin(low)]).astype(np.float32)


def fused_body(
    x_given, dealing, seq_lengths, first_gain, query_weight, key_weight, value_weight,
    output_weight, second_gain, gate_weight, up_weight, down_weight, grad_output,
):
    groups, piece_rows, dim = x_given.shape
    hw = query_weight.shape[1]
    local_hidden = gate_weight.shape[1]
    chunk = 256
    nf = local_hidden // chunk
    nz = groups // 4
    rows = query_weight.shape[0]
    pw = hw // HD * 64
    seq_len = groups * 64
    vm, anym, sm = (
        pl.BlockSpec(memory_space=pltpu.VMEM),
        pl.BlockSpec(memory_space=pl.ANY),
        pl.BlockSpec(memory_space=pltpu.SMEM),
    )
    blocks = (groups, piece_rows, dim)
    pairs = (groups, 2, piece_rows)

    def gathered(width, lead=()):
        return pltpu.VMEM(lead + (nz, 2, 2, rows, width), BF)

    kd = nz // 2

    def landing(width, lead=()):
        return [
            pltpu.VMEM(lead + (nz, 2, rows, width), BF),
            pltpu.VMEM(lead + (kd, 2, 2, rows, width), BF),
            pltpu.VMEM(lead + (nz - kd, 2, rows, width), BF),
            pltpu.VMEM(lead + (nz, rows, width), BF),
        ]

    units = nf + 2
    dma = pltpu.SemaphoreType.DMA
    scratch = (
        [pltpu.VMEM(blocks, BF)] * 3
        + [pltpu.VMEM((rows, 3 * hw), BF), pltpu.VMEM((nf, rows, 3 * chunk), BF)]
        + [gathered(3 * hw), gathered(hw), gathered(3 * chunk, (nf,))]
        + [pltpu.VMEM((dim, 3 * pw), BF), pltpu.VMEM((dim, pw), BF)]
        + [pltpu.VMEM((hw, pw), BF)] * 2
        + [pltpu.VMEM((seq_len, 128), F32)] * 2
        + [pltpu.VMEM((32, seq_len), F32)] * 2
        + [pltpu.VMEM(pairs + (dim,), BF)]
        + [pltpu.VMEM(pairs + (pw,), BF)] * 3
        + [pltpu.VMEM((pw, seq_len), BF)] * 2
        + [pltpu.VMEM(pairs + (pw,), BF)]
        + [pltpu.VMEM((8, seq_len), F32)]
        + [pltpu.VMEM(blocks, F32)]
        + [pltpu.VMEM(blocks, BF)] * 4
        + [pltpu.VMEM(blocks, F32)]
        + [pltpu.VMEM((groups, piece_rows, 128), F32)] * 2
        + [pltpu.VMEM(pairs + (dim,), BF)] * 2
        + [pltpu.VMEM(pairs + (dim,), F32)] * 2
        + [pltpu.VMEM((seq_len, 3 * chunk), BF)]
        + [pltpu.VMEM(pairs + (pw,), BF)]
        + [pltpu.VMEM((16, seq_len), F32)]
        + landing(3 * hw)
        + landing(hw)
        + landing(3 * chunk, (nf,))
        + [pltpu.VMEM(blocks, BF)]
        + [pltpu.VMEM((rows, 128), F32)] * 3
        + [dma(())] * 4
        + [dma((units,)), dma((units,)), dma((units,)), dma((units, 2)), dma((units, nz + 3))]
        + [dma((units, 2)), dma((units, 2)), dma((units,)), dma((units, 2 * nz + 2))]
        + [dma((8,)), dma((8,))]
        + [dma(())] * 6
    )
    small = jax.ShapeDtypeStruct((rows, hw), F32)
    wide = jax.ShapeDtypeStruct((rows, local_hidden), F32)
    piece = jax.ShapeDtypeStruct(blocks, BF)
    outs = pl.pallas_call(
        functools.partial(fused_kernel, (nz, nf, dim, hw, chunk, rows)),
        out_shape=[piece, piece, small, small, small, small, wide, wide, wide]
        + [jax.ShapeDtypeStruct((1, rows), F32)] * 2,
        in_specs=[sm, sm, vm, anym] + [vm] * 10,
        out_specs=[anym] + [vm] * 10,
        scratch_shapes=scratch,
        compiler_params=pltpu.CompilerParams(
            collective_id=0, has_side_effects=True, vmem_limit_bytes=VMEM_LIMIT
        ),
        name="layer",
    )(
        dealing, seq_lengths, x_given, grad_output.reshape(blocks),
        first_gain.reshape(1, rows), second_gain.reshape(1, rows),
        query_weight, key_weight, value_weight, output_weight, gate_weight, up_weight, down_weight,
        rotary_tables(seq_len // 32),
    )
    outs = pl.pallas_call(
        pass_on,
        out_shape=[jax.ShapeDtypeStruct(o.shape, o.dtype) for o in outs],
        in_specs=[vm] * len(outs),
        out_specs=[vm] * len(outs),
        name="results",
    )(*outs)
    layer_out, grad_in, gq, gk, gv, go, gg, gu, gd, gain_one, gain_two = outs
    return (
        layer_out.reshape(grad_output.shape), grad_in, gain_one.reshape(rows), gq, gk, gv, go,
        gain_two.reshape(rows), gg, gu, gd,
    )


def pass_on(*refs):
    count = len(refs) // 2
    for i in range(count):
        refs[count + i][...] = refs[i][...]


def fits_fused(mesh):
    return mesh.shape["tensor"] == 2 and mesh.shape["dp"] % 8 == 0


def solution(mesh):
    placed = (
        P(None, ("dp", "tensor"), None),
        P(),
        P(),
        P("dp"),
        P("dp", "tensor"),
        P("dp", "tensor"),
        P("dp", "tensor"),
        P("dp", "tensor"),
        P("dp"),
        P("dp", "tensor"),
        P("dp", "tensor"),
        P("dp", "tensor"),
        P("dp", None, "tensor", None, None),
    )
    return jax.shard_map(
        fused_body if fits_fused(mesh) else body,
        mesh=mesh,
        in_specs=placed,
        out_specs=(
            P("dp", None, "tensor", None, None),
            P(None, ("dp", "tensor"), None),
            P("dp"),
            P("dp", "tensor"),
            P("dp", "tensor"),
            P("dp", "tensor"),
            P("dp", "tensor"),
            P("dp"),
            P("dp", "tensor"),
            P("dp", "tensor"),
            P("dp", "tensor"),
        ),
        check_vma=False,
    )
```

```python
import functools

import jax
import jax.numpy as jnp
import numpy as np
from jax import lax
from jax.experimental import pallas as pl
from jax.experimental.pallas import tpu as pltpu
from jax.sharding import PartitionSpec as P

HD = 48


EPS = 1e-05
BASE = 10000.0
VMEM_LIMIT = 64 * 1024 * 1024 - 65536


def tables(positions, head_size):
    freq_index = jnp.arange(head_size // 2, dtype=jnp.float32)
    frequency = BASE ** (-2.0 * freq_index / head_size)
    angles = positions[:, None] * frequency[None, :]
    return (jnp.cos(angles)[:, None, :], jnp.sin(angles)[:, None, :])


def rotary(values, cosine, sine_table):
    half_width = values.shape[-1] // 2
    first_half = values[..., :half_width]
    second_half = values[..., half_width:]
    return jnp.concatenate(
        [
            first_half * cosine - second_half * sine_table,
            second_half * cosine + first_half * sine_table,
        ],
        axis=-1,
    )


def rotary_back(values, cosine, sine_table):
    half_width = values.shape[-1] // 2
    first_half = values[..., :half_width]
    second_half = values[..., half_width:]
    return jnp.concatenate(
        [
            first_half * cosine + second_half * sine_table,
            second_half * cosine - first_half * sine_table,
        ],
        axis=-1,
    )


def row_dot(left_side, right_side):
    return jnp.dot(left_side, right_side, preferred_element_type=jnp.float32)


def dot_trans(left_side, right_side):
    return lax.dot_general(
        left_side, right_side, (((1,), (1,)), ((), ())), preferred_element_type=jnp.float32
    )


def dot_first(left_side, right_side):
    return lax.dot_general(
        left_side, right_side, (((0,), (0,)), ((), ())), preferred_element_type=jnp.float32
    )


def tensor_major(values, groups, pieces, piece_rows):
    columns = values.shape[1]
    return (
        values.reshape(groups, pieces, piece_rows, columns)
        .transpose(1, 0, 2, 3)
        .reshape(groups * pieces * piece_rows, columns)
    )


def rms_back(grad_normed, x_rows, scale_rows, gain):
    normed = x_rows * scale_rows
    weighted = grad_normed * gain
    x_grad = scale_rows * (weighted - normed * jnp.mean(weighted * normed, axis=-1, keepdims=True))
    return (x_grad, jnp.sum(grad_normed * normed, axis=0))


def block_scores(queries, key_rows, query_start, key_start, block_rows, score_scale):
    query_part = lax.dynamic_slice_in_dim(queries, query_start, block_rows, 0)
    key_part = lax.dynamic_slice_in_dim(key_rows, key_start, block_rows, 0)
    scores = (
        jnp.einsum("qhd,khd->hqk", query_part, key_part, preferred_element_type=jnp.float32)
        * score_scale
    )
    row_offsets = jnp.arange(block_rows)
    allowed = (key_start + row_offsets)[None, :] <= (query_start + row_offsets)[:, None]
    return jnp.where(allowed[None], scores, -1e30)


def attend_forward(queries, key_rows, value_rows, live_blocks, block_rows, score_scale):
    seq_len, heads, head_size = queries.shape

    def one_block(query_index, state_now):
        outputs, log_sums = state_now
        query_start = query_index * block_rows

        def stats(key_index, carried):
            running, exp_total = carried
            scores = block_scores(
                queries, key_rows, query_start, key_index * block_rows, block_rows, score_scale
            )
            newest = jnp.maximum(running, jnp.max(scores, axis=-1))
            exp_total = exp_total * jnp.exp(running - newest) + jnp.sum(
                jnp.exp(scores - newest[..., None]), axis=-1
            )
            return (newest, exp_total)

        initial = (
            jnp.full((heads, block_rows), -1e30, jnp.float32),
            jnp.zeros((heads, block_rows), jnp.float32),
        )
        running, exp_total = lax.fori_loop(0, query_index + 1, stats, initial)
        log_sum = running + jnp.log(exp_total)

        def accumulate(key_index, accumulated):
            key_start = key_index * block_rows
            scores = block_scores(
                queries, key_rows, query_start, key_start, block_rows, score_scale
            )
            prob_low = jnp.exp(scores - log_sum[..., None]).astype(jnp.bfloat16)
            value_part = lax.dynamic_slice_in_dim(value_rows, key_start, block_rows, 0)
            return accumulated + jnp.einsum(
                "hqk,khd->qhd", prob_low, value_part, preferred_element_type=jnp.float32
            )

        result = lax.fori_loop(
            0, query_index + 1, accumulate, jnp.zeros((block_rows, heads, head_size), jnp.float32)
        )
        outputs = lax.dynamic_update_slice_in_dim(outputs, result, query_start, 0)
        log_sums = lax.dynamic_update_slice_in_dim(log_sums, log_sum, query_start, 1)
        return (outputs, log_sums)

    initial = (
        jnp.zeros((seq_len, heads, head_size), jnp.float32),
        jnp.zeros((heads, seq_len), jnp.float32),
    )
    return lax.fori_loop(0, live_blocks, one_block, initial)


def attend_backward(
    queries, key_rows, value_rows, outputs, log_sums, out_grad, live_blocks, block_rows, score_scale
):
    seq_len, heads, head_size = queries.shape
    row_delta = jnp.einsum("qhd,qhd->hq", out_grad.astype(jnp.float32), outputs)

    def one_block(query_index, state_now):
        query_grads, key_grads, value_grads = state_now
        query_start = query_index * block_rows
        query_part = lax.dynamic_slice_in_dim(queries, query_start, block_rows, 0)
        grad_part = lax.dynamic_slice_in_dim(out_grad, query_start, block_rows, 0)
        logsum_part = lax.dynamic_slice_in_dim(log_sums, query_start, block_rows, 1)
        delta_part = lax.dynamic_slice_in_dim(row_delta, query_start, block_rows, 1)

        def inner(key_index, carried):
            query_acc, key_grads, value_grads = carried
            key_start = key_index * block_rows
            key_part = lax.dynamic_slice_in_dim(key_rows, key_start, block_rows, 0)
            value_part = lax.dynamic_slice_in_dim(value_rows, key_start, block_rows, 0)
            scores = block_scores(
                queries, key_rows, query_start, key_start, block_rows, score_scale
            )
            prob_soft = jnp.exp(scores - logsum_part[..., None])
            prob_low = prob_soft.astype(jnp.bfloat16)
            prob_grad = jnp.einsum(
                "qhd,khd->hqk", grad_part, value_part, preferred_element_type=jnp.float32
            )
            score_grad = (prob_soft * (prob_grad - delta_part[..., None])).astype(jnp.bfloat16)
            query_acc = (
                query_acc
                + jnp.einsum(
                    "hqk,khd->qhd", score_grad, key_part, preferred_element_type=jnp.float32
                )
                * score_scale
            )
            key_new = (
                jnp.einsum(
                    "hqk,qhd->khd", score_grad, query_part, preferred_element_type=jnp.float32
                )
                * score_scale
            )
            value_new = jnp.einsum(
                "hqk,qhd->khd", prob_low, grad_part, preferred_element_type=jnp.float32
            )
            key_old = lax.dynamic_slice_in_dim(key_grads, key_start, block_rows, 0)
            value_old = lax.dynamic_slice_in_dim(value_grads, key_start, block_rows, 0)
            key_grads = lax.dynamic_update_slice_in_dim(key_grads, key_old + key_new, key_start, 0)
            value_grads = lax.dynamic_update_slice_in_dim(
                value_grads, value_old + value_new, key_start, 0
            )
            return (query_acc, key_grads, value_grads)

        initial = (jnp.zeros((block_rows, heads, head_size), jnp.float32), key_grads, value_grads)
        query_acc, key_grads, value_grads = lax.fori_loop(0, query_index + 1, inner, initial)
        query_grads = lax.dynamic_update_slice_in_dim(query_grads, query_acc, query_start, 0)
        return (query_grads, key_grads, value_grads)

    zero_grads = jnp.zeros((seq_len, heads, head_size), jnp.float32)
    return lax.fori_loop(0, live_blocks, one_block, (zero_grads, zero_grads, zero_grads))


def body(
    x_given,
    dealing,
    seq_lengths,
    first_gain,
    query_weight,
    key_weight,
    value_weight,
    output_weight,
    second_gain,
    gate_weight,
    up_weight,
    down_weight,
    grad_output,
):
    groups = lax.axis_size("dp")
    pieces = lax.axis_size("tensor")
    group_index = lax.axis_index("dp")
    piece_index = lax.axis_index("tensor")
    seq_count, piece_rows, features = x_given.shape
    tokens = groups * piece_rows
    seq_len = tokens * pieces
    head_width = query_weight.shape[1]
    heads_local = head_width // HD
    block_rows = min(512, seq_len)
    score_scale = HD ** (-0.5)
    sequence = dealing[group_index]
    length = seq_lengths[sequence]
    live_blocks = (length + block_rows - 1) // block_rows
    outgoing = jnp.take(x_given, dealing, axis=0)
    arrived = lax.all_to_all(outgoing, "dp", split_axis=0, concat_axis=1, tiled=True)
    x_rows = arrived.reshape(tokens, features).astype(jnp.float32)
    row_ids = jnp.arange(tokens)
    positions_local = (
        row_ids // piece_rows * pieces + piece_index
    ) * piece_rows + row_ids % piece_rows
    live_rows = (positions_local < length).astype(jnp.float32)[:, None]
    columns = (
        lax.all_gather(gate_weight, "tensor", axis=1, tiled=True),
        lax.all_gather(up_weight, "tensor", axis=1, tiled=True),
        lax.all_gather(down_weight, "tensor", axis=1, tiled=True),
    )
    gathered = (
        lax.all_gather(first_gain, "dp", axis=0, tiled=True),
        lax.all_gather(second_gain, "dp", axis=0, tiled=True),
        lax.all_gather(query_weight, "dp", axis=0, tiled=True),
        lax.all_gather(key_weight, "dp", axis=0, tiled=True),
        lax.all_gather(value_weight, "dp", axis=0, tiled=True),
        lax.all_gather(output_weight, "dp", axis=0, tiled=True),
        lax.all_gather(columns[0], "dp", axis=0, tiled=True),
        lax.all_gather(columns[1], "dp", axis=0, tiled=True),
        lax.all_gather(columns[2], "dp", axis=0, tiled=True),
    )
    (
        gain_one,
        gain_two,
        query_full,
        key_full,
        value_full,
        out_full,
        gate_full,
        up_full,
        down_full,
    ) = gathered
    qkv_weight = jnp.concatenate([query_full, key_full, value_full], axis=1)
    scale_one = lax.rsqrt(jnp.mean(x_rows * x_rows, axis=-1, keepdims=True) + EPS)
    normed = (x_rows * scale_one * gain_one).astype(jnp.bfloat16)
    normed_full = lax.all_gather(
        normed.reshape(groups, 1, piece_rows, features), "tensor", axis=1, tiled=True
    ).reshape(seq_len, features)
    projected = row_dot(normed_full, qkv_weight)
    cosine, sine_table = tables(jnp.arange(seq_len, dtype=jnp.float32), HD)
    queries = rotary(
        projected[:, :head_width].reshape(seq_len, heads_local, HD), cosine, sine_table
    ).astype(jnp.bfloat16)
    key_rows = rotary(
        projected[:, head_width : 2 * head_width].reshape(seq_len, heads_local, HD),
        cosine,
        sine_table,
    ).astype(jnp.bfloat16)
    value_rows = (
        projected[:, 2 * head_width :].astype(jnp.bfloat16).reshape(seq_len, heads_local, HD)
    )
    mixed, log_sums = attend_forward(
        queries, key_rows, value_rows, live_blocks, block_rows, score_scale
    )
    mixed_low = mixed.reshape(seq_len, head_width).astype(jnp.bfloat16)
    mixed_major = tensor_major(mixed_low, groups, pieces, piece_rows)
    attention = lax.psum_scatter(
        dot_trans(mixed_major, out_full).astype(jnp.bfloat16),
        "tensor",
        scatter_dimension=0,
        tiled=True,
    ).astype(jnp.float32)
    hidden_one = x_rows + live_rows * attention
    scale_two = lax.rsqrt(jnp.mean(hidden_one * hidden_one, axis=-1, keepdims=True) + EPS)
    normed_two = (hidden_one * scale_two * gain_two).astype(jnp.bfloat16)
    gate_act = row_dot(normed_two, gate_full)
    up_act = row_dot(normed_two, up_full)
    sigmoid_act = jax.nn.sigmoid(gate_act)
    silu_act = gate_act * sigmoid_act
    hidden = (silu_act * up_act).astype(jnp.bfloat16)
    branch = dot_trans(hidden, down_full)
    result = hidden_one + live_rows * branch
    layer_out = result.astype(jnp.bfloat16).reshape(1, groups, 1, piece_rows, features)
    out_grad = grad_output.reshape(tokens, features).astype(jnp.float32)
    branch_grad = (live_rows * out_grad).astype(jnp.bfloat16)
    hidden_grad = row_dot(branch_grad, down_full)
    down_term = dot_first(branch_grad, hidden)
    gate_grad = (
        hidden_grad * up_act * sigmoid_act * (1.0 + gate_act * (1.0 - sigmoid_act))
    ).astype(jnp.bfloat16)
    up_grad = (hidden_grad * silu_act).astype(jnp.bfloat16)
    normed_two_grad = dot_trans(gate_grad, gate_full) + dot_trans(up_grad, up_full)
    gate_term = dot_first(normed_two, gate_grad)
    up_term = dot_first(normed_two, up_grad)
    hidden_one_grad, gain_two_term = rms_back(normed_two_grad, hidden_one, scale_two, gain_two)
    hidden_one_grad = hidden_one_grad + out_grad
    attention_grad = (live_rows * hidden_one_grad).astype(jnp.bfloat16)
    attention_full = lax.all_gather(
        attention_grad.reshape(groups, 1, piece_rows, features), "tensor", axis=1, tiled=True
    ).reshape(seq_len, features)
    mixed_grad = row_dot(attention_full, out_full).astype(jnp.bfloat16)
    out_term = dot_first(attention_full, mixed_low)
    query_grads, key_grads, value_grads = attend_backward(
        queries,
        key_rows,
        value_rows,
        mixed,
        log_sums,
        mixed_grad.reshape(seq_len, heads_local, HD),
        live_blocks,
        block_rows,
        score_scale,
    )
    query_back = (
        rotary_back(query_grads, cosine, sine_table)
        .reshape(seq_len, head_width)
        .astype(jnp.bfloat16)
    )
    key_back = (
        rotary_back(key_grads, cosine, sine_table).reshape(seq_len, head_width).astype(jnp.bfloat16)
    )
    value_back = value_grads.reshape(seq_len, head_width).astype(jnp.bfloat16)
    projected_grad = jnp.concatenate([query_back, key_back, value_back], axis=1)
    qkv_term = dot_first(normed_full, projected_grad)
    grad_major = tensor_major(projected_grad, groups, pieces, piece_rows)
    normed_grad = lax.psum_scatter(
        dot_trans(grad_major, qkv_weight).astype(jnp.bfloat16),
        "tensor",
        scatter_dimension=0,
        tiled=True,
    ).astype(jnp.float32)
    input_grad, gain_one_term = rms_back(normed_grad, x_rows, scale_one, gain_one)
    input_grad = input_grad + hidden_one_grad
    returned = lax.all_to_all(
        input_grad.astype(jnp.bfloat16).reshape(groups, piece_rows, features),
        "dp",
        split_axis=0,
        concat_axis=0,
        tiled=True,
    )
    grad_in = jnp.zeros_like(x_given).at[dealing].set(returned)
    gain_pair = jnp.stack([gain_one_term, gain_two_term], axis=1)
    query_term = qkv_term[:, :head_width]
    key_term = qkv_term[:, head_width : 2 * head_width]
    value_term = qkv_term[:, 2 * head_width :]
    summed = (
        lax.psum_scatter(
            gain_pair.astype(jnp.bfloat16), "dp", scatter_dimension=0, tiled=True
        ).astype(jnp.float32),
        lax.psum_scatter(
            query_term.astype(jnp.bfloat16), "dp", scatter_dimension=0, tiled=True
        ).astype(jnp.float32),
        lax.psum_scatter(
            key_term.astype(jnp.bfloat16), "dp", scatter_dimension=0, tiled=True
        ).astype(jnp.float32),
        lax.psum_scatter(
            value_term.astype(jnp.bfloat16), "dp", scatter_dimension=0, tiled=True
        ).astype(jnp.float32),
        lax.psum_scatter(
            out_term.astype(jnp.bfloat16), "dp", scatter_dimension=0, tiled=True
        ).astype(jnp.float32),
        lax.psum_scatter(
            gate_term.astype(jnp.bfloat16), "dp", scatter_dimension=0, tiled=True
        ).astype(jnp.float32),
        lax.psum_scatter(
            up_term.astype(jnp.bfloat16), "dp", scatter_dimension=0, tiled=True
        ).astype(jnp.float32),
        lax.psum_scatter(
            down_term.astype(jnp.bfloat16), "dp", scatter_dimension=0, tiled=True
        ).astype(jnp.float32),
    )
    across = (
        lax.psum_scatter(
            jnp.tile(summed[0], (1, pieces)).astype(jnp.bfloat16),
            "tensor",
            scatter_dimension=1,
            tiled=True,
        ).astype(jnp.float32),
        lax.psum_scatter(
            summed[5].astype(jnp.bfloat16), "tensor", scatter_dimension=1, tiled=True
        ).astype(jnp.float32),
        lax.psum_scatter(
            summed[6].astype(jnp.bfloat16), "tensor", scatter_dimension=1, tiled=True
        ).astype(jnp.float32),
        lax.psum_scatter(
            summed[7].astype(jnp.bfloat16), "tensor", scatter_dimension=1, tiled=True
        ).astype(jnp.float32),
    )
    gain_sums = across[0]
    query_sum, key_sum, value_sum, out_sum = (summed[1], summed[2], summed[3], summed[4])
    gate_sum, up_sum, down_sum = (across[1], across[2], across[3])
    return (
        layer_out,
        grad_in,
        gain_sums[:, 0],
        query_sum,
        key_sum,
        value_sum,
        out_sum,
        gain_sums[:, 1],
        gate_sum,
        up_sum,
        down_sum,
    )


MESH = pl.DeviceIdType.MESH
BF = jnp.bfloat16
F32 = jnp.float32
NN = (((1,), (0,)), ((), ()))
NT = (((1,), (1,)), ((), ()))
TN = (((0,), (0,)), ((), ()))
LOG2E = 1.4426950408889634
ROWS = 256


def mm(kind, left_side, right_side):
    return lax.dot_general(left_side, right_side, kind, preferred_element_type=F32)


def fused_kernel(
    shape,
    deal, lens, x_ref, dy_ref, g1, g2, wq, wk, wv, wo, wg, wu, wd, tab,
    lo_ref, gi_ref, dq_out, dk_out, dv_out, do_out, dg_out, du_out, dd_out, dg1_out, dg2_out,
    xs, xbuf, dybuf, src_a, src_f, w_a, w_f, wp, wop, eqk, ev, cosb, sinb, ct, st,
    abuf, qb, kb, vb, vt, ot, ob, lse, own, sb1, sb2, rb1, rb2, x1b, rb, bb0, bb1, dd0, dd1,
    facc, uacc, act, delta, urecv, frecv, usend, fsend,
    rx_a, ry_a, ry2_a, rz_a, rx_f, rz_f, ret, gs, gr,
    a2a_s, a2a_r, dy_s, dy_r, ag_z, ag_x, ag_y, ag_d, ag_s, rs_x, rs_y, rs_z, rs_s,
    agf_z, agf_f, agf_x, agf_s, rsf_x, rsf_z, rsf_s, ex_s, ex_r, b_s, b_r, us_s, us_r, fs_s, fs_r,
    uy_s, uy_r, lo_r, ret_s, ret_r, gg_s, gg_r, free,
):
    nz, dim, hw, fq, nrow = shape
    groups = 4 * nz
    seq_len = 64 * groups
    half = dim // 2
    nrb = seq_len // ROWS
    kd = nz // 2
    dp = lax.axis_index("dp")
    y = lax.axis_index("tensor")
    z = dp // 4
    x = (dp // 2) % 2
    c = dp % 2
    xb, yb, oth = 1 - x, 1 - y, 1 - c
    home = c == y
    away = c != y
    slot = (z * 2 + x) * 2 + y
    score_scale = HD ** (-0.5)

    def dev(z_, x_, c_, y_):
        return ((z_ * 2 + x_) * 2 + c_, y_)

    partner = dev(z, x, oth, y)
    xnbr = dev(z, xb, c, y)
    ynbr = dev(z, x, c, yb)
    other_slot = (z * 2 + x) * 2 + yb

    def rc(src, dst, ss, rs, to):
        return pltpu.make_async_remote_copy(
            src_ref=src, dst_ref=dst, send_sem=ss, recv_sem=rs, device_id=to, device_id_type=MESH
        )

    def wait(ref, sem):
        pltpu.make_async_copy(ref, ref, sem).wait()

    bar = pltpu.get_barrier_semaphore()
    ndev = groups * 2

    def greet(i, _):
        t = lax.rem(dp * 2 + y + i, ndev)
        pl.semaphore_signal(bar, inc=1, device_id=(t // 2, t % 2), device_id_type=MESH)
        return 0

    lax.fori_loop(1, ndev, greet, 0)
    pl.semaphore_wait(bar, ndev - 1)

    def unit(k):
        return (wo if k == 3 else src_a.at[k]), w_a.at[k], k

    def zsend(k):
        src, buf, n = unit(k)
        for i in range(1, nz):
            zt = lax.rem(z + i, nz)
            rc(src, buf.at[z, x, c], ag_s.at[n, i - 1], ag_z.at[n], dev(zt, x, y, y)).start()

        @pl.when(home)
        def _():
            pltpu.make_async_copy(src, buf.at[z, x, c], ag_z.at[n]).start()

        @pl.when(away)
        def _():
            rc(src, buf.at[z, x, c], ag_s.at[n, nz - 1], ag_z.at[n], dev(z, x, y, y)).start()

    def ag1(k):
        src, buf, n = unit(k)

        @pl.when(home)
        def _():
            wait(buf.at[:, x], ag_z.at[n])
            rc(buf.at[:, x], buf.at[:, x], ag_s.at[n, nz], ag_y.at[n], ynbr).start()
            rc(buf.at[:, x], buf.at[:, x], ag_s.at[n, nz + 1], ag_x.at[n], xnbr).start()

    def ag2(k):
        src, buf, n = unit(k)

        @pl.when(home)
        def _():
            wait(buf.at[:, xb], ag_x.at[n])
            part = buf.at[pl.ds(0, kd), xb]
            rc(part, part, ag_s.at[n, nz + 2], ag_d.at[n, 0], ynbr).start()

        @pl.when(away)
        def _():
            wait(buf.at[:, x], ag_y.at[n])
            part = buf.at[pl.ds(kd, nz - kd), x]
            rc(part, part, ag_s.at[n, nz + 2], ag_d.at[n, 1], xnbr).start()

    def ag3(k):
        src, buf, n = unit(k)

        @pl.when(away)
        def _():
            wait(buf.at[pl.ds(0, kd), xb], ag_d.at[n, 0])
            wait(buf.at[pl.ds(kd, nz - kd), xb], ag_d.at[n, 1])

    def ag_done(k):
        src, buf, n = unit(k)
        for i in range(nz - 1):
            wait(src, ag_s.at[n, i])

        @pl.when(home)
        def _():
            wait(buf.at[:, x], ag_s.at[n, nz])
            wait(buf.at[:, x], ag_s.at[n, nz + 1])
            wait(buf.at[pl.ds(0, kd), xb], ag_s.at[n, nz + 2])

        @pl.when(away)
        def _():
            wait(src, ag_s.at[n, nz - 1])
            wait(buf.at[pl.ds(kd, nz - kd), x], ag_s.at[n, nz + 2])

    def rs_unit(k):
        return w_a.at[k], rx_a.at[k], ry_a.at[k], ry2_a.at[k], rz_a.at[k], k

    def src_unit(m, cc):
        ref = wd if m == 2 else src_f.at[m]
        return ref.at[:, cc * fq : (cc + 1) * fq]

    at_end = (z == 0) | (z == nz - 1)
    relay = jnp.where(z < nz // 2, nz - 1, 0)

    def zsendf(m):
        land = w_f.at[m, z, x, c]
        for i in range(nz):
            zt = lax.rem(z + i, nz)
            span = jnp.abs(zt - z)
            for cc in range(2):
                src = src_unit(m, cc)
                to = dev(zt, x, cc, y)
                far = rc(src, land, agf_s.at[m, 2 * i + cc], agf_z.at[m], to)
                fed = rc(src, land, agf_s.at[m, 2 * i + cc], agf_f.at[m], to)
                if i:
                    passed = at_end & (span == nz - 2)
                    pl.when(passed)(fed.start)
                    pl.when(jnp.logical_not(passed) & (span < nz - 1))(far.start)
                else:
                    pl.when(c != cc)(far.start)
                    pl.when(c == cc)(pltpu.make_async_copy(src, land, agf_z.at[m]).start)

    def agf1(m):
        block = w_f.at[m, relay, x]
        wait(block, agf_f.at[m])
        far = rc(block, block, agf_s.at[m, 2 * nz + 1], agf_f.at[m], dev(nz - 1 - relay, x, c, y))
        pl.when(jnp.logical_not(at_end))(far.start)
        wait(w_f.at[m, pl.ds(0, nz - 1), x], agf_z.at[m])
        rc(w_f.at[m, :, x], w_f.at[m, :, x], agf_s.at[m, 2 * nz], agf_x.at[m], xnbr).start()

    def agf2(m):
        wait(w_f.at[m, :, xb], agf_x.at[m])

    def agf_done(m):
        for i in range(nz):
            span = jnp.abs(lax.rem(z + i, nz) - z)
            for cc in range(2):
                sent = (span < nz - 1) if i else (c != cc)

                @pl.when(sent)
                def _():
                    wait(src_unit(m, cc), agf_s.at[m, 2 * i + cc])

        @pl.when(jnp.logical_not(at_end))
        def _():
            wait(w_f.at[m, 0, x], agf_s.at[m, 2 * nz + 1])

        wait(w_f.at[m, :, x], agf_s.at[m, 2 * nz])

    def rsf0(m):
        rc(w_f.at[m, :, xb], rx_f.at[m], rsf_s.at[m, 2 * nz], rsf_x.at[m], xnbr).start()

    def rsf1(m):
        wait(rx_f.at[m], rsf_x.at[m])
        for v in range(2):

            @pl.when(x == v)
            def _():
                rx_f[m] = (w_f[m, :, v].astype(F32) + rx_f[m].astype(F32)).astype(BF)

        for i in range(nz):
            zt = lax.rem(z + i, nz)
            for cc in range(2):
                src, land = rx_f.at[m, zt, cc], rz_f.at[m, z, c]
                far = rc(src, land, rsf_s.at[m, 2 * i + cc], rsf_z.at[m], dev(zt, x, cc, y))
                if i:
                    far.start()
                else:
                    pl.when(c != cc)(far.start)
                    pl.when(c == cc)(pltpu.make_async_copy(src, land, rsf_z.at[m]).start)

    def rsf3(m):
        wait(rz_f.at[m], rsf_z.at[m])
        halves = []
        for cc in range(2):
            total = rz_f[m, 0, cc].astype(F32)
            for i in range(1, nz):
                total = total + rz_f[m, i, cc].astype(F32)
            halves.append(total)
        return jnp.concatenate(halves, axis=1)

    def rsf_done(m):
        for i in range(nz):
            for cc in range(2):
                if i:
                    wait(rz_f.at[m, 0, 0], rsf_s.at[m, 2 * i + cc])
                else:

                    @pl.when(c != cc)
                    def _():
                        wait(rz_f.at[m, 0, 0], rsf_s.at[m, cc])

        wait(rx_f.at[m], rsf_s.at[m, 2 * nz])

    lo_z = pl.ds(0, kd)
    hi_z = pl.ds(kd, nz - kd)

    def at_unit(ref, k, *spot):
        return ref[(k,) + spot].astype(F32)

    def put_unit(ref, k, total, *spot):
        ref[(k,) + spot] = total.astype(BF)

    every = slice(None)

    def by_x(step):
        for v in range(2):
            pl.when(x == v)(functools.partial(step, v, 1 - v))

    def rs0(k):
        g, rx, ry, ry2, rz, n = rs_unit(k)
        rc(g.at[hi_z, xb], rx.at[hi_z], rs_s.at[n, 0], rs_x.at[n, 1], xnbr).start()

        @pl.when(away)
        def _():
            rc(g.at[lo_z], ry, rs_s.at[n, 1], rs_y.at[n, 0], ynbr).start()

    def rs1(k):
        g, rx, ry, ry2, rz, n = rs_unit(k)
        g_all, rx_all, ry_all, ry2_all = w_a, rx_a, ry_a, ry2_a

        @pl.when(away)
        def _():
            wait(rx.at[hi_z], rs_x.at[n, 1])

            @by_x
            def _(v, vb):
                put_unit(ry2_all, k, at_unit(g_all, k, hi_z, v) + at_unit(rx_all, k, hi_z))

            rc(ry2, ry2, rs_s.at[n, 2], rs_y.at[n, 1], ynbr).start()

        @pl.when(home)
        def _():
            wait(ry, rs_y.at[n, 0])

            @by_x
            def _(v, vb):
                total = at_unit(g_all, k, lo_z, vb) + at_unit(ry_all, k, every, vb)
                put_unit(ry_all, k, total, every, vb)

            rc(ry.at[:, xb], rx.at[lo_z], rs_s.at[n, 2], rs_x.at[n, 0], xnbr).start()

    def rs2(k):
        g, rx, ry, ry2, rz, n = rs_unit(k)
        g_all, rx_all, ry_all, ry2_all = w_a, rx_a, ry_a, ry2_a

        @pl.when(home)
        def _():
            wait(rx.at[hi_z], rs_x.at[n, 1])
            wait(ry2, rs_y.at[n, 1])

            @by_x
            def _(v, vb):
                total = at_unit(g_all, k, hi_z, v) + at_unit(rx_all, k, hi_z) + at_unit(ry2_all, k)
                put_unit(rx_all, k, total, hi_z)

            wait(rx.at[lo_z], rs_x.at[n, 0])

            @by_x
            def _(v, vb):
                total = at_unit(g_all, k, lo_z, v) + at_unit(ry_all, k, every, v)
                put_unit(rx_all, k, total + at_unit(rx_all, k, lo_z), lo_z)

            for i in range(1, nz):
                zt = lax.rem(z + i, nz)
                for cc in range(2):
                    rc(
                        rx.at[zt, cc], rz.at[z], rs_s.at[n, 3 + 2 * (i - 1) + cc], rs_z.at[n],
                        dev(zt, x, cc, y),
                    ).start()
            rc(rx.at[z, oth], rz.at[z], rs_s.at[n, 2 * nz + 1], rs_z.at[n], partner).start()
            pltpu.make_async_copy(rx.at[z, c], rz.at[z], rs_z.at[n]).start()

    def rs_done(k):
        g, rx, ry, ry2, rz, n = rs_unit(k)
        wait(rx.at[hi_z], rs_s.at[n, 0])

        @pl.when(away)
        def _():
            wait(ry, rs_s.at[n, 1])
            wait(ry2, rs_s.at[n, 2])

        @pl.when(home)
        def _():
            wait(rx.at[lo_z], rs_s.at[n, 2])
            for i in range(2 * (nz - 1) + 1):
                wait(rz.at[0], rs_s.at[n, 3 + i])

    def rs3(k):
        g, rx, ry, ry2, rz, n = rs_unit(k)
        wait(rz, rs_z.at[n])
        total = None
        for i in range(nz):
            part = rz_a[k, i].astype(F32)
            total = part if total is None else total + part
        return total

    fetch = pltpu.make_async_copy(x_ref, ret, lo_r)
    fetch.start()
    square = (nrow, nrow)
    on_diag = lax.broadcasted_iota(jnp.int32, square, 0) == lax.broadcasted_iota(
        jnp.int32, square, 1
    )

    def column(ref):
        spread = jnp.where(on_diag, ref[...].astype(F32), 0.0)
        return jnp.sum(spread, axis=1, keepdims=True)

    gain1 = column(g1)
    gain2 = column(g2)
    for i, w in enumerate((wq, wk, wv)):
        src_a[i] = (w[...].astype(F32) * gain1).astype(BF)
        zsend(i)

    def stage(j, _):
        xs[j] = ret[deal[j]]
        return 0

    fetch.wait()
    lax.fori_loop(0, groups, stage, 0)

    def deal_out(i, _):
        j = lax.rem(slot + i, groups)
        dpd = (j // 2) * 2 + y
        td = j % 2
        same = (dpd == dp) & (td == y)

        @pl.when(same)
        def _():
            pltpu.make_async_copy(xs.at[j], xbuf.at[dp], a2a_r).start()

        @pl.when(jnp.logical_not(same))
        def _():
            rc(xs.at[j], xbuf.at[dp], a2a_s, a2a_r, (dpd, td)).start()

        return 0

    lax.fori_loop(0, groups, deal_out, 0)

    src_f[0] = (wg[...].astype(F32) * gain2).astype(BF)
    src_f[1] = (wu[...].astype(F32) * gain2).astype(BF)

    def rope_rows(i, _):
        ca, sa = tab[0, pl.ds(i, 1), :], tab[1, pl.ds(i, 1), :]
        cb, sb = tab[2], tab[3]
        at = pl.ds(pl.multiple_of(i * 32, 32), 32)
        cosb[at, :] = ca * cb - sa * sb
        sinb[at, :] = sa * cb + ca * sb
        return 0

    lax.fori_loop(0, seq_len // 32, rope_rows, 0)
    for i in range(nrb):
        at = slice(i * ROWS, (i + 1) * ROWS)
        ct[:, at] = cosb[at, :].T[0:32]
        st[:, at] = sinb[at, :].T[0:32]
    pw = wop.shape[1]
    row = lax.broadcasted_iota(jnp.int32, (hw, pw), 0)
    col = lax.broadcasted_iota(jnp.int32, (hw, pw), 1)
    low = col & 31
    spot = ((col >> 8) * 4 + ((col >> 5) & 3)) * HD + ((col >> 7) & 1) * (HD // 2) + low
    eqk[...] = jnp.where((row == spot) & (low < HD // 2), 1.0, 0.0).astype(BF)
    low = col & 63
    ev[...] = jnp.where((row == (col >> 6) * HD + low) & (low < HD), 1.0, 0.0).astype(BF)

    length = lens[deal[slot]]
    other_length = lens[deal[other_slot]]

    def live_at(i):
        at = (i * 2 + c) * 32 + lax.broadcasted_iota(jnp.int32, (32, 1), 0)
        return at < length

    def mean(values):
        return jnp.mean(values, axis=1, keepdims=True)

    def swap_start(n, src, dst):
        rc(src, dst, ex_s.at[n], ex_r.at[n], partner).start()

    def blk(i):
        return pl.ds(i * (ROWS // 64), ROWS // 64)

    for i in range(3):
        ag1(i)
    zsend(3)
    zsendf(0)

    def gather_dy(mine):
        pltpu.make_async_copy(dy_ref, mine.at[:, y], dy_r.at[0]).start()

    def send_dy(far):
        rc(dy_ref, far.at[:, y], dy_s.at[0], dy_r.at[1], ynbr).start()

    for i in range(3):
        ag2(i)
    wait(xbuf, a2a_r)
    zsendf(1)

    def norm_one(i, _):
        rows_now = xbuf[i].astype(F32)
        r = lax.rsqrt(mean(rows_now * rows_now) + EPS)
        rb[i] = jnp.broadcast_to(r, (32, 128))
        abuf[i, c] = (rows_now * r).astype(BF)
        return 0

    lax.fori_loop(0, groups, norm_one, 0, unroll=2)
    swap_start(0, abuf.at[:, c], abuf.at[:, c])
    for i in range(3):
        ag3(i)
        e = eqk if i < 2 else ev
        wp[:, i * pw : (i + 1) * pw] = mm(
            NN, w_a[i].reshape(dim, hw), e[...]
        ).astype(BF)
    @pl.when(home)
    def _():
        gather_dy(dd0)
        send_dy(dd1)

    @pl.when(away)
    def _():
        gather_dy(dd1)
        send_dy(dd0)

    ag1(3)
    zsendf(2)
    wait(abuf.at[:, oth], ex_r.at[0])

    query_scale = score_scale * LOG2E
    lane64 = lax.broadcasted_iota(jnp.int32, (ROWS, pw), 1) & 63

    def project(i, _):
        a = abuf[blk(i)].reshape(ROWS, dim)
        at = pl.ds(pl.multiple_of(i * ROWS, ROWS), ROWS)
        cos, sin = cosb[at, :], sinb[at, :]
        for t, (dst, scale) in enumerate(((qb, query_scale), (kb, 1.0))):
            u = mm(NN, a, wp[:, t * pw : (t + 1) * pw]) * scale
            for g in range(pw // 256):
                f1 = u[:, g * 256 : g * 256 + 128]
                f2 = u[:, g * 256 + 128 : g * 256 + 256]
                dst[blk(i), :, :, g * 256 : g * 256 + 128] = (
                    (f1 * cos - f2 * sin).astype(BF).reshape(ROWS // 64, 2, 32, 128)
                )
                dst[blk(i), :, :, g * 256 + 128 : g * 256 + 256] = (
                    (f2 * cos + f1 * sin).astype(BF).reshape(ROWS // 64, 2, 32, 128)
                )
        v = mm(NN, a, wp[:, 2 * pw : 3 * pw])
        v = jnp.where(lane64 == HD, 1.0, v).astype(BF)
        vb[blk(i)] = v.reshape(ROWS // 64, 2, 32, pw)
        vt[:, at] = v.T
        return 0

    lax.fori_loop(0, nrb, project, 0)
    ag2(3)
    agf1(0)

    lane = lax.broadcasted_iota(jnp.int32, (ROWS, 256), 1)
    diag = lax.broadcasted_iota(jnp.int32, (ROWS, ROWS), 0) <= lax.broadcasted_iota(
        jnp.int32, (ROWS, ROWS), 1
    )

    def rows_of(ref, first, count, lanes):
        return ref[pl.ds(first // 64, count // 64), :, :, lanes].reshape(count, 256)

    def attend(i):
        keys = (i + 1) * ROWS

        def group(g, _):
            lanes = pl.ds(pl.multiple_of(g * 256, 256), 256)
            q = rows_of(qb, i * ROWS, ROWS, lanes)
            for hh in range(4):
                qm = jnp.where(((lane >> 5) & 3) == hh, q, jnp.zeros_like(q))
                sd = mm(NT, rows_of(kb, i * ROWS, ROWS, lanes), qm)
                sd = jnp.where(diag, sd, -1e30)
                top = jnp.max(sd, axis=0, keepdims=True)
                if i:
                    s = mm(NT, rows_of(kb, 0, i * ROWS, lanes), qm)
                    top = jnp.maximum(top, jnp.max(s, axis=0, keepdims=True))
                    p = jnp.concatenate(
                        [jnp.exp2(s - top).astype(BF), jnp.exp2(sd - top).astype(BF)], axis=0
                    )
                else:
                    p = jnp.exp2(sd - top).astype(BF)
                hs = pl.multiple_of(g * 256 + hh * 64, 64)
                o = mm(NN, vt[pl.ds(hs, 64), 0:keys], p)
                total = o[HD : HD + 1, :]
                ot[pl.ds(hs, 64), i * ROWS : keys] = (o * (1.0 / total)).astype(BF)
                lse[pl.ds(g * 4 + hh, 1), i * ROWS : keys] = top + jnp.log2(total)
            return 0

        lax.fori_loop(0, pw // 256, group, 0)

    def hand_dy(mine):
        wait(mine.at[:, y], dy_r.at[0])
        wait(mine.at[:, yb], dy_r.at[1])
        rc(mine, mine, ex_s.at[1], ex_r.at[1], partner).start()

    def during_zero():
        agf1(1)

    def during_one():
        ag3(3)
        wop[...] = mm(NN, w_a[3].reshape(dim, hw), ev[...]).astype(BF)

    def during_two():
        pl.when(home)(lambda: hand_dy(dd0))
        pl.when(away)(lambda: hand_dy(dd1))

    def settle_dy():
        pl.when(home)(lambda: wait(dd1, ex_r.at[1]))
        pl.when(away)(lambda: wait(dd0, ex_r.at[1]))
        wait(dd0, ex_s.at[1])

        def save_dy(i, _):
            dybuf[i] = dd0[i, c]
            return 0

        lax.fori_loop(0, groups, save_dy, 0)

        def mask_dy(i, _):
            at = i * ROWS + lax.broadcasted_iota(jnp.int32, (ROWS, 1), 0)
            zeros = jnp.zeros((ROWS, dim), BF)
            for ref, count in ((dd0, length), (dd1, other_length)):
                masked = jnp.where(at < count, ref[blk(i)].reshape(ROWS, dim), zeros)
                ref[blk(i)] = masked.reshape(ROWS // 64, 2, 32, dim)
            return 0

        lax.fori_loop(0, nrb, mask_dy, 0)

    def with_steps(part, steps):
        for i in range(nrb):
            part(i)
            for at, step in steps:
                if min(at, nrb - 1) == i:
                    step()

    with_steps(attend, ((0, during_zero), (1, during_one), (2, during_two)))
    agf1(2)

    def turn(i, _):
        at = pl.ds(pl.multiple_of(i * ROWS, ROWS), ROWS)
        ob[blk(i)] = ot[:, at].T.reshape(ROWS // 64, 2, 32, pw)
        return 0

    lax.fori_loop(0, nrb, turn, 0)

    half_rows = ROWS // 32

    def att_other(j, _):
        at = pl.ds(j * half_rows, half_rows)
        o = ob[at, oth].reshape(ROWS, pw)
        sb1[at] = mm(NT, o, wop[...]).astype(BF).reshape(half_rows, 32, dim)
        return 0

    def att_own(j, _):
        at = pl.ds(j * half_rows, half_rows)
        o = ob[at, c].reshape(ROWS, pw)
        own[at] = mm(NT, o, wop[...]).reshape(half_rows, 32, dim)
        return 0

    lax.fori_loop(0, groups // half_rows, att_other, 0)
    swap_start(2, sb1, rb1)
    lax.fori_loop(0, groups // half_rows, att_own, 0)
    wait(rb1, ex_r.at[2])

    low_lanes = lax.broadcasted_iota(jnp.int32, (32, 128), 1) < 64

    def norm_two(i, _):
        att = own[i] + rb1[i].astype(F32)
        x1 = xbuf[i].astype(F32) + jnp.where(live_at(i), att, 0.0)
        x1b[i] = x1
        r = lax.rsqrt(mean(x1 * x1) + EPS)
        rb[i] = jnp.where(low_lanes, rb[i], r)
        bb0[i, c] = (x1 * r).astype(BF)
        return 0

    hg = groups // 2

    for hf in range(2):
        lax.fori_loop(hf * hg, (hf + 1) * hg, norm_two, 0, unroll=2)
        at = pl.ds(hf * hg, hg)
        rc(bb0.at[at, c], bb1.at[at, c], b_s.at[1, hf], b_r.at[1, hf], ynbr).start()
        rc(bb0.at[at, c], bb0.at[at, c], b_s.at[0, hf], b_r.at[0, hf], partner).start()

    def hand_b(hf):
        at = pl.ds(hf * hg, hg)
        wait(bb1.at[at, c], b_r.at[1, hf])
        rc(bb1.at[at, c], bb1.at[at, c], b_s.at[2, hf], b_r.at[2, hf], partner).start()

    def ffn(own_seq, i):
        b_ref, d_ref, count = (bb0, dd0, length) if own_seq else (bb1, dd1, other_length)
        base = 0 if own_seq else seq_len
        b = b_ref[blk(i)].reshape(ROWS, dim)
        d = d_ref[blk(i)].reshape(ROWS, dim)
        w_g, w_u, w_d = (w_f[m].reshape(dim, fq) for m in range(3))
        gate = mm(NN, b, w_g)
        up = mm(NN, b, w_u)
        dh = mm(NN, d, w_d)
        sg = jax.nn.sigmoid(gate)
        silu = gate * sg
        hid = (silu * up).astype(BF)
        dgate = (dh * up * sg * (1.0 + gate * (1.0 - sg))).astype(BF)
        dup = (dh * silu).astype(BF)
        at = pl.ds(pl.multiple_of(base + i * ROWS, ROWS), ROWS)
        act[at, 0:fq] = dgate
        act[at, fq : 2 * fq] = dup
        act[at, 2 * fq : 3 * fq] = hid
        u = (mm(NT, dgate, w_g) + mm(NT, dup, w_u)).reshape(ROWS // 64, 2, 32, dim)
        n = i if own_seq else i + nrb
        uacc[blk(i), 0 if own_seq else 1] = jnp.where(c == 0, u[:, 0], u[:, 1])

        @pl.when(n >= 2)
        def _():
            wait(usend.at[0], us_s.at[n - 2])

        ring = n % 2
        usend[ring] = jnp.where(c == 0, u[:, 1], u[:, 0]).astype(BF)
        part = pl.ds(n * (ROWS // 64), ROWS // 64)
        rc(usend.at[ring], urecv.at[part], us_s.at[n], us_r.at[n], partner).start()
        alive = i * ROWS + lax.broadcasted_iota(jnp.int32, (ROWS, 1), 0) < count
        out = jnp.where(alive, mm(NT, hid, w_d), 0.0).reshape(ROWS // 64, 2, 32, dim)

        @pl.when(home if own_seq else away)
        def _():
            facc[blk(i)] = out

        @pl.when(away if own_seq else home)
        def _():
            @pl.when(i >= 2)
            def _():
                wait(fsend.at[0], fs_s.at[i - 2])

            slot_now = i % 2
            if own_seq:
                x1 = x1b[blk(i)]
                fsend[slot_now, :, 0] = (out[:, 0] + jnp.where(c == 0, x1, 0.0)).astype(BF)
                fsend[slot_now, :, 1] = (out[:, 1] + jnp.where(c == 1, x1, 0.0)).astype(BF)
            else:
                fsend[slot_now] = out.astype(BF)
            rc(fsend.at[slot_now], frecv.at[blk(i)], fs_s.at[i], fs_r.at[i], partner).start()

    settle_dy()
    for m in range(3):
        agf2(m)
    for hf in range(2):
        wait(bb0.at[pl.ds(hf * hg, hg), oth], b_r.at[0, hf])

    def ffn_own(i, _):
        ffn(True, i)

        @pl.when(i == nrb - 2)
        def _():
            hand_b(0)

        return 0

    lax.fori_loop(0, nrb, ffn_own, 0)
    hand_b(1)

    per = ROWS // 64

    def join_u(i):
        at = pl.ds((nrb + i) * per, per)
        wait(urecv.at[at], us_r.at[nrb + i])
        sb1[pl.ds(i * per, per)] = (uacc[blk(i), 1] + urecv[at].astype(F32)).astype(BF)
        at = pl.ds(i * per, per)
        rc(sb1.at[at], rb1.at[at], uy_s.at[0, i], uy_r.at[0, i], ynbr).start()

    def ffn_other(i, _):
        for hf in range(2):

            @pl.when(i == hf * nrb // 2)
            def _():
                wait(bb1.at[pl.ds(hf * hg, hg), oth], b_r.at[2, hf])

        ffn(False, i)

        @pl.when(i >= 1)
        def _():
            join_u(i - 1)

        return 0

    wait(sb1, ex_s.at[2])
    lax.fori_loop(0, nrb, ffn_other, 0)
    join_u(nrb - 1)

    for i in range(nrb):
        wait(frecv.at[blk(i)], fs_r.at[i])

    def join_out(i, _):
        sb2[i] = (facc[i, yb] + frecv[i, yb].astype(F32)).astype(BF)
        mine = facc[i, y] + frecv[i, y].astype(F32)
        own[i] = mine + jnp.where(home, x1b[i], 0.0)
        return 0

    lax.fori_loop(0, groups, join_out, 0)
    rc(sb2, rb2, uy_s.at[1, 0], uy_r.at[1, 0], ynbr).start()

    def weight_grad(m, refs, first):
        agf_done(m)
        rows_half = half // 64

        def one_half(part, _):
            feats = pl.ds(pl.multiple_of(part * half, 128), half)
            t = None
            for n, ref in enumerate(refs):
                left = ref[:, :, :, feats].reshape(seq_len, half)
                term = mm(TN, left, act[n * seq_len : (n + 1) * seq_len, first : first + fq])
                t = term if t is None else t + term
            facc[pl.ds(part * rows_half, rows_half), :, :, 0:fq] = t.reshape(rows_half, 2, 32, fq)
            return 0

        lax.fori_loop(0, 2, one_half, 0)
        for part in range(2):
            zs = slice(part * nz // 2, (part + 1) * nz // 2)
            t = facc[part * rows_half : (part + 1) * rows_half, :, :, 0:fq].reshape(half, fq)
            w_f[m, zs] = t.astype(BF).reshape(nz // 2, 2, 2, nrow, fq)
        rsf0(m)

    weight_grad(0, (bb0, bb1), 0)
    weight_grad(1, (bb0, bb1), fq)
    pl.semaphore_signal(free, inc=1, device_id=partner, device_id_type=MESH)
    weight_grad(2, (dd0, dd1), 2 * fq)
    rsf1(0)
    for i in range(nrb):
        at = pl.ds(i * per, per)
        wait(urecv.at[at], us_r.at[i])

    @pl.when(home)
    def _():
        wait(xs.at[pl.ds(0, groups - 1)], a2a_s)

    @pl.when(away)
    def _():
        wait(xs, a2a_s)

    for hf in range(2):
        at = pl.ds(hf * hg, hg)
        wait(bb0.at[at, c], b_s.at[0, hf])
        wait(bb0.at[at, c], b_s.at[1, hf])
    for i in range(nrb):
        wait(rb1.at[pl.ds(i * per, per)], uy_r.at[0, i])

    def norm_three(i, _):
        alive = live_at(i)
        x1 = x1b[i]
        r = rb[i][:, 64:65]
        n = x1 * r
        u = uacc[i, 0] + urecv[i].astype(F32) + rb1[i].astype(F32)
        dx1 = dybuf[i].astype(F32) + r * (u - n * mean(u * n))
        bb0[i, c] = jnp.where(alive, dx1, 0.0).astype(BF)
        x1b[i] = dx1
        return 0

    lax.fori_loop(0, groups, norm_three, 0, unroll=2)
    pl.semaphore_wait(free, 1)
    swap_start(6, bb0.at[:, c], bb0.at[:, c])

    def turn_k(i, _):
        at = pl.ds(pl.multiple_of(i * ROWS, ROWS), ROWS)
        t = kb[blk(i)].reshape(ROWS, pw).T
        for h in range(pw // 64):
            for part in range(2):
                first = (h // 4) * 256 + part * 128 + (h % 4) * 32
                vt[h * 64 + part * 32 : h * 64 + part * 32 + 32, at] = t[first : first + 32]
        return 0

    lax.fori_loop(0, nrb, turn_k, 0)
    heads16 = lax.broadcasted_iota(jnp.int32, (16, pw), 0)
    pick = jnp.where(
        (lax.broadcasted_iota(jnp.int32, (16, pw), 1) >> 6) == heads16, 1.0, 0.0
    ).astype(BF)
    wait(bb0.at[:, oth], ex_r.at[6])

    for hf in range(2):
        wait(bb1.at[pl.ds(hf * hg, hg), c], b_s.at[2, hf])

    def out_back(i, _):
        at = pl.ds(pl.multiple_of(i * ROWS, ROWS), ROWS)
        t = mm(NN, bb0[blk(i)].reshape(ROWS, dim), wop[...]).astype(BF)
        bb1[blk(i), :, :, 0:pw] = t.reshape(ROWS // 64, 2, 32, pw)
        prod = t.astype(F32) * ob[blk(i)].reshape(ROWS, pw).astype(F32)
        delta[:, at] = mm(NT, pick, prod.astype(BF))
        return 0

    lax.fori_loop(0, nrb, out_back, 0)
    ag_done(3)
    for m in range(2):
        left = bb0[:, :, :, m * half : (m + 1) * half].reshape(seq_len, half)
        t = mm(TN, left, ob[...].reshape(seq_len, pw)).astype(BF)
        zs = slice(m * nz // 2, (m + 1) * nz // 2)
        w_a[3, zs] = mm(NT, t, ev[...]).astype(BF).reshape(nz // 2, 2, 2, nrow, hw)
    rs0(3)

    def attend_back(i):
        keys = (i + 1) * ROWS

        def group(g, _):
            lanes = pl.ds(pl.multiple_of(g * 256, 256), 256)
            q = rows_of(qb, i * ROWS, ROWS, lanes)
            d = rows_of(bb1, i * ROWS, ROWS, lanes)
            for hh in range(4):
                qm = jnp.where(((lane >> 5) & 3) == hh, q, jnp.zeros_like(q))
                dm = jnp.where((lane >> 6) == hh, d, jnp.zeros_like(d))
                row_lse = lse[pl.ds(g * 4 + hh, 1), i * ROWS : keys]
                row_delta = delta[pl.ds(g * 4 + hh, 1), i * ROWS : keys]

                def part(first, count, masked):
                    s = mm(NT, rows_of(kb, first, count, lanes), qm)
                    if masked:
                        s = jnp.where(diag, s, -1e30)
                    p = jnp.exp2(s - row_lse)
                    dp_ = mm(NT, rows_of(vb, first, count, lanes), dm)
                    ds = (p * (dp_ - row_delta)).astype(BF)
                    at = pl.ds(first // 64, count // 64)
                    dv_part = mm(NN, p.astype(BF), dm).reshape(count // 64, 2, 32, 256)
                    dk_part = mm(NN, ds, qm).reshape(count // 64, 2, 32, 256)
                    if masked and hh == 0:
                        uacc[at, :, :, lanes] = dv_part
                        facc[at, :, :, lanes] = dk_part
                    else:
                        uacc[at, :, :, lanes] += dv_part
                        facc[at, :, :, lanes] += dk_part
                    return ds

                ds = part(i * ROWS, ROWS, True)
                if i:
                    ds = jnp.concatenate([part(0, i * ROWS, False), ds], axis=0)
                hs = pl.multiple_of(g * 256 + hh * 64, 64)
                t = mm(NN, vt[pl.ds(hs, 64), 0:keys], ds) * score_scale
                c_now, s_now = ct[:, i * ROWS : keys], st[:, i * ROWS : keys]
                f1, f2 = t[0:32], t[32:64]
                hs = pl.multiple_of(g * 256 + hh * 32, 32)
                ot[pl.ds(hs, 32), i * ROWS : keys] = (f1 * c_now + f2 * s_now).astype(BF)
                ot[pl.ds(hs + 128, 32), i * ROWS : keys] = (f2 * c_now - f1 * s_now).astype(BF)
            return 0

        lax.fori_loop(0, pw // 256, group, 0)

    def back_zero():
        rsf1(1)

    def back_one():
        rsf1(2)

    def back_two():
        rs1(3)

    with_steps(
        attend_back,
        ((0, back_zero), (1, back_one), (2, back_two)),
    )

    def turn_back(i, _):
        at = pl.ds(pl.multiple_of(i * ROWS, ROWS), ROWS)
        qb[blk(i)] = ot[:, at].T.reshape(ROWS // 64, 2, 32, pw)
        vb[blk(i)] = uacc[blk(i), :, :, 0:pw].astype(BF)
        cos, sin = cosb[at, :], sinb[at, :]
        for g in range(pw // 256):
            f1 = facc[blk(i), :, :, g * 256 : g * 256 + 128].reshape(ROWS, 128)
            f2 = facc[blk(i), :, :, g * 256 + 128 : g * 256 + 256].reshape(ROWS, 128)
            kb[blk(i), :, :, g * 256 : g * 256 + 128] = (
                ((f1 * cos + f2 * sin) * (1.0 / LOG2E)).astype(BF).reshape(ROWS // 64, 2, 32, 128)
            )
            kb[blk(i), :, :, g * 256 + 128 : g * 256 + 256] = (
                ((f2 * cos - f1 * sin) * (1.0 / LOG2E)).astype(BF).reshape(ROWS // 64, 2, 32, 128)
            )
        return 0

    lax.fori_loop(0, nrb, turn_back, 0)
    for t, (src, e) in enumerate(((qb, eqk), (kb, eqk), (vb, ev))):
        ag_done(t)
        for m in range(2):
            left = abuf[:, :, :, m * half : (m + 1) * half].reshape(seq_len, half)
            part = mm(TN, left, src[...].reshape(seq_len, pw)).astype(BF)
            zs = slice(m * nz // 2, (m + 1) * nz // 2)
            w_a[t, zs] = mm(NT, part, e[...]).astype(BF).reshape(nz // 2, 2, 2, nrow, hw)
        rs0(t)
    for hf in range(2):
        for i in range(hf * nrb // 2, (hf + 1) * nrb // 2):
            wait(sb1.at[pl.ds(i * per, per)], uy_s.at[0, i])

    wait(rb2, uy_r.at[1, 0])

    def finish_out(i, _):
        sb2[i] = (own[i] + rb2[i].astype(F32)).astype(BF)
        return 0

    wait(sb2, uy_s.at[1, 0])
    lax.fori_loop(0, groups, finish_out, 0)
    pltpu.make_async_copy(sb2, lo_ref, lo_r).start()

    def da_rows(at, which):
        total = None
        for t, src in enumerate((qb, kb, vb)):
            term = mm(NT, src[at, which].reshape(ROWS, pw), wp[:, t * pw : (t + 1) * pw])
            total = term if total is None else total + term
        return total.reshape(half_rows, 32, dim)

    def da_other(j, _):
        at = pl.ds(j * half_rows, half_rows)
        sb1[at] = da_rows(at, oth).astype(BF)
        return 0

    def da_own(j, _):
        at = pl.ds(j * half_rows, half_rows)
        own[at] = da_rows(at, c)
        return 0

    lax.fori_loop(0, groups // half_rows, da_other, 0)
    swap_start(7, sb1, rb1)
    lax.fori_loop(0, groups // half_rows, da_own, 0)
    rs2(3)

    wait(rb1, ex_r.at[7])

    def norm_four(i, _):
        rows_now = xbuf[i].astype(F32)
        r = rb[i][:, 0:1]
        n = rows_now * r
        u = own[i] + rb1[i].astype(F32)
        dx = x1b[i] + r * (u - n * mean(u * n))
        xs[i] = dx.astype(BF)
        same = (i == dp) & (c == y)

        @pl.when(same)
        def _():
            pltpu.make_async_copy(xs.at[i], ret.at[slot], ret_r).start()

        @pl.when(jnp.logical_not(same))
        def _():
            rc(xs.at[i], ret.at[slot], ret_s, ret_r, (i, c)).start()

        return 0

    lax.fori_loop(0, groups, norm_four, 0)
    for i in range(3):
        rs1(i)
    for i in range(3):
        rs2(i)

    d_g, d_u = rsf3(0), rsf3(1)
    dg_out[...] = d_g * gain2
    du_out[...] = d_u * gain2
    both = d_g * wg[...].astype(F32) + d_u * wu[...].astype(F32)
    sums2 = jnp.sum(both, axis=1, keepdims=True)
    dd_out[...] = rsf3(2)
    do_out[...] = rs3(3)
    sums1 = jnp.zeros((nrow, 1), F32)
    for i, (w, out) in enumerate(((wq, dq_out), (wk, dk_out), (wv, dv_out))):
        part = rs3(i)
        out[...] = part * gain1
        sums1 = sums1 + jnp.sum(part * w[...].astype(F32), axis=1, keepdims=True)
    first_half = lax.broadcasted_iota(jnp.int32, (nrow, 128), 1) < 64
    gs[...] = jnp.where(first_half, sums1, sums2)
    rc(gs, gr, gg_s, gg_r, ynbr).start()

    wait(ret, ret_r)

    def restore(s, _):
        def find(j, at):
            return jnp.where(deal[j] == s, j, at)

        sb2[s] = ret[lax.fori_loop(0, groups, find, 0)]
        return 0

    wait(sb2, lo_r)
    lax.fori_loop(0, groups, restore, 0)
    give = pltpu.make_async_copy(sb2, gi_ref, lo_r)
    give.start()
    wait(gr, gg_r)
    both = gs[...] + gr[...]
    dg1_out[...] = jnp.sum(jnp.where(on_diag, both[:, 0:1], 0.0), axis=0, keepdims=True)
    dg2_out[...] = jnp.sum(jnp.where(on_diag, both[:, 64:65], 0.0), axis=0, keepdims=True)

    wait(gs, gg_s)
    for m in range(3):
        rsf_done(m)
    for i in range(4):
        rs_done(i)

    wait(dybuf, dy_s.at[0])
    give.wait()
    @pl.when(home)
    def _():
        wait(xs.at[pl.ds(0, groups - 1)], ret_s)

    @pl.when(away)
    def _():
        wait(xs, ret_s)

    wait(abuf.at[:, c], ex_s.at[0])
    for i in range(2):
        wait(usend.at[i], us_s.at[2 * nrb - 2 + i])
        wait(fsend.at[i], fs_s.at[nrb - 2 + i])
    wait(bb0.at[:, c], ex_s.at[6])
    wait(sb1, ex_s.at[7])


def rotary_tables(count):
    lanes = np.arange(128) % 32
    frequency = np.where(lanes < HD // 2, BASE ** (-2.0 * lanes / HD), 0.0)
    high = np.zeros((32, 128))
    high[:count] = 32.0 * np.arange(count)[:, None] * frequency[None, :]
    low = np.arange(32)[:, None] * frequency[None, :]
    return np.stack([np.cos(high), np.sin(high), np.cos(low), np.sin(low)]).astype(np.float32)


def fused_body(
    x_given, dealing, seq_lengths, first_gain, query_weight, key_weight, value_weight,
    output_weight, second_gain, gate_weight, up_weight, down_weight, grad_output,
):
    groups, piece_rows, dim = x_given.shape
    hw = query_weight.shape[1]
    local_hidden = gate_weight.shape[1]
    fq = local_hidden // 2
    nz = groups // 4
    rows = query_weight.shape[0]
    pw = hw // HD * 64
    seq_len = groups * 64
    vm, anym, sm = (
        pl.BlockSpec(memory_space=pltpu.VMEM),
        pl.BlockSpec(memory_space=pl.ANY),
        pl.BlockSpec(memory_space=pltpu.SMEM),
    )
    blocks = (groups, piece_rows, dim)
    pairs = (groups, 2, piece_rows)

    def gathered(width, lead=()):
        return pltpu.VMEM(lead + (nz, 2, 2, rows, width), BF)

    kd = nz // 2

    def landing(width, lead=()):
        return [
            pltpu.VMEM(lead + (nz, 2, rows, width), BF),
            pltpu.VMEM(lead + (kd, 2, 2, rows, width), BF),
            pltpu.VMEM(lead + (nz - kd, 2, rows, width), BF),
            pltpu.VMEM(lead + (nz, rows, width), BF),
        ]

    nrb = seq_len // ROWS
    dma = pltpu.SemaphoreType.DMA
    scratch = (
        [pltpu.VMEM(blocks, BF)] * 3
        + [pltpu.VMEM((3, rows, hw), BF), pltpu.VMEM((2, rows, local_hidden), BF)]
        + [gathered(hw, (4,)), gathered(fq, (3,))]
        + [pltpu.VMEM((dim, 3 * pw), BF), pltpu.VMEM((dim, pw), BF)]
        + [pltpu.VMEM((hw, pw), BF)] * 2
        + [pltpu.VMEM((seq_len, 128), F32)] * 2
        + [pltpu.VMEM((32, seq_len), F32)] * 2
        + [pltpu.VMEM(pairs + (dim,), BF)]
        + [pltpu.VMEM(pairs + (pw,), BF)] * 3
        + [pltpu.VMEM((pw, seq_len), BF)] * 2
        + [pltpu.VMEM(pairs + (pw,), BF)]
        + [pltpu.VMEM((8, seq_len), F32)]
        + [pltpu.VMEM(blocks, F32)]
        + [pltpu.VMEM(blocks, BF)] * 4
        + [pltpu.VMEM(blocks, F32)]
        + [pltpu.VMEM((groups, piece_rows, 128), F32)]
        + [pltpu.VMEM(pairs + (dim,), BF)] * 4
        + [pltpu.VMEM(pairs + (dim,), F32)] * 2
        + [pltpu.VMEM((2 * seq_len, 3 * fq), BF)]
        + [pltpu.VMEM((16, seq_len), F32)]
        + [pltpu.VMEM((2 * groups, piece_rows, dim), BF), pltpu.VMEM(pairs + (dim,), BF)]
        + [pltpu.VMEM((2, ROWS // 64, piece_rows, dim), BF)]
        + [pltpu.VMEM((2, ROWS // 64, 2, piece_rows, dim), BF)]
        + landing(hw, (4,))
        + [pltpu.VMEM((3, nz, 2, rows, fq), BF)] * 2
        + [pltpu.VMEM(blocks, BF)]
        + [pltpu.VMEM((rows, 128), F32)] * 2
        + [dma(()), dma(()), dma((1,)), dma((2,))]
        + [dma((4,)), dma((4,)), dma((4,)), dma((4, 2)), dma((4, nz + 3))]
        + [dma((4, 2)), dma((4, 2)), dma((4,)), dma((4, 2 * nz + 2))]
        + [dma((3,)), dma((3,)), dma((3,)), dma((3, 2 * nz + 2))]
        + [dma((3,)), dma((3,)), dma((3, 2 * nz + 1))]
        + [dma((8,)), dma((8,)), dma((3, 2)), dma((3, 2))]
        + [dma((2 * nrb,)), dma((2 * nrb,)), dma((nrb,)), dma((nrb,))]
        + [dma((2, nrb)), dma((2, nrb)), dma(())]
        + [dma(())] * 4
        + [pltpu.SemaphoreType.REGULAR]
    )
    small = jax.ShapeDtypeStruct((rows, hw), F32)
    wide = jax.ShapeDtypeStruct((rows, local_hidden), F32)
    piece = jax.ShapeDtypeStruct(blocks, BF)
    outs = pl.pallas_call(
        functools.partial(fused_kernel, (nz, dim, hw, fq, rows)),
        out_shape=[piece, piece, small, small, small, small, wide, wide, wide]
        + [jax.ShapeDtypeStruct((1, rows), F32)] * 2,
        in_specs=[sm, sm, anym, anym] + [vm] * 10,
        out_specs=[anym] * 2 + [vm] * 9,
        scratch_shapes=scratch,
        compiler_params=pltpu.CompilerParams(
            collective_id=0, has_side_effects=True, vmem_limit_bytes=VMEM_LIMIT
        ),
        name="layer",
    )(
        dealing, seq_lengths, x_given, grad_output.reshape(blocks),
        first_gain.reshape(1, rows), second_gain.reshape(1, rows),
        query_weight, key_weight, value_weight, output_weight, gate_weight, up_weight, down_weight,
        rotary_tables(seq_len // 32),
    )
    outs = pl.pallas_call(
        pass_on,
        out_shape=[jax.ShapeDtypeStruct(o.shape, o.dtype) for o in outs],
        in_specs=[vm] * len(outs),
        out_specs=[vm] * len(outs),
        name="results",
    )(*outs)
    layer_out, grad_in, gq, gk, gv, go, gg, gu, gd, gain_one, gain_two = outs
    return (
        layer_out.reshape(grad_output.shape), grad_in, gain_one.reshape(rows), gq, gk, gv, go,
        gain_two.reshape(rows), gg, gu, gd,
    )


def pass_on(*refs):
    count = len(refs) // 2
    for i in range(count):
        refs[count + i][...] = refs[i][...]


def fits_fused(mesh):
    return mesh.shape["tensor"] == 2 and mesh.shape["dp"] % 8 == 0


def solution(mesh):
    placed = (
        P(None, ("dp", "tensor"), None),
        P(),
        P(),
        P("dp"),
        P("dp", "tensor"),
        P("dp", "tensor"),
        P("dp", "tensor"),
        P("dp", "tensor"),
        P("dp"),
        P("dp", "tensor"),
        P("dp", "tensor"),
        P("dp", "tensor"),
        P("dp", None, "tensor", None, None),
    )
    return jax.shard_map(
        fused_body if fits_fused(mesh) else body,
        mesh=mesh,
        in_specs=placed,
        out_specs=(
            P("dp", None, "tensor", None, None),
            P(None, ("dp", "tensor"), None),
            P("dp"),
            P("dp", "tensor"),
            P("dp", "tensor"),
            P("dp", "tensor"),
            P("dp", "tensor"),
            P("dp"),
            P("dp", "tensor"),
            P("dp", "tensor"),
            P("dp", "tensor"),
        ),
        check_vma=False,
    )
```

```python
import functools

import jax
import jax.numpy as jnp
import numpy as np
from jax import lax
from jax.experimental import pallas as pl
from jax.experimental.pallas import tpu as pltpu
from jax.sharding import PartitionSpec as P

HD = 48


EPS = 1e-05
BASE = 10000.0
VMEM_LIMIT = 64 * 1024 * 1024 - 65536


def tables(positions, head_size):
    freq_index = jnp.arange(head_size // 2, dtype=jnp.float32)
    frequency = BASE ** (-2.0 * freq_index / head_size)
    angles = positions[:, None] * frequency[None, :]
    return (jnp.cos(angles)[:, None, :], jnp.sin(angles)[:, None, :])


def rotary(values, cosine, sine_table):
    half_width = values.shape[-1] // 2
    first_half = values[..., :half_width]
    second_half = values[..., half_width:]
    return jnp.concatenate(
        [
            first_half * cosine - second_half * sine_table,
            second_half * cosine + first_half * sine_table,
        ],
        axis=-1,
    )


def rotary_back(values, cosine, sine_table):
    half_width = values.shape[-1] // 2
    first_half = values[..., :half_width]
    second_half = values[..., half_width:]
    return jnp.concatenate(
        [
            first_half * cosine + second_half * sine_table,
            second_half * cosine - first_half * sine_table,
        ],
        axis=-1,
    )


def row_dot(left_side, right_side):
    return jnp.dot(left_side, right_side, preferred_element_type=jnp.float32)


def dot_trans(left_side, right_side):
    return lax.dot_general(
        left_side, right_side, (((1,), (1,)), ((), ())), preferred_element_type=jnp.float32
    )


def dot_first(left_side, right_side):
    return lax.dot_general(
        left_side, right_side, (((0,), (0,)), ((), ())), preferred_element_type=jnp.float32
    )


def tensor_major(values, groups, pieces, piece_rows):
    columns = values.shape[1]
    return (
        values.reshape(groups, pieces, piece_rows, columns)
        .transpose(1, 0, 2, 3)
        .reshape(groups * pieces * piece_rows, columns)
    )


def rms_back(grad_normed, x_rows, scale_rows, gain):
    normed = x_rows * scale_rows
    weighted = grad_normed * gain
    x_grad = scale_rows * (weighted - normed * jnp.mean(weighted * normed, axis=-1, keepdims=True))
    return (x_grad, jnp.sum(grad_normed * normed, axis=0))


def block_scores(queries, key_rows, query_start, key_start, block_rows, score_scale):
    query_part = lax.dynamic_slice_in_dim(queries, query_start, block_rows, 0)
    key_part = lax.dynamic_slice_in_dim(key_rows, key_start, block_rows, 0)
    scores = (
        jnp.einsum("qhd,khd->hqk", query_part, key_part, preferred_element_type=jnp.float32)
        * score_scale
    )
    row_offsets = jnp.arange(block_rows)
    allowed = (key_start + row_offsets)[None, :] <= (query_start + row_offsets)[:, None]
    return jnp.where(allowed[None], scores, -1e30)


def attend_forward(queries, key_rows, value_rows, live_blocks, block_rows, score_scale):
    seq_len, heads, head_size = queries.shape

    def one_block(query_index, state_now):
        outputs, log_sums = state_now
        query_start = query_index * block_rows

        def stats(key_index, carried):
            running, exp_total = carried
            scores = block_scores(
                queries, key_rows, query_start, key_index * block_rows, block_rows, score_scale
            )
            newest = jnp.maximum(running, jnp.max(scores, axis=-1))
            exp_total = exp_total * jnp.exp(running - newest) + jnp.sum(
                jnp.exp(scores - newest[..., None]), axis=-1
            )
            return (newest, exp_total)

        initial = (
            jnp.full((heads, block_rows), -1e30, jnp.float32),
            jnp.zeros((heads, block_rows), jnp.float32),
        )
        running, exp_total = lax.fori_loop(0, query_index + 1, stats, initial)
        log_sum = running + jnp.log(exp_total)

        def accumulate(key_index, accumulated):
            key_start = key_index * block_rows
            scores = block_scores(
                queries, key_rows, query_start, key_start, block_rows, score_scale
            )
            prob_low = jnp.exp(scores - log_sum[..., None]).astype(jnp.bfloat16)
            value_part = lax.dynamic_slice_in_dim(value_rows, key_start, block_rows, 0)
            return accumulated + jnp.einsum(
                "hqk,khd->qhd", prob_low, value_part, preferred_element_type=jnp.float32
            )

        result = lax.fori_loop(
            0, query_index + 1, accumulate, jnp.zeros((block_rows, heads, head_size), jnp.float32)
        )
        outputs = lax.dynamic_update_slice_in_dim(outputs, result, query_start, 0)
        log_sums = lax.dynamic_update_slice_in_dim(log_sums, log_sum, query_start, 1)
        return (outputs, log_sums)

    initial = (
        jnp.zeros((seq_len, heads, head_size), jnp.float32),
        jnp.zeros((heads, seq_len), jnp.float32),
    )
    return lax.fori_loop(0, live_blocks, one_block, initial)


def attend_backward(
    queries, key_rows, value_rows, outputs, log_sums, out_grad, live_blocks, block_rows, score_scale
):
    seq_len, heads, head_size = queries.shape
    row_delta = jnp.einsum("qhd,qhd->hq", out_grad.astype(jnp.float32), outputs)

    def one_block(query_index, state_now):
        query_grads, key_grads, value_grads = state_now
        query_start = query_index * block_rows
        query_part = lax.dynamic_slice_in_dim(queries, query_start, block_rows, 0)
        grad_part = lax.dynamic_slice_in_dim(out_grad, query_start, block_rows, 0)
        logsum_part = lax.dynamic_slice_in_dim(log_sums, query_start, block_rows, 1)
        delta_part = lax.dynamic_slice_in_dim(row_delta, query_start, block_rows, 1)

        def inner(key_index, carried):
            query_acc, key_grads, value_grads = carried
            key_start = key_index * block_rows
            key_part = lax.dynamic_slice_in_dim(key_rows, key_start, block_rows, 0)
            value_part = lax.dynamic_slice_in_dim(value_rows, key_start, block_rows, 0)
            scores = block_scores(
                queries, key_rows, query_start, key_start, block_rows, score_scale
            )
            prob_soft = jnp.exp(scores - logsum_part[..., None])
            prob_low = prob_soft.astype(jnp.bfloat16)
            prob_grad = jnp.einsum(
                "qhd,khd->hqk", grad_part, value_part, preferred_element_type=jnp.float32
            )
            score_grad = (prob_soft * (prob_grad - delta_part[..., None])).astype(jnp.bfloat16)
            query_acc = (
                query_acc
                + jnp.einsum(
                    "hqk,khd->qhd", score_grad, key_part, preferred_element_type=jnp.float32
                )
                * score_scale
            )
            key_new = (
                jnp.einsum(
                    "hqk,qhd->khd", score_grad, query_part, preferred_element_type=jnp.float32
                )
                * score_scale
            )
            value_new = jnp.einsum(
                "hqk,qhd->khd", prob_low, grad_part, preferred_element_type=jnp.float32
            )
            key_old = lax.dynamic_slice_in_dim(key_grads, key_start, block_rows, 0)
            value_old = lax.dynamic_slice_in_dim(value_grads, key_start, block_rows, 0)
            key_grads = lax.dynamic_update_slice_in_dim(key_grads, key_old + key_new, key_start, 0)
            value_grads = lax.dynamic_update_slice_in_dim(
                value_grads, value_old + value_new, key_start, 0
            )
            return (query_acc, key_grads, value_grads)

        initial = (jnp.zeros((block_rows, heads, head_size), jnp.float32), key_grads, value_grads)
        query_acc, key_grads, value_grads = lax.fori_loop(0, query_index + 1, inner, initial)
        query_grads = lax.dynamic_update_slice_in_dim(query_grads, query_acc, query_start, 0)
        return (query_grads, key_grads, value_grads)

    zero_grads = jnp.zeros((seq_len, heads, head_size), jnp.float32)
    return lax.fori_loop(0, live_blocks, one_block, (zero_grads, zero_grads, zero_grads))


def body(
    x_given,
    dealing,
    seq_lengths,
    first_gain,
    query_weight,
    key_weight,
    value_weight,
    output_weight,
    second_gain,
    gate_weight,
    up_weight,
    down_weight,
    grad_output,
):
    groups = lax.axis_size("dp")
    pieces = lax.axis_size("tensor")
    group_index = lax.axis_index("dp")
    piece_index = lax.axis_index("tensor")
    seq_count, piece_rows, features = x_given.shape
    tokens = groups * piece_rows
    seq_len = tokens * pieces
    head_width = query_weight.shape[1]
    heads_local = head_width // HD
    block_rows = min(512, seq_len)
    score_scale = HD ** (-0.5)
    sequence = dealing[group_index]
    length = seq_lengths[sequence]
    live_blocks = (length + block_rows - 1) // block_rows
    outgoing = jnp.take(x_given, dealing, axis=0)
    arrived = lax.all_to_all(outgoing, "dp", split_axis=0, concat_axis=1, tiled=True)
    x_rows = arrived.reshape(tokens, features).astype(jnp.float32)
    row_ids = jnp.arange(tokens)
    positions_local = (
        row_ids // piece_rows * pieces + piece_index
    ) * piece_rows + row_ids % piece_rows
    live_rows = (positions_local < length).astype(jnp.float32)[:, None]
    columns = (
        lax.all_gather(gate_weight, "tensor", axis=1, tiled=True),
        lax.all_gather(up_weight, "tensor", axis=1, tiled=True),
        lax.all_gather(down_weight, "tensor", axis=1, tiled=True),
    )
    gathered = (
        lax.all_gather(first_gain, "dp", axis=0, tiled=True),
        lax.all_gather(second_gain, "dp", axis=0, tiled=True),
        lax.all_gather(query_weight, "dp", axis=0, tiled=True),
        lax.all_gather(key_weight, "dp", axis=0, tiled=True),
        lax.all_gather(value_weight, "dp", axis=0, tiled=True),
        lax.all_gather(output_weight, "dp", axis=0, tiled=True),
        lax.all_gather(columns[0], "dp", axis=0, tiled=True),
        lax.all_gather(columns[1], "dp", axis=0, tiled=True),
        lax.all_gather(columns[2], "dp", axis=0, tiled=True),
    )
    (
        gain_one,
        gain_two,
        query_full,
        key_full,
        value_full,
        out_full,
        gate_full,
        up_full,
        down_full,
    ) = gathered
    qkv_weight = jnp.concatenate([query_full, key_full, value_full], axis=1)
    scale_one = lax.rsqrt(jnp.mean(x_rows * x_rows, axis=-1, keepdims=True) + EPS)
    normed = (x_rows * scale_one * gain_one).astype(jnp.bfloat16)
    normed_full = lax.all_gather(
        normed.reshape(groups, 1, piece_rows, features), "tensor", axis=1, tiled=True
    ).reshape(seq_len, features)
    projected = row_dot(normed_full, qkv_weight)
    cosine, sine_table = tables(jnp.arange(seq_len, dtype=jnp.float32), HD)
    queries = rotary(
        projected[:, :head_width].reshape(seq_len, heads_local, HD), cosine, sine_table
    ).astype(jnp.bfloat16)
    key_rows = rotary(
        projected[:, head_width : 2 * head_width].reshape(seq_len, heads_local, HD),
        cosine,
        sine_table,
    ).astype(jnp.bfloat16)
    value_rows = (
        projected[:, 2 * head_width :].astype(jnp.bfloat16).reshape(seq_len, heads_local, HD)
    )
    mixed, log_sums = attend_forward(
        queries, key_rows, value_rows, live_blocks, block_rows, score_scale
    )
    mixed_low = mixed.reshape(seq_len, head_width).astype(jnp.bfloat16)
    mixed_major = tensor_major(mixed_low, groups, pieces, piece_rows)
    attention = lax.psum_scatter(
        dot_trans(mixed_major, out_full).astype(jnp.bfloat16),
        "tensor",
        scatter_dimension=0,
        tiled=True,
    ).astype(jnp.float32)
    hidden_one = x_rows + live_rows * attention
    scale_two = lax.rsqrt(jnp.mean(hidden_one * hidden_one, axis=-1, keepdims=True) + EPS)
    normed_two = (hidden_one * scale_two * gain_two).astype(jnp.bfloat16)
    gate_act = row_dot(normed_two, gate_full)
    up_act = row_dot(normed_two, up_full)
    sigmoid_act = jax.nn.sigmoid(gate_act)
    silu_act = gate_act * sigmoid_act
    hidden = (silu_act * up_act).astype(jnp.bfloat16)
    branch = dot_trans(hidden, down_full)
    result = hidden_one + live_rows * branch
    layer_out = result.astype(jnp.bfloat16).reshape(1, groups, 1, piece_rows, features)
    out_grad = grad_output.reshape(tokens, features).astype(jnp.float32)
    branch_grad = (live_rows * out_grad).astype(jnp.bfloat16)
    hidden_grad = row_dot(branch_grad, down_full)
    down_term = dot_first(branch_grad, hidden)
    gate_grad = (
        hidden_grad * up_act * sigmoid_act * (1.0 + gate_act * (1.0 - sigmoid_act))
    ).astype(jnp.bfloat16)
    up_grad = (hidden_grad * silu_act).astype(jnp.bfloat16)
    normed_two_grad = dot_trans(gate_grad, gate_full) + dot_trans(up_grad, up_full)
    gate_term = dot_first(normed_two, gate_grad)
    up_term = dot_first(normed_two, up_grad)
    hidden_one_grad, gain_two_term = rms_back(normed_two_grad, hidden_one, scale_two, gain_two)
    hidden_one_grad = hidden_one_grad + out_grad
    attention_grad = (live_rows * hidden_one_grad).astype(jnp.bfloat16)
    attention_full = lax.all_gather(
        attention_grad.reshape(groups, 1, piece_rows, features), "tensor", axis=1, tiled=True
    ).reshape(seq_len, features)
    mixed_grad = row_dot(attention_full, out_full).astype(jnp.bfloat16)
    out_term = dot_first(attention_full, mixed_low)
    query_grads, key_grads, value_grads = attend_backward(
        queries,
        key_rows,
        value_rows,
        mixed,
        log_sums,
        mixed_grad.reshape(seq_len, heads_local, HD),
        live_blocks,
        block_rows,
        score_scale,
    )
    query_back = (
        rotary_back(query_grads, cosine, sine_table)
        .reshape(seq_len, head_width)
        .astype(jnp.bfloat16)
    )
    key_back = (
        rotary_back(key_grads, cosine, sine_table).reshape(seq_len, head_width).astype(jnp.bfloat16)
    )
    value_back = value_grads.reshape(seq_len, head_width).astype(jnp.bfloat16)
    projected_grad = jnp.concatenate([query_back, key_back, value_back], axis=1)
    qkv_term = dot_first(normed_full, projected_grad)
    grad_major = tensor_major(projected_grad, groups, pieces, piece_rows)
    normed_grad = lax.psum_scatter(
        dot_trans(grad_major, qkv_weight).astype(jnp.bfloat16),
        "tensor",
        scatter_dimension=0,
        tiled=True,
    ).astype(jnp.float32)
    input_grad, gain_one_term = rms_back(normed_grad, x_rows, scale_one, gain_one)
    input_grad = input_grad + hidden_one_grad
    returned = lax.all_to_all(
        input_grad.astype(jnp.bfloat16).reshape(groups, piece_rows, features),
        "dp",
        split_axis=0,
        concat_axis=0,
        tiled=True,
    )
    grad_in = jnp.zeros_like(x_given).at[dealing].set(returned)
    gain_pair = jnp.stack([gain_one_term, gain_two_term], axis=1)
    query_term = qkv_term[:, :head_width]
    key_term = qkv_term[:, head_width : 2 * head_width]
    value_term = qkv_term[:, 2 * head_width :]
    summed = (
        lax.psum_scatter(
            gain_pair.astype(jnp.bfloat16), "dp", scatter_dimension=0, tiled=True
        ).astype(jnp.float32),
        lax.psum_scatter(
            query_term.astype(jnp.bfloat16), "dp", scatter_dimension=0, tiled=True
        ).astype(jnp.float32),
        lax.psum_scatter(
            key_term.astype(jnp.bfloat16), "dp", scatter_dimension=0, tiled=True
        ).astype(jnp.float32),
        lax.psum_scatter(
            value_term.astype(jnp.bfloat16), "dp", scatter_dimension=0, tiled=True
        ).astype(jnp.float32),
        lax.psum_scatter(
            out_term.astype(jnp.bfloat16), "dp", scatter_dimension=0, tiled=True
        ).astype(jnp.float32),
        lax.psum_scatter(
            gate_term.astype(jnp.bfloat16), "dp", scatter_dimension=0, tiled=True
        ).astype(jnp.float32),
        lax.psum_scatter(
            up_term.astype(jnp.bfloat16), "dp", scatter_dimension=0, tiled=True
        ).astype(jnp.float32),
        lax.psum_scatter(
            down_term.astype(jnp.bfloat16), "dp", scatter_dimension=0, tiled=True
        ).astype(jnp.float32),
    )
    across = (
        lax.psum_scatter(
            jnp.tile(summed[0], (1, pieces)).astype(jnp.bfloat16),
            "tensor",
            scatter_dimension=1,
            tiled=True,
        ).astype(jnp.float32),
        lax.psum_scatter(
            summed[5].astype(jnp.bfloat16), "tensor", scatter_dimension=1, tiled=True
        ).astype(jnp.float32),
        lax.psum_scatter(
            summed[6].astype(jnp.bfloat16), "tensor", scatter_dimension=1, tiled=True
        ).astype(jnp.float32),
        lax.psum_scatter(
            summed[7].astype(jnp.bfloat16), "tensor", scatter_dimension=1, tiled=True
        ).astype(jnp.float32),
    )
    gain_sums = across[0]
    query_sum, key_sum, value_sum, out_sum = (summed[1], summed[2], summed[3], summed[4])
    gate_sum, up_sum, down_sum = (across[1], across[2], across[3])
    return (
        layer_out,
        grad_in,
        gain_sums[:, 0],
        query_sum,
        key_sum,
        value_sum,
        out_sum,
        gain_sums[:, 1],
        gate_sum,
        up_sum,
        down_sum,
    )


MESH = pl.DeviceIdType.MESH
BF = jnp.bfloat16
F32 = jnp.float32
NN = (((1,), (0,)), ((), ()))
NT = (((1,), (1,)), ((), ()))
TN = (((0,), (0,)), ((), ()))
LOG2E = 1.4426950408889634
ROWS = 256


def mm(kind, left_side, right_side):
    return lax.dot_general(left_side, right_side, kind, preferred_element_type=F32)


def fused_kernel(
    shape,
    deal, lens, x_ref, dy_ref, g1, g2, wq, wk, wv, wo, wg, wu, wd, tab,
    lo_ref, gi_ref, dq_out, dk_out, dv_out, do_out, dg_out, du_out, dd_out, dg1_out, dg2_out,
    xs, xbuf, dybuf, src_a, src_f, w_a, w_f, wp, wop, eqk, ev, cosb, sinb, ct, st,
    abuf, qb, kb, vb, vt, ot, ob, lse, own, sb1, sb2, rb1, rb2, x1b, rb, bb0, bb1, dd0, dd1,
    facc, uacc, act, delta, urecv, frecv, usend, fsend,
    rx_a, ry_a, ry2_a, rz_a, rx_f, rz_f, ret, gs, gr,
    a2a_s, a2a_r, dy_s, dy_r, ag_z, ag_x, ag_y, ag_d, ag_s, rs_x, rs_y, rs_z, rs_s,
    agf_z, agf_f, agf_x, agf_s, rsf_x, rsf_z, rsf_s, ex_s, ex_r, b_s, b_r, us_s, us_r, fs_s, fs_r,
    uy_s, uy_r, lo_r, ret_s, ret_r, gg_s, gg_r, free,
):
    nz, dim, hw, fq, nrow = shape
    groups = 4 * nz
    seq_len = 64 * groups
    half = dim // 2
    nrb = seq_len // ROWS
    kd = nz // 2
    dp = lax.axis_index("dp")
    y = lax.axis_index("tensor")
    z = dp // 4
    x = (dp // 2) % 2
    c = dp % 2
    xb, yb, oth = 1 - x, 1 - y, 1 - c
    home = c == y
    away = c != y
    slot = (z * 2 + x) * 2 + y
    score_scale = HD ** (-0.5)

    def dev(z_, x_, c_, y_):
        return ((z_ * 2 + x_) * 2 + c_, y_)

    partner = dev(z, x, oth, y)
    xnbr = dev(z, xb, c, y)
    ynbr = dev(z, x, c, yb)
    other_slot = (z * 2 + x) * 2 + yb

    def rc(src, dst, ss, rs, to):
        return pltpu.make_async_remote_copy(
            src_ref=src, dst_ref=dst, send_sem=ss, recv_sem=rs, device_id=to, device_id_type=MESH
        )

    def wait(ref, sem):
        pltpu.make_async_copy(ref, ref, sem).wait()

    bar = pltpu.get_barrier_semaphore()
    ndev = groups * 2

    def greet(i, _):
        t = lax.rem(dp * 2 + y + i, ndev)
        pl.semaphore_signal(bar, inc=1, device_id=(t // 2, t % 2), device_id_type=MESH)
        return 0

    lax.fori_loop(1, ndev, greet, 0)
    pl.semaphore_wait(bar, ndev - 1)

    def unit(k):
        return (wo if k == 3 else src_a.at[k]), w_a.at[k], k

    def zsend(k):
        src, buf, n = unit(k)
        for i in range(1, nz):
            zt = lax.rem(z + i, nz)
            rc(src, buf.at[z, x, c], ag_s.at[n, i - 1], ag_z.at[n], dev(zt, x, y, y)).start()

        @pl.when(home)
        def _():
            pltpu.make_async_copy(src, buf.at[z, x, c], ag_z.at[n]).start()

        @pl.when(away)
        def _():
            rc(src, buf.at[z, x, c], ag_s.at[n, nz - 1], ag_z.at[n], dev(z, x, y, y)).start()

    def ag1(k):
        src, buf, n = unit(k)

        @pl.when(home)
        def _():
            wait(buf.at[:, x], ag_z.at[n])
            rc(buf.at[:, x], buf.at[:, x], ag_s.at[n, nz], ag_y.at[n], ynbr).start()
            rc(buf.at[:, x], buf.at[:, x], ag_s.at[n, nz + 1], ag_x.at[n], xnbr).start()

    def ag2(k):
        src, buf, n = unit(k)

        @pl.when(home)
        def _():
            wait(buf.at[:, xb], ag_x.at[n])
            part = buf.at[pl.ds(0, kd), xb]
            rc(part, part, ag_s.at[n, nz + 2], ag_d.at[n, 0], ynbr).start()

        @pl.when(away)
        def _():
            wait(buf.at[:, x], ag_y.at[n])
            part = buf.at[pl.ds(kd, nz - kd), x]
            rc(part, part, ag_s.at[n, nz + 2], ag_d.at[n, 1], xnbr).start()

    def ag3(k):
        src, buf, n = unit(k)

        @pl.when(away)
        def _():
            wait(buf.at[pl.ds(0, kd), xb], ag_d.at[n, 0])
            wait(buf.at[pl.ds(kd, nz - kd), xb], ag_d.at[n, 1])

    def ag_done(k):
        src, buf, n = unit(k)
        for i in range(nz - 1):
            wait(src, ag_s.at[n, i])

        @pl.when(home)
        def _():
            wait(buf.at[:, x], ag_s.at[n, nz])
            wait(buf.at[:, x], ag_s.at[n, nz + 1])
            wait(buf.at[pl.ds(0, kd), xb], ag_s.at[n, nz + 2])

        @pl.when(away)
        def _():
            wait(src, ag_s.at[n, nz - 1])
            wait(buf.at[pl.ds(kd, nz - kd), x], ag_s.at[n, nz + 2])

    def rs_unit(k):
        return w_a.at[k], rx_a.at[k], ry_a.at[k], ry2_a.at[k], rz_a.at[k], k

    def src_unit(m, cc):
        ref = wd if m == 2 else src_f.at[m]
        return ref.at[:, cc * fq : (cc + 1) * fq]

    at_end = (z == 0) | (z == nz - 1)
    relay = jnp.where(z < nz // 2, nz - 1, 0)

    def zsendf(m):
        land = w_f.at[m, z, x, c]
        for i in range(nz):
            zt = lax.rem(z + i, nz)
            span = jnp.abs(zt - z)
            for cc in range(2):
                src = src_unit(m, cc)
                to = dev(zt, x, cc, y)
                far = rc(src, land, agf_s.at[m, 2 * i + cc], agf_z.at[m], to)
                fed = rc(src, land, agf_s.at[m, 2 * i + cc], agf_f.at[m], to)
                if i:
                    passed = at_end & (span == nz - 2)
                    pl.when(passed)(fed.start)
                    pl.when(jnp.logical_not(passed) & (span < nz - 1))(far.start)
                else:
                    pl.when(c != cc)(far.start)
                    pl.when(c == cc)(pltpu.make_async_copy(src, land, agf_z.at[m]).start)

    def agf1(m):
        block = w_f.at[m, relay, x]
        wait(block, agf_f.at[m])
        far = rc(block, block, agf_s.at[m, 2 * nz + 1], agf_f.at[m], dev(nz - 1 - relay, x, c, y))
        pl.when(jnp.logical_not(at_end))(far.start)
        wait(w_f.at[m, pl.ds(0, nz - 1), x], agf_z.at[m])
        rc(w_f.at[m, :, x], w_f.at[m, :, x], agf_s.at[m, 2 * nz], agf_x.at[m], xnbr).start()

    def agf2(m):
        wait(w_f.at[m, :, xb], agf_x.at[m])

    def agf_done(m):
        for i in range(nz):
            span = jnp.abs(lax.rem(z + i, nz) - z)
            for cc in range(2):
                sent = (span < nz - 1) if i else (c != cc)

                @pl.when(sent)
                def _():
                    wait(src_unit(m, cc), agf_s.at[m, 2 * i + cc])

        @pl.when(jnp.logical_not(at_end))
        def _():
            wait(w_f.at[m, 0, x], agf_s.at[m, 2 * nz + 1])

        wait(w_f.at[m, :, x], agf_s.at[m, 2 * nz])

    def rsf0(m):
        rc(w_f.at[m, :, xb], rx_f.at[m], rsf_s.at[m, 2 * nz], rsf_x.at[m], xnbr).start()

    def rsf1(m):
        wait(rx_f.at[m], rsf_x.at[m])
        for v in range(2):

            @pl.when(x == v)
            def _():
                rx_f[m] = (w_f[m, :, v].astype(F32) + rx_f[m].astype(F32)).astype(BF)

        for i in range(nz):
            zt = lax.rem(z + i, nz)
            for cc in range(2):
                src, land = rx_f.at[m, zt, cc], rz_f.at[m, z, c]
                far = rc(src, land, rsf_s.at[m, 2 * i + cc], rsf_z.at[m], dev(zt, x, cc, y))
                if i:
                    far.start()
                else:
                    pl.when(c != cc)(far.start)
                    pl.when(c == cc)(pltpu.make_async_copy(src, land, rsf_z.at[m]).start)

    def rsf3(m):
        wait(rz_f.at[m], rsf_z.at[m])
        halves = []
        for cc in range(2):
            total = rz_f[m, 0, cc].astype(F32)
            for i in range(1, nz):
                total = total + rz_f[m, i, cc].astype(F32)
            halves.append(total)
        return jnp.concatenate(halves, axis=1)

    def rsf_done(m):
        for i in range(nz):
            for cc in range(2):
                if i:
                    wait(rz_f.at[m, 0, 0], rsf_s.at[m, 2 * i + cc])
                else:

                    @pl.when(c != cc)
                    def _():
                        wait(rz_f.at[m, 0, 0], rsf_s.at[m, cc])

        wait(rx_f.at[m], rsf_s.at[m, 2 * nz])

    lo_z = pl.ds(0, kd)
    hi_z = pl.ds(kd, nz - kd)

    def at_unit(ref, k, *spot):
        return ref[(k,) + spot].astype(F32)

    def put_unit(ref, k, total, *spot):
        ref[(k,) + spot] = total.astype(BF)

    every = slice(None)

    def by_x(step):
        for v in range(2):
            pl.when(x == v)(functools.partial(step, v, 1 - v))

    def rs0(k):
        g, rx, ry, ry2, rz, n = rs_unit(k)
        rc(g.at[hi_z, xb], rx.at[hi_z], rs_s.at[n, 0], rs_x.at[n, 1], xnbr).start()

        @pl.when(away)
        def _():
            rc(g.at[lo_z], ry, rs_s.at[n, 1], rs_y.at[n, 0], ynbr).start()

    def rs1(k):
        g, rx, ry, ry2, rz, n = rs_unit(k)
        g_all, rx_all, ry_all, ry2_all = w_a, rx_a, ry_a, ry2_a

        @pl.when(away)
        def _():
            wait(rx.at[hi_z], rs_x.at[n, 1])

            @by_x
            def _(v, vb):
                put_unit(ry2_all, k, at_unit(g_all, k, hi_z, v) + at_unit(rx_all, k, hi_z))

            rc(ry2, ry2, rs_s.at[n, 2], rs_y.at[n, 1], ynbr).start()

        @pl.when(home)
        def _():
            wait(ry, rs_y.at[n, 0])

            @by_x
            def _(v, vb):
                total = at_unit(g_all, k, lo_z, vb) + at_unit(ry_all, k, every, vb)
                put_unit(ry_all, k, total, every, vb)

            rc(ry.at[:, xb], rx.at[lo_z], rs_s.at[n, 2], rs_x.at[n, 0], xnbr).start()

    def rs2(k):
        g, rx, ry, ry2, rz, n = rs_unit(k)
        g_all, rx_all, ry_all, ry2_all = w_a, rx_a, ry_a, ry2_a

        @pl.when(home)
        def _():
            wait(rx.at[hi_z], rs_x.at[n, 1])
            wait(ry2, rs_y.at[n, 1])

            @by_x
            def _(v, vb):
                total = at_unit(g_all, k, hi_z, v) + at_unit(rx_all, k, hi_z) + at_unit(ry2_all, k)
                put_unit(rx_all, k, total, hi_z)

            wait(rx.at[lo_z], rs_x.at[n, 0])

            @by_x
            def _(v, vb):
                total = at_unit(g_all, k, lo_z, v) + at_unit(ry_all, k, every, v)
                put_unit(rx_all, k, total + at_unit(rx_all, k, lo_z), lo_z)

            for i in range(1, nz):
                zt = lax.rem(z + i, nz)
                for cc in range(2):
                    rc(
                        rx.at[zt, cc], rz.at[z], rs_s.at[n, 3 + 2 * (i - 1) + cc], rs_z.at[n],
                        dev(zt, x, cc, y),
                    ).start()
            rc(rx.at[z, oth], rz.at[z], rs_s.at[n, 2 * nz + 1], rs_z.at[n], partner).start()
            pltpu.make_async_copy(rx.at[z, c], rz.at[z], rs_z.at[n]).start()

    def rs_done(k):
        g, rx, ry, ry2, rz, n = rs_unit(k)
        wait(rx.at[hi_z], rs_s.at[n, 0])

        @pl.when(away)
        def _():
            wait(ry, rs_s.at[n, 1])
            wait(ry2, rs_s.at[n, 2])

        @pl.when(home)
        def _():
            wait(rx.at[lo_z], rs_s.at[n, 2])
            for i in range(2 * (nz - 1) + 1):
                wait(rz.at[0], rs_s.at[n, 3 + i])

    def rs3(k):
        g, rx, ry, ry2, rz, n = rs_unit(k)
        wait(rz, rs_z.at[n])
        total = None
        for i in range(nz):
            part = rz_a[k, i].astype(F32)
            total = part if total is None else total + part
        return total

    fetch = pltpu.make_async_copy(x_ref, ret, lo_r)
    fetch.start()
    square = (nrow, nrow)
    on_diag = lax.broadcasted_iota(jnp.int32, square, 0) == lax.broadcasted_iota(
        jnp.int32, square, 1
    )

    def column(ref):
        spread = jnp.where(on_diag, ref[...].astype(F32), 0.0)
        return jnp.sum(spread, axis=1, keepdims=True)

    gain1 = column(g1)
    gain2 = column(g2)
    for i, w in enumerate((wq, wk, wv)):
        src_a[i] = (w[...].astype(F32) * gain1).astype(BF)
        zsend(i)

    def stage(j, _):
        xs[j] = ret[deal[j]]
        return 0

    fetch.wait()
    lax.fori_loop(0, groups, stage, 0)

    def deal_out(i, _):
        j = lax.rem(slot + i, groups)
        dpd = (j // 2) * 2 + y
        td = j % 2
        same = (dpd == dp) & (td == y)

        @pl.when(same)
        def _():
            pltpu.make_async_copy(xs.at[j], xbuf.at[dp], a2a_r).start()

        @pl.when(jnp.logical_not(same))
        def _():
            rc(xs.at[j], xbuf.at[dp], a2a_s, a2a_r, (dpd, td)).start()

        return 0

    lax.fori_loop(0, groups, deal_out, 0)

    src_f[0] = (wg[...].astype(F32) * gain2).astype(BF)
    src_f[1] = (wu[...].astype(F32) * gain2).astype(BF)

    def rope_rows(i, _):
        ca, sa = tab[0, pl.ds(i, 1), :], tab[1, pl.ds(i, 1), :]
        cb, sb = tab[2], tab[3]
        at = pl.ds(pl.multiple_of(i * 32, 32), 32)
        cosb[at, :] = ca * cb - sa * sb
        sinb[at, :] = sa * cb + ca * sb
        return 0

    lax.fori_loop(0, seq_len // 32, rope_rows, 0)
    for i in range(nrb):
        at = slice(i * ROWS, (i + 1) * ROWS)
        ct[:, at] = cosb[at, :].T[0:32]
        st[:, at] = sinb[at, :].T[0:32]
    pw = wop.shape[1]
    row = lax.broadcasted_iota(jnp.int32, (hw, pw), 0)
    col = lax.broadcasted_iota(jnp.int32, (hw, pw), 1)
    low = col & 31
    spot = ((col >> 8) * 4 + ((col >> 5) & 3)) * HD + ((col >> 7) & 1) * (HD // 2) + low
    eqk[...] = jnp.where((row == spot) & (low < HD // 2), 1.0, 0.0).astype(BF)
    low = col & 63
    ev[...] = jnp.where((row == (col >> 6) * HD + low) & (low < HD), 1.0, 0.0).astype(BF)

    length = lens[deal[slot]]
    other_length = lens[deal[other_slot]]

    def live_at(i):
        at = (i * 2 + c) * 32 + lax.broadcasted_iota(jnp.int32, (32, 1), 0)
        return at < length

    def mean(values):
        return jnp.mean(values, axis=1, keepdims=True)

    def swap_start(n, src, dst):
        rc(src, dst, ex_s.at[n], ex_r.at[n], partner).start()

    def blk(i):
        return pl.ds(i * (ROWS // 64), ROWS // 64)

    for i in range(3):
        ag1(i)
    zsend(3)
    zsendf(0)

    def gather_dy(mine):
        pltpu.make_async_copy(dy_ref, mine.at[:, y], dy_r.at[0]).start()

    def send_dy(far):
        rc(dy_ref, far.at[:, y], dy_s.at[0], dy_r.at[1], ynbr).start()

    for i in range(3):
        ag2(i)
    wait(xbuf, a2a_r)
    zsendf(1)

    def norm_one(i, _):
        rows_now = xbuf[i].astype(F32)
        r = lax.rsqrt(mean(rows_now * rows_now) + EPS)
        rb[i] = jnp.broadcast_to(r, (32, 128))
        abuf[i, c] = (rows_now * r).astype(BF)
        return 0

    lax.fori_loop(0, groups, norm_one, 0, unroll=2)
    swap_start(0, abuf.at[:, c], abuf.at[:, c])
    for i in range(3):
        ag3(i)
        e = eqk if i < 2 else ev
        wp[:, i * pw : (i + 1) * pw] = mm(
            NN, w_a[i].reshape(dim, hw), e[...]
        ).astype(BF)
    @pl.when(home)
    def _():
        gather_dy(dd0)
        send_dy(dd1)

    @pl.when(away)
    def _():
        gather_dy(dd1)
        send_dy(dd0)

    ag1(3)
    zsendf(2)
    wait(abuf.at[:, oth], ex_r.at[0])

    query_scale = score_scale * LOG2E
    lane64 = lax.broadcasted_iota(jnp.int32, (ROWS, pw), 1) & 63

    def project(i, _):
        a = abuf[blk(i)].reshape(ROWS, dim)
        at = pl.ds(pl.multiple_of(i * ROWS, ROWS), ROWS)
        cos, sin = cosb[at, :], sinb[at, :]
        for t, (dst, scale) in enumerate(((qb, query_scale), (kb, 1.0))):
            u = mm(NN, a, wp[:, t * pw : (t + 1) * pw]) * scale
            for g in range(pw // 256):
                f1 = u[:, g * 256 : g * 256 + 128]
                f2 = u[:, g * 256 + 128 : g * 256 + 256]
                dst[blk(i), :, :, g * 256 : g * 256 + 128] = (
                    (f1 * cos - f2 * sin).astype(BF).reshape(ROWS // 64, 2, 32, 128)
                )
                dst[blk(i), :, :, g * 256 + 128 : g * 256 + 256] = (
                    (f2 * cos + f1 * sin).astype(BF).reshape(ROWS // 64, 2, 32, 128)
                )
        v = mm(NN, a, wp[:, 2 * pw : 3 * pw])
        v = jnp.where(lane64 == HD, 1.0, v).astype(BF)
        vb[blk(i)] = v.reshape(ROWS // 64, 2, 32, pw)
        vt[:, at] = v.T
        return 0

    lax.fori_loop(0, nrb, project, 0)
    ag2(3)
    agf1(0)

    lane = lax.broadcasted_iota(jnp.int32, (ROWS, 256), 1)
    diag = lax.broadcasted_iota(jnp.int32, (ROWS, ROWS), 0) <= lax.broadcasted_iota(
        jnp.int32, (ROWS, ROWS), 1
    )

    def rows_of(ref, first, count, lanes):
        return ref[pl.ds(first // 64, count // 64), :, :, lanes].reshape(count, 256)

    def attend(i):
        keys = (i + 1) * ROWS

        def group(g, _):
            lanes = pl.ds(pl.multiple_of(g * 256, 256), 256)
            q = rows_of(qb, i * ROWS, ROWS, lanes)
            for hh in range(4):
                qm = jnp.where(((lane >> 5) & 3) == hh, q, jnp.zeros_like(q))
                sd = mm(NT, rows_of(kb, i * ROWS, ROWS, lanes), qm)
                sd = jnp.where(diag, sd, -1e30)
                top = jnp.max(sd, axis=0, keepdims=True)
                if i:
                    s = mm(NT, rows_of(kb, 0, i * ROWS, lanes), qm)
                    top = jnp.maximum(top, jnp.max(s, axis=0, keepdims=True))
                    p = jnp.concatenate(
                        [jnp.exp2(s - top).astype(BF), jnp.exp2(sd - top).astype(BF)], axis=0
                    )
                else:
                    p = jnp.exp2(sd - top).astype(BF)
                hs = pl.multiple_of(g * 256 + hh * 64, 64)
                o = mm(NN, vt[pl.ds(hs, 64), 0:keys], p)
                total = o[HD : HD + 1, :]
                ot[pl.ds(hs, 64), i * ROWS : keys] = (o * (1.0 / total)).astype(BF)
                lse[pl.ds(g * 4 + hh, 1), i * ROWS : keys] = top + jnp.log2(total)
            return 0

        lax.fori_loop(0, pw // 256, group, 0)

    def hand_dy(mine):
        wait(mine.at[:, y], dy_r.at[0])
        wait(mine.at[:, yb], dy_r.at[1])
        rc(mine, mine, ex_s.at[1], ex_r.at[1], partner).start()

    def during_zero():
        agf1(1)

    def during_one():
        ag3(3)
        wop[...] = mm(NN, w_a[3].reshape(dim, hw), ev[...]).astype(BF)

    def during_two():
        pl.when(home)(lambda: hand_dy(dd0))
        pl.when(away)(lambda: hand_dy(dd1))

    def settle_dy():
        pl.when(home)(lambda: wait(dd1, ex_r.at[1]))
        pl.when(away)(lambda: wait(dd0, ex_r.at[1]))
        wait(dd0, ex_s.at[1])

        def save_dy(i, _):
            dybuf[i] = dd0[i, c]
            return 0

        lax.fori_loop(0, groups, save_dy, 0)

        def mask_dy(i, _):
            at = i * ROWS + lax.broadcasted_iota(jnp.int32, (ROWS, 1), 0)
            zeros = jnp.zeros((ROWS, dim), BF)
            for ref, count in ((dd0, length), (dd1, other_length)):
                masked = jnp.where(at < count, ref[blk(i)].reshape(ROWS, dim), zeros)
                ref[blk(i)] = masked.reshape(ROWS // 64, 2, 32, dim)
            return 0

        lax.fori_loop(0, nrb, mask_dy, 0)

    def with_steps(part, steps):
        for i in range(nrb):
            part(i)
            for at, step in steps:
                if min(at, nrb - 1) == i:
                    step()

    with_steps(attend, ((0, during_zero), (1, during_one), (2, during_two)))
    agf1(2)

    def turn(i, _):
        at = pl.ds(pl.multiple_of(i * ROWS, ROWS), ROWS)
        ob[blk(i)] = ot[:, at].T.reshape(ROWS // 64, 2, 32, pw)
        return 0

    lax.fori_loop(0, nrb, turn, 0)

    half_rows = ROWS // 32

    def att_other(j, _):
        at = pl.ds(j * half_rows, half_rows)
        o = ob[at, oth].reshape(ROWS, pw)
        sb1[at] = mm(NT, o, wop[...]).astype(BF).reshape(half_rows, 32, dim)
        return 0

    def att_own(j, _):
        at = pl.ds(j * half_rows, half_rows)
        o = ob[at, c].reshape(ROWS, pw)
        own[at] = mm(NT, o, wop[...]).reshape(half_rows, 32, dim)
        return 0

    lax.fori_loop(0, groups // half_rows, att_other, 0)
    swap_start(2, sb1, rb1)
    lax.fori_loop(0, groups // half_rows, att_own, 0)
    wait(rb1, ex_r.at[2])

    low_lanes = lax.broadcasted_iota(jnp.int32, (32, 128), 1) < 64

    def norm_two(i, _):
        att = own[i] + rb1[i].astype(F32)
        x1 = xbuf[i].astype(F32) + jnp.where(live_at(i), att, 0.0)
        x1b[i] = x1
        r = lax.rsqrt(mean(x1 * x1) + EPS)
        rb[i] = jnp.where(low_lanes, rb[i], r)
        bb0[i, c] = (x1 * r).astype(BF)
        return 0

    hg = groups // 2

    for hf in range(2):
        lax.fori_loop(hf * hg, (hf + 1) * hg, norm_two, 0, unroll=2)
        at = pl.ds(hf * hg, hg)
        rc(bb0.at[at, c], bb1.at[at, c], b_s.at[1, hf], b_r.at[1, hf], ynbr).start()
        rc(bb0.at[at, c], bb0.at[at, c], b_s.at[0, hf], b_r.at[0, hf], partner).start()

    def hand_b(hf):
        at = pl.ds(hf * hg, hg)
        wait(bb1.at[at, c], b_r.at[1, hf])
        rc(bb1.at[at, c], bb1.at[at, c], b_s.at[2, hf], b_r.at[2, hf], partner).start()

    def ffn(own_seq, i):
        b_ref, d_ref, count = (bb0, dd0, length) if own_seq else (bb1, dd1, other_length)
        base = 0 if own_seq else seq_len
        b = b_ref[blk(i)].reshape(ROWS, dim)
        d = d_ref[blk(i)].reshape(ROWS, dim)
        w_g, w_u, w_d = (w_f[m].reshape(dim, fq) for m in range(3))
        gate = mm(NN, b, w_g)
        up = mm(NN, b, w_u)
        dh = mm(NN, d, w_d)
        sg = jax.nn.sigmoid(gate)
        silu = gate * sg
        hid = (silu * up).astype(BF)
        dgate = (dh * up * sg * (1.0 + gate * (1.0 - sg))).astype(BF)
        dup = (dh * silu).astype(BF)
        at = pl.ds(pl.multiple_of(base + i * ROWS, ROWS), ROWS)
        act[at, 0:fq] = dgate
        act[at, fq : 2 * fq] = dup
        act[at, 2 * fq : 3 * fq] = hid
        u = (mm(NT, dgate, w_g) + mm(NT, dup, w_u)).reshape(ROWS // 64, 2, 32, dim)
        n = i if own_seq else i + nrb
        uacc[blk(i), 0 if own_seq else 1] = jnp.where(c == 0, u[:, 0], u[:, 1])

        @pl.when(n >= 2)
        def _():
            wait(usend.at[0], us_s.at[n - 2])

        ring = n % 2
        usend[ring] = jnp.where(c == 0, u[:, 1], u[:, 0]).astype(BF)
        part = pl.ds(n * (ROWS // 64), ROWS // 64)
        rc(usend.at[ring], urecv.at[part], us_s.at[n], us_r.at[n], partner).start()
        alive = i * ROWS + lax.broadcasted_iota(jnp.int32, (ROWS, 1), 0) < count
        out = jnp.where(alive, mm(NT, hid, w_d), 0.0).reshape(ROWS // 64, 2, 32, dim)

        @pl.when(home if own_seq else away)
        def _():
            facc[blk(i)] = out

        @pl.when(away if own_seq else home)
        def _():
            @pl.when(i >= 2)
            def _():
                wait(fsend.at[0], fs_s.at[i - 2])

            slot_now = i % 2
            if own_seq:
                x1 = x1b[blk(i)]
                fsend[slot_now, :, 0] = (out[:, 0] + jnp.where(c == 0, x1, 0.0)).astype(BF)
                fsend[slot_now, :, 1] = (out[:, 1] + jnp.where(c == 1, x1, 0.0)).astype(BF)
            else:
                fsend[slot_now] = out.astype(BF)
            rc(fsend.at[slot_now], frecv.at[blk(i)], fs_s.at[i], fs_r.at[i], partner).start()

    settle_dy()
    for m in range(3):
        agf2(m)
    for hf in range(2):
        wait(bb0.at[pl.ds(hf * hg, hg), oth], b_r.at[0, hf])

    def ffn_own(i, _):
        ffn(True, i)

        @pl.when(i == nrb - 2)
        def _():
            hand_b(0)

        return 0

    lax.fori_loop(0, nrb, ffn_own, 0)
    hand_b(1)

    per = ROWS // 64

    def join_u(i):
        at = pl.ds((nrb + i) * per, per)
        wait(urecv.at[at], us_r.at[nrb + i])
        sb1[pl.ds(i * per, per)] = (uacc[blk(i), 1] + urecv[at].astype(F32)).astype(BF)
        at = pl.ds(i * per, per)
        rc(sb1.at[at], rb1.at[at], uy_s.at[0, i], uy_r.at[0, i], ynbr).start()

    def ffn_other(i, _):
        for hf in range(2):

            @pl.when(i == hf * nrb // 2)
            def _():
                wait(bb1.at[pl.ds(hf * hg, hg), oth], b_r.at[2, hf])

        ffn(False, i)

        @pl.when(i >= 1)
        def _():
            join_u(i - 1)

        return 0

    wait(sb1, ex_s.at[2])
    lax.fori_loop(0, nrb, ffn_other, 0)
    join_u(nrb - 1)

    for i in range(nrb):
        wait(frecv.at[blk(i)], fs_r.at[i])

    def join_out(i, _):
        sb2[i] = (facc[i, yb] + frecv[i, yb].astype(F32)).astype(BF)
        mine = facc[i, y] + frecv[i, y].astype(F32)
        own[i] = mine + jnp.where(home, x1b[i], 0.0)
        return 0

    lax.fori_loop(0, groups, join_out, 0)
    rc(sb2, rb2, uy_s.at[1, 0], uy_r.at[1, 0], ynbr).start()

    def weight_grad(m, refs, first):
        agf_done(m)
        rows_half = half // 64

        def one_half(part, _):
            feats = pl.ds(pl.multiple_of(part * half, 128), half)
            t = None
            for n, ref in enumerate(refs):
                left = ref[:, :, :, feats].reshape(seq_len, half)
                term = mm(TN, left, act[n * seq_len : (n + 1) * seq_len, first : first + fq])
                t = term if t is None else t + term
            facc[pl.ds(part * rows_half, rows_half), :, :, 0:fq] = t.reshape(rows_half, 2, 32, fq)
            return 0

        lax.fori_loop(0, 2, one_half, 0)
        for part in range(2):
            zs = slice(part * nz // 2, (part + 1) * nz // 2)
            t = facc[part * rows_half : (part + 1) * rows_half, :, :, 0:fq].reshape(half, fq)
            w_f[m, zs] = t.astype(BF).reshape(nz // 2, 2, 2, nrow, fq)
        rsf0(m)

    weight_grad(0, (bb0, bb1), 0)
    weight_grad(1, (bb0, bb1), fq)
    pl.semaphore_signal(free, inc=1, device_id=partner, device_id_type=MESH)
    weight_grad(2, (dd0, dd1), 2 * fq)
    for i in range(nrb):
        at = pl.ds(i * per, per)
        wait(urecv.at[at], us_r.at[i])

    @pl.when(home)
    def _():
        wait(xs.at[pl.ds(0, groups - 1)], a2a_s)

    @pl.when(away)
    def _():
        wait(xs, a2a_s)

    for hf in range(2):
        at = pl.ds(hf * hg, hg)
        wait(bb0.at[at, c], b_s.at[0, hf])
        wait(bb0.at[at, c], b_s.at[1, hf])
    for i in range(nrb):
        wait(rb1.at[pl.ds(i * per, per)], uy_r.at[0, i])

    def norm_three(i, _):
        alive = live_at(i)
        x1 = x1b[i]
        r = rb[i][:, 64:65]
        n = x1 * r
        u = uacc[i, 0] + urecv[i].astype(F32) + rb1[i].astype(F32)
        dx1 = dybuf[i].astype(F32) + r * (u - n * mean(u * n))
        bb0[i, c] = jnp.where(alive, dx1, 0.0).astype(BF)
        x1b[i] = dx1
        return 0

    lax.fori_loop(0, groups, norm_three, 0, unroll=2)
    pl.semaphore_wait(free, 1)
    swap_start(6, bb0.at[:, c], bb0.at[:, c])
    rsf1(0)

    def turn_k(i, _):
        at = pl.ds(pl.multiple_of(i * ROWS, ROWS), ROWS)
        t = kb[blk(i)].reshape(ROWS, pw).T
        for h in range(pw // 64):
            for part in range(2):
                first = (h // 4) * 256 + part * 128 + (h % 4) * 32
                vt[h * 64 + part * 32 : h * 64 + part * 32 + 32, at] = t[first : first + 32]
        return 0

    lax.fori_loop(0, nrb, turn_k, 0)
    heads16 = lax.broadcasted_iota(jnp.int32, (16, pw), 0)
    pick = jnp.where(
        (lax.broadcasted_iota(jnp.int32, (16, pw), 1) >> 6) == heads16, 1.0, 0.0
    ).astype(BF)
    wait(bb0.at[:, oth], ex_r.at[6])

    for hf in range(2):
        wait(bb1.at[pl.ds(hf * hg, hg), c], b_s.at[2, hf])

    def out_back(i, _):
        at = pl.ds(pl.multiple_of(i * ROWS, ROWS), ROWS)
        t = mm(NN, bb0[blk(i)].reshape(ROWS, dim), wop[...]).astype(BF)
        bb1[blk(i), :, :, 0:pw] = t.reshape(ROWS // 64, 2, 32, pw)
        prod = t.astype(F32) * ob[blk(i)].reshape(ROWS, pw).astype(F32)
        delta[:, at] = mm(NT, pick, prod.astype(BF))
        return 0

    lax.fori_loop(0, nrb, out_back, 0)
    ag_done(3)
    for m in range(2):
        left = bb0[:, :, :, m * half : (m + 1) * half].reshape(seq_len, half)
        t = mm(TN, left, ob[...].reshape(seq_len, pw)).astype(BF)
        zs = slice(m * nz // 2, (m + 1) * nz // 2)
        w_a[3, zs] = mm(NT, t, ev[...]).astype(BF).reshape(nz // 2, 2, 2, nrow, hw)
    rs0(3)

    def attend_back(i):
        keys = (i + 1) * ROWS

        def group(g, _):
            lanes = pl.ds(pl.multiple_of(g * 256, 256), 256)
            q = rows_of(qb, i * ROWS, ROWS, lanes)
            d = rows_of(bb1, i * ROWS, ROWS, lanes)
            for hh in range(4):
                qm = jnp.where(((lane >> 5) & 3) == hh, q, jnp.zeros_like(q))
                dm = jnp.where((lane >> 6) == hh, d, jnp.zeros_like(d))
                row_lse = lse[pl.ds(g * 4 + hh, 1), i * ROWS : keys]
                row_delta = delta[pl.ds(g * 4 + hh, 1), i * ROWS : keys]

                def part(first, count, masked):
                    s = mm(NT, rows_of(kb, first, count, lanes), qm)
                    if masked:
                        s = jnp.where(diag, s, -1e30)
                    p = jnp.exp2(s - row_lse)
                    dp_ = mm(NT, rows_of(vb, first, count, lanes), dm)
                    ds = (p * (dp_ - row_delta)).astype(BF)
                    at = pl.ds(first // 64, count // 64)
                    dv_part = mm(NN, p.astype(BF), dm).reshape(count // 64, 2, 32, 256)
                    dk_part = mm(NN, ds, qm).reshape(count // 64, 2, 32, 256)
                    if masked and hh == 0:
                        uacc[at, :, :, lanes] = dv_part
                        facc[at, :, :, lanes] = dk_part
                    else:
                        uacc[at, :, :, lanes] += dv_part
                        facc[at, :, :, lanes] += dk_part
                    return ds

                ds = part(i * ROWS, ROWS, True)
                if i:
                    ds = jnp.concatenate([part(0, i * ROWS, False), ds], axis=0)
                hs = pl.multiple_of(g * 256 + hh * 64, 64)
                t = mm(NN, vt[pl.ds(hs, 64), 0:keys], ds) * score_scale
                c_now, s_now = ct[:, i * ROWS : keys], st[:, i * ROWS : keys]
                f1, f2 = t[0:32], t[32:64]
                hs = pl.multiple_of(g * 256 + hh * 32, 32)
                ot[pl.ds(hs, 32), i * ROWS : keys] = (f1 * c_now + f2 * s_now).astype(BF)
                ot[pl.ds(hs + 128, 32), i * ROWS : keys] = (f2 * c_now - f1 * s_now).astype(BF)
            return 0

        lax.fori_loop(0, pw // 256, group, 0)

    def back_zero():
        pass

    def back_one():
        rsf1(1)

    def back_two():
        rsf1(2)

    with_steps(
        attend_back,
        ((0, back_zero), (1, back_one), (2, back_two)),
    )

    def turn_back(i, _):
        at = pl.ds(pl.multiple_of(i * ROWS, ROWS), ROWS)
        qb[blk(i)] = ot[:, at].T.reshape(ROWS // 64, 2, 32, pw)
        vb[blk(i)] = uacc[blk(i), :, :, 0:pw].astype(BF)
        cos, sin = cosb[at, :], sinb[at, :]
        for g in range(pw // 256):
            f1 = facc[blk(i), :, :, g * 256 : g * 256 + 128].reshape(ROWS, 128)
            f2 = facc[blk(i), :, :, g * 256 + 128 : g * 256 + 256].reshape(ROWS, 128)
            kb[blk(i), :, :, g * 256 : g * 256 + 128] = (
                ((f1 * cos + f2 * sin) * (1.0 / LOG2E)).astype(BF).reshape(ROWS // 64, 2, 32, 128)
            )
            kb[blk(i), :, :, g * 256 + 128 : g * 256 + 256] = (
                ((f2 * cos - f1 * sin) * (1.0 / LOG2E)).astype(BF).reshape(ROWS // 64, 2, 32, 128)
            )
        return 0

    lax.fori_loop(0, nrb, turn_back, 0)
    for t, (src, e) in enumerate(((qb, eqk), (kb, eqk), (vb, ev))):
        ag_done(t)
        for m in range(2):
            left = abuf[:, :, :, m * half : (m + 1) * half].reshape(seq_len, half)
            part = mm(TN, left, src[...].reshape(seq_len, pw)).astype(BF)
            zs = slice(m * nz // 2, (m + 1) * nz // 2)
            w_a[t, zs] = mm(NT, part, e[...]).astype(BF).reshape(nz // 2, 2, 2, nrow, hw)
        rs0(t)
    for hf in range(2):
        for i in range(hf * nrb // 2, (hf + 1) * nrb // 2):
            wait(sb1.at[pl.ds(i * per, per)], uy_s.at[0, i])

    wait(rb2, uy_r.at[1, 0])

    def finish_out(i, _):
        sb2[i] = (own[i] + rb2[i].astype(F32)).astype(BF)
        return 0

    wait(sb2, uy_s.at[1, 0])
    lax.fori_loop(0, groups, finish_out, 0)
    pltpu.make_async_copy(sb2, lo_ref, lo_r).start()

    def da_rows(at, which):
        total = None
        for t, src in enumerate((qb, kb, vb)):
            term = mm(NT, src[at, which].reshape(ROWS, pw), wp[:, t * pw : (t + 1) * pw])
            total = term if total is None else total + term
        return total.reshape(half_rows, 32, dim)

    def da_other(j, _):
        at = pl.ds(j * half_rows, half_rows)
        sb1[at] = da_rows(at, oth).astype(BF)
        return 0

    def da_own(j, _):
        at = pl.ds(j * half_rows, half_rows)
        own[at] = da_rows(at, c)
        return 0

    lax.fori_loop(0, groups // half_rows, da_other, 0)
    swap_start(7, sb1, rb1)
    lax.fori_loop(0, groups // half_rows, da_own, 0)
    rs1(3)

    wait(rb1, ex_r.at[7])

    def norm_four(i, _):
        rows_now = xbuf[i].astype(F32)
        r = rb[i][:, 0:1]
        n = rows_now * r
        u = own[i] + rb1[i].astype(F32)
        dx = x1b[i] + r * (u - n * mean(u * n))
        xs[i] = dx.astype(BF)
        same = (i == dp) & (c == y)

        @pl.when(same)
        def _():
            pltpu.make_async_copy(xs.at[i], ret.at[slot], ret_r).start()

        @pl.when(jnp.logical_not(same))
        def _():
            rc(xs.at[i], ret.at[slot], ret_s, ret_r, (i, c)).start()

        return 0

    lax.fori_loop(0, groups, norm_four, 0)
    for i in range(3):
        rs1(i)
    rs2(3)
    for i in range(3):
        rs2(i)

    d_g, d_u = rsf3(0), rsf3(1)
    dg_out[...] = d_g * gain2
    du_out[...] = d_u * gain2
    both = d_g * wg[...].astype(F32) + d_u * wu[...].astype(F32)
    sums2 = jnp.sum(both, axis=1, keepdims=True)
    dd_out[...] = rsf3(2)
    do_out[...] = rs3(3)
    sums1 = jnp.zeros((nrow, 1), F32)
    for i, (w, out) in enumerate(((wq, dq_out), (wk, dk_out), (wv, dv_out))):
        part = rs3(i)
        out[...] = part * gain1
        sums1 = sums1 + jnp.sum(part * w[...].astype(F32), axis=1, keepdims=True)
    first_half = lax.broadcasted_iota(jnp.int32, (nrow, 128), 1) < 64
    gs[...] = jnp.where(first_half, sums1, sums2)
    rc(gs, gr, gg_s, gg_r, ynbr).start()

    wait(ret, ret_r)

    def restore(s, _):
        def find(j, at):
            return jnp.where(deal[j] == s, j, at)

        sb2[s] = ret[lax.fori_loop(0, groups, find, 0)]
        return 0

    wait(sb2, lo_r)
    lax.fori_loop(0, groups, restore, 0)
    give = pltpu.make_async_copy(sb2, gi_ref, lo_r)
    give.start()
    wait(gr, gg_r)
    both = gs[...] + gr[...]
    dg1_out[...] = jnp.sum(jnp.where(on_diag, both[:, 0:1], 0.0), axis=0, keepdims=True)
    dg2_out[...] = jnp.sum(jnp.where(on_diag, both[:, 64:65], 0.0), axis=0, keepdims=True)

    wait(gs, gg_s)
    for m in range(3):
        rsf_done(m)
    for i in range(4):
        rs_done(i)

    wait(dybuf, dy_s.at[0])
    give.wait()
    @pl.when(home)
    def _():
        wait(xs.at[pl.ds(0, groups - 1)], ret_s)

    @pl.when(away)
    def _():
        wait(xs, ret_s)

    wait(abuf.at[:, c], ex_s.at[0])
    for i in range(2):
        wait(usend.at[i], us_s.at[2 * nrb - 2 + i])
        wait(fsend.at[i], fs_s.at[nrb - 2 + i])
    wait(bb0.at[:, c], ex_s.at[6])
    wait(sb1, ex_s.at[7])


def rotary_tables(count):
    lanes = np.arange(128) % 32
    frequency = np.where(lanes < HD // 2, BASE ** (-2.0 * lanes / HD), 0.0)
    high = np.zeros((32, 128))
    high[:count] = 32.0 * np.arange(count)[:, None] * frequency[None, :]
    low = np.arange(32)[:, None] * frequency[None, :]
    return np.stack([np.cos(high), np.sin(high), np.cos(low), np.sin(low)]).astype(np.float32)


def fused_body(
    x_given, dealing, seq_lengths, first_gain, query_weight, key_weight, value_weight,
    output_weight, second_gain, gate_weight, up_weight, down_weight, grad_output,
):
    groups, piece_rows, dim = x_given.shape
    hw = query_weight.shape[1]
    local_hidden = gate_weight.shape[1]
    fq = local_hidden // 2
    nz = groups // 4
    rows = query_weight.shape[0]
    pw = hw // HD * 64
    seq_len = groups * 64
    vm, anym, sm = (
        pl.BlockSpec(memory_space=pltpu.VMEM),
        pl.BlockSpec(memory_space=pl.ANY),
        pl.BlockSpec(memory_space=pltpu.SMEM),
    )
    blocks = (groups, piece_rows, dim)
    pairs = (groups, 2, piece_rows)

    def gathered(width, lead=()):
        return pltpu.VMEM(lead + (nz, 2, 2, rows, width), BF)

    kd = nz // 2

    def landing(width, lead=()):
        return [
            pltpu.VMEM(lead + (nz, 2, rows, width), BF),
            pltpu.VMEM(lead + (kd, 2, 2, rows, width), BF),
            pltpu.VMEM(lead + (nz - kd, 2, rows, width), BF),
            pltpu.VMEM(lead + (nz, rows, width), BF),
        ]

    nrb = seq_len // ROWS
    dma = pltpu.SemaphoreType.DMA
    scratch = (
        [pltpu.VMEM(blocks, BF)] * 3
        + [pltpu.VMEM((3, rows, hw), BF), pltpu.VMEM((2, rows, local_hidden), BF)]
        + [gathered(hw, (4,)), gathered(fq, (3,))]
        + [pltpu.VMEM((dim, 3 * pw), BF), pltpu.VMEM((dim, pw), BF)]
        + [pltpu.VMEM((hw, pw), BF)] * 2
        + [pltpu.VMEM((seq_len, 128), F32)] * 2
        + [pltpu.VMEM((32, seq_len), F32)] * 2
        + [pltpu.VMEM(pairs + (dim,), BF)]
        + [pltpu.VMEM(pairs + (pw,), BF)] * 3
        + [pltpu.VMEM((pw, seq_len), BF)] * 2
        + [pltpu.VMEM(pairs + (pw,), BF)]
        + [pltpu.VMEM((8, seq_len), F32)]
        + [pltpu.VMEM(blocks, F32)]
        + [pltpu.VMEM(blocks, BF)] * 4
        + [pltpu.VMEM(blocks, F32)]
        + [pltpu.VMEM((groups, piece_rows, 128), F32)]
        + [pltpu.VMEM(pairs + (dim,), BF)] * 4
        + [pltpu.VMEM(pairs + (dim,), F32)] * 2
        + [pltpu.VMEM((2 * seq_len, 3 * fq), BF)]
        + [pltpu.VMEM((16, seq_len), F32)]
        + [pltpu.VMEM((2 * groups, piece_rows, dim), BF), pltpu.VMEM(pairs + (dim,), BF)]
        + [pltpu.VMEM((2, ROWS // 64, piece_rows, dim), BF)]
        + [pltpu.VMEM((2, ROWS // 64, 2, piece_rows, dim), BF)]
        + landing(hw, (4,))
        + [pltpu.VMEM((3, nz, 2, rows, fq), BF)] * 2
        + [pltpu.VMEM(blocks, BF)]
        + [pltpu.VMEM((rows, 128), F32)] * 2
        + [dma(()), dma(()), dma((1,)), dma((2,))]
        + [dma((4,)), dma((4,)), dma((4,)), dma((4, 2)), dma((4, nz + 3))]
        + [dma((4, 2)), dma((4, 2)), dma((4,)), dma((4, 2 * nz + 2))]
        + [dma((3,)), dma((3,)), dma((3,)), dma((3, 2 * nz + 2))]
        + [dma((3,)), dma((3,)), dma((3, 2 * nz + 1))]
        + [dma((8,)), dma((8,)), dma((3, 2)), dma((3, 2))]
        + [dma((2 * nrb,)), dma((2 * nrb,)), dma((nrb,)), dma((nrb,))]
        + [dma((2, nrb)), dma((2, nrb)), dma(())]
        + [dma(())] * 4
        + [pltpu.SemaphoreType.REGULAR]
    )
    small = jax.ShapeDtypeStruct((rows, hw), F32)
    wide = jax.ShapeDtypeStruct((rows, local_hidden), F32)
    piece = jax.ShapeDtypeStruct(blocks, BF)
    outs = pl.pallas_call(
        functools.partial(fused_kernel, (nz, dim, hw, fq, rows)),
        out_shape=[piece, piece, small, small, small, small, wide, wide, wide]
        + [jax.ShapeDtypeStruct((1, rows), F32)] * 2,
        in_specs=[sm, sm, anym, anym] + [vm] * 10,
        out_specs=[anym] * 2 + [vm] * 9,
        scratch_shapes=scratch,
        compiler_params=pltpu.CompilerParams(
            collective_id=0, has_side_effects=True, vmem_limit_bytes=VMEM_LIMIT
        ),
        name="layer",
    )(
        dealing, seq_lengths, x_given, grad_output.reshape(blocks),
        first_gain.reshape(1, rows), second_gain.reshape(1, rows),
        query_weight, key_weight, value_weight, output_weight, gate_weight, up_weight, down_weight,
        rotary_tables(seq_len // 32),
    )
    outs = pl.pallas_call(
        pass_on,
        out_shape=[jax.ShapeDtypeStruct(o.shape, o.dtype) for o in outs],
        in_specs=[vm] * len(outs),
        out_specs=[vm] * len(outs),
        name="results",
    )(*outs)
    layer_out, grad_in, gq, gk, gv, go, gg, gu, gd, gain_one, gain_two = outs
    return (
        layer_out.reshape(grad_output.shape), grad_in, gain_one.reshape(rows), gq, gk, gv, go,
        gain_two.reshape(rows), gg, gu, gd,
    )


def pass_on(*refs):
    count = len(refs) // 2
    for i in range(count):
        refs[count + i][...] = refs[i][...]


def fits_fused(mesh):
    return mesh.shape["tensor"] == 2 and mesh.shape["dp"] % 8 == 0


def solution(mesh):
    placed = (
        P(None, ("dp", "tensor"), None),
        P(),
        P(),
        P("dp"),
        P("dp", "tensor"),
        P("dp", "tensor"),
        P("dp", "tensor"),
        P("dp", "tensor"),
        P("dp"),
        P("dp", "tensor"),
        P("dp", "tensor"),
        P("dp", "tensor"),
        P("dp", None, "tensor", None, None),
    )
    return jax.shard_map(
        fused_body if fits_fused(mesh) else body,
        mesh=mesh,
        in_specs=placed,
        out_specs=(
            P("dp", None, "tensor", None, None),
            P(None, ("dp", "tensor"), None),
            P("dp"),
            P("dp", "tensor"),
            P("dp", "tensor"),
            P("dp", "tensor"),
            P("dp", "tensor"),
            P("dp"),
            P("dp", "tensor"),
            P("dp", "tensor"),
            P("dp", "tensor"),
        ),
        check_vma=False,
    )
```
